32 devices in a mesh: dp: 8 (over z, x), mp: 4 (over y, core).
Axes of the slice: x: 2, y: 2, z: 4, core: 2. Of those that a mesh axis runs over, the one named last changes fastest.
Arguments:
- tokens: bfloat16 [13312, 768], P(('dp', 'mp')), may hold values from -6 to 6
- lengths: int32 [8, 3], P('dp'), may hold values from 100 to 781, as said below
- cotangent: bfloat16 [13312, 768], P(('dp', 'mp')), may hold values from -6 to 6
- qkv_weight: float32 [3, 768, 768], P(None, 'dp', 'mp'), may hold values from -0.21875 to 0.21875
- out_weight: float32 [768, 768], P('mp', 'dp'), may hold values from -0.875 to 0.875
- up_weight: float32 [768, 3072], P('dp', 'mp'), may hold values from -0.21875 to 0.21875
- down_weight: float32 [3072, 768], P('mp', 'dp'), may hold values from -0.109375 to 0.109375
- head_bias: float32 [2, 768], P(None, 'mp'), may hold values from -4 to 4
- up_bias: float32 [3072], P('mp'), may hold values from -6 to 6
- norm_vectors: float32 [6, 768], replicated, may hold values from -1.2 to 1.6
- qkv_moment: float32 [3, 768, 768], P(None, 'dp', 'mp'), may hold values from -160 to 160
- out_moment: float32 [768, 768], P('mp', 'dp'), may hold values from -160 to 160
- up_moment: float32 [768, 3072], P('dp', 'mp'), may hold values from -160 to 160
- down_moment: float32 [3072, 768], P('mp', 'dp'), may hold values from -160 to 160
- head_bias_moment: float32 [2, 768], P(None, 'mp'), may hold values from -160 to 160
- up_bias_moment: float32 [3072], P('mp'), may hold values from -160 to 160
- norm_moment: float32 [6, 768], replicated, may hold values from -160 to 160
- qkv_average: float32 [3, 768, 768], P(None, 'dp', 'mp'), may hold values from -0.21875 to 0.21875
- out_average: float32 [768, 768], P('mp', 'dp'), may hold values from -0.875 to 0.875
- up_average: float32 [768, 3072], P('dp', 'mp'), may hold values from -0.21875 to 0.21875
- down_average: float32 [3072, 768], P('mp', 'dp'), may hold values from -0.109375 to 0.109375
- head_bias_average: float32 [2, 768], P(None, 'mp'), may hold values from -4 to 4
- up_bias_average: float32 [3072], P('mp'), may hold values from -6 to 6
- norm_average: float32 [6, 768], replicated, may hold values from -1.2 to 1.6
Outputs:
- layer_out: bfloat16 [13312, 768], P(('dp', 'mp'))
- tokens_grad: float32 [13312, 768], P(('dp', 'mp'))
- qkv_grad: float32 [3, 768, 768], P(None, 'dp', 'mp')
- out_grad: float32 [768, 768], P('mp', 'dp')
- up_grad: float32 [768, 3072], P('dp', 'mp')
- down_grad: float32 [3072, 768], P('mp', 'dp')
- head_bias_grad: float32 [2, 768], P(None, 'mp')
- up_bias_grad: float32 [3072], P('mp')
- norm_grad: float32 [6, 768], replicated
- qkv_next: float32 [3, 768, 768], P(None, 'dp', 'mp')
- out_next: float32 [768, 768], P('mp', 'dp')
- up_next: float32 [768, 3072], P('dp', 'mp')
- down_next: float32 [3072, 768], P('mp', 'dp')
- head_bias_next: float32 [2, 768], P(None, 'mp')
- up_bias_next: float32 [3072], P('mp')
- norm_next: float32 [6, 768], replicated
- qkv_moment_next: float32 [3, 768, 768], P(None, 'dp', 'mp')
- out_moment_next: float32 [768, 768], P('mp', 'dp')
- up_moment_next: float32 [768, 3072], P('dp', 'mp')
- down_moment_next: float32 [3072, 768], P('mp', 'dp')
- head_bias_moment_next: float32 [2, 768], P(None, 'mp')
- up_bias_moment_next: float32 [3072], P('mp')
- norm_moment_next: float32 [6, 768], replicated
- qkv_average_next: float32 [3, 768, 768], P(None, 'dp', 'mp')
- out_average_next: float32 [768, 768], P('mp', 'dp')
- up_average_next: float32 [768, 3072], P('dp', 'mp')
- down_average_next: float32 [3072, 768], P('mp', 'dp')
- head_bias_average_next: float32 [2, 768], P(None, 'mp')
- up_bias_average_next: float32 [3072], P('mp')
- norm_average_next: float32 [6, 768], replicated
The draws below stay inside these ranges and needn't reach their ends.
Inputs may be any that keep to these rules, and one draw needn't show every extreme that they name: Column b holds the lengths of bucket b: from 100 to 200, 200 to 400, 390 to 781; in every draw some utterance of each bucket has the bucket's most.
All inputs are finite; a program needn't handle non-finite values.
Results may differ from the reference program's by a relative error of at most 0.018.
Values may be sent and summed in bfloat16 or wider, within the bound.
A program may use at most 128 MiB of HBM per device.

```python
import math
import jax
import jax.numpy as jnp
from jax import lax

D = 768
HEADS = 12
HEAD_DIM = 64
FF = 3072
UTT = 1
LEN1 = 256
LEN2 = 512
LEN3 = 896
MOST1 = 200
MOST2 = 400
MOST3 = 781
GROUP = 1664
TOKENS = 13312
N_DP = 8


def draw_lengths(key, part):
    row_count = N_DP * UTT
    base = jax.random.fold_in(key, 11)
    key_len, key_pick = jax.random.split(base)
    lowest = jnp.array([MOST1 // 2, MOST2 // 2, MOST3 // 2], jnp.int32)
    highest = jnp.array([MOST1, MOST2, MOST3], jnp.int32)
    drawn = jax.random.randint(key_len, (row_count, 3), lowest[None, :], highest[None, :] + 1, dtype=jnp.int32)
    picked = jax.random.randint(key_pick, (3,), 0, row_count, dtype=jnp.int32)
    rows_index = jnp.arange(row_count, dtype=jnp.int32)[:, None]
    return jnp.where(rows_index == picked[None, :], highest[None, :], drawn).astype(jnp.int32)


def norm_rows(key, salt):
    noise = jnp.clip(jax.random.normal(jax.random.fold_in(key, salt), (6, D), jnp.float32), -4.0, 4.0)
    scales = jnp.array([0.3, 0.3, 0.15, 0.3, 0.15, 0.3], jnp.float32)
    offsets = jnp.array([0.0, 0.0, 1.0, 0.0, 1.0, 0.0], jnp.float32)
    return offsets[:, None] + scales[:, None] * noise


def draw_norm_vectors(key, part):
    return norm_rows(key, 21)


def draw_norm_average(key, part):
    return norm_rows(key, 22)


def block_scale(own_key, shape, shards, low, largest):
    loudness, own = 1.0, jax.random.fold_in(own_key, 6)
    for dim, parts in shards:
        draws = jnp.exp(jax.random.uniform(jax.random.fold_in(own, dim), (parts,), jnp.float32, low / len(shards), largest / len(shards)))
        loudness = loudness * jnp.repeat(draws, shape[dim] // parts).reshape([-1 if axis == dim else 1 for axis in range(len(shape))])
    return loudness


def bell_draw(own_key, dims, width, limit, cuts=(), kind=jnp.bfloat16):
    entries = jax.random.normal(own_key, dims, jnp.float32) * width
    if len(cuts) > 0:
        entries = block_scale(own_key, dims, cuts, -0.22, 0.18) * entries
    return jnp.clip(entries, min=-limit, max=limit).astype(kind)


def setup_inputs(seed: int = 0) -> dict:
    splits = jax.random.split(jax.random.key(seed), 25)
    tokens = bell_draw(splits[0], (TOKENS, D), 1.0, 6.0, ((0, 32),))
    lengths = draw_lengths(jax.random.fold_in(splits[24], 71), 0)
    cotangent = bell_draw(splits[2], (TOKENS, D), 1.0, 6.0, ((0, 32),))
    qkv_weight = bell_draw(splits[3], (3, D, D), D ** -0.5, 0.21875, ((1, 8), (2, 4)), jnp.float32)
    out_weight = bell_draw(splits[4], (D, D), (D // 16) ** -0.5, 0.875, ((0, 4), (1, 8)), jnp.float32)
    up_weight = bell_draw(splits[5], (D, FF), D ** -0.5, 0.21875, ((0, 8), (1, 4)), jnp.float32)
    down_weight = bell_draw(splits[6], (FF, D), FF ** -0.5, 0.109375, ((0, 4), (1, 8)), jnp.float32)
    head_bias = bell_draw(splits[7], (2, D), 0.3, 4.0, ((1, 4),), jnp.float32)
    up_bias = bell_draw(splits[8], (FF,), 0.5, 6.0, ((0, 4),), jnp.float32)
    norm_vectors = draw_norm_vectors(jax.random.fold_in(splits[24], 71), 0)
    qkv_moment = bell_draw(splits[10], (3, D, D), (0.3 * (1000 * N_DP * UTT) ** 0.5), 160.0, ((1, 8), (2, 4)), jnp.float32)
    out_moment = bell_draw(splits[11], (D, D), (0.3 * (1000 * N_DP * UTT) ** 0.5), 160.0, ((0, 4), (1, 8)), jnp.float32)
    up_moment = bell_draw(splits[12], (D, FF), (0.3 * (1000 * N_DP * UTT) ** 0.5), 160.0, ((0, 8), (1, 4)), jnp.float32)
    down_moment = bell_draw(splits[13], (FF, D), (0.3 * (1000 * N_DP * UTT) ** 0.5), 160.0, ((0, 4), (1, 8)), jnp.float32)
    head_bias_moment = bell_draw(splits[14], (2, D), (0.3 * (1000 * N_DP * UTT) ** 0.5), 160.0, ((1, 4),), jnp.float32)
    up_bias_moment = bell_draw(splits[15], (FF,), (0.3 * (1000 * N_DP * UTT) ** 0.5), 160.0, ((0, 4),), jnp.float32)
    norm_moment = bell_draw(splits[16], (6, D), (0.3 * (1000 * N_DP * UTT) ** 0.5), 160.0, (), jnp.float32)
    qkv_average = bell_draw(splits[17], (3, D, D), D ** -0.5, 0.21875, ((1, 8), (2, 4)), jnp.float32)
    out_average = bell_draw(splits[18], (D, D), (D // 16) ** -0.5, 0.875, ((0, 4), (1, 8)), jnp.float32)
    up_average = bell_draw(splits[19], (D, FF), D ** -0.5, 0.21875, ((0, 8), (1, 4)), jnp.float32)
    down_average = bell_draw(splits[20], (FF, D), FF ** -0.5, 0.109375, ((0, 4), (1, 8)), jnp.float32)
    head_bias_average = bell_draw(splits[21], (2, D), 0.3, 4.0, ((1, 4),), jnp.float32)
    up_bias_average = bell_draw(splits[22], (FF,), 0.5, 6.0, ((0, 4),), jnp.float32)
    norm_average = draw_norm_average(jax.random.fold_in(splits[24], 71), 0)
    return dict(tokens=tokens, lengths=lengths, cotangent=cotangent, qkv_weight=qkv_weight, out_weight=out_weight, up_weight=up_weight, down_weight=down_weight, head_bias=head_bias, up_bias=up_bias, norm_vectors=norm_vectors, qkv_moment=qkv_moment, out_moment=out_moment, up_moment=up_moment, down_moment=down_moment, head_bias_moment=head_bias_moment, up_bias_moment=up_bias_moment, norm_moment=norm_moment, qkv_average=qkv_average, out_average=out_average, up_average=up_average, down_average=down_average, head_bias_average=head_bias_average, up_bias_average=up_bias_average, norm_average=norm_average)


@jax.custom_vjp
def low(v):
    return lax.optimization_barrier(v.astype(jnp.bfloat16)).astype(jnp.float32)

@jax.custom_vjp
def low_back(v):
    return v

def low_keep(v):
    return (low(v), None)

def low_pass(kept, grad):
    return (grad,)

def back_keep(v):
    return (v, None)

def back_low(kept, grad):
    return (low(grad),)
low.defvjp(low_keep, low_pass)
low_back.defvjp(back_keep, back_low)
EPS = 1e-05
MOMENTUM = 0.5
DECAY = 0.5
RATE_SCALES = (0.02, 0.16, 0.02, 0.02, 0.02, 0.32, 0.16)
NEG_FILL = -1000000000.0

def layer_norm(values, gain_vec, shift_vec):
    center = values - lax.optimization_barrier(jnp.mean(values, axis=-1, keepdims=True))
    spread = lax.optimization_barrier(jnp.mean(center * center, axis=-1, keepdims=True))
    return center * lax.rsqrt(spread + EPS) * gain_vec + shift_vec

def bucket_list():
    listing = []
    offset = 0
    for bucket, extent in enumerate((LEN1, LEN2, LEN3)):
        listing.append((bucket, offset, extent))
        offset += UTT * extent
    return listing

def row_valid(lengths):
    pieces = []
    for bucket, offset, extent in bucket_list():
        inside = jnp.arange(extent)[None, :] < lengths[:, bucket][:, None]
        pieces.append(inside.astype(jnp.float32).reshape(UTT * extent))
    return jnp.concatenate(pieces)

def attend_slots(block_qkv, inside):
    highest = lax.Precision.HIGHEST
    score_scale = HEAD_DIM ** (-0.5)
    scores = jnp.einsum('uqhd,ukhd->uhqk', block_qkv[0], block_qkv[1], precision=highest) * score_scale
    scores = low_back(jnp.where(inside[:, None, None, :], scores, NEG_FILL))
    row_peak = lax.optimization_barrier(jnp.max(scores, axis=-1, keepdims=True))
    exp_scores = jnp.exp(scores - row_peak)
    probs = exp_scores / lax.optimization_barrier(jnp.sum(exp_scores, axis=-1, keepdims=True))
    return jnp.einsum('uhqk,ukhd->uqhd', low(probs), block_qkv[2], precision=highest)

def group_forward(params, rows_in, lengths):
    qkv_weight, out_weight, up_weight, down_weight, head_bias, up_bias, norm_vectors = params
    highest = lax.Precision.HIGHEST
    bias_rows = jnp.stack([head_bias[0], jnp.zeros_like(head_bias[0]), head_bias[1]])
    qkv = jnp.einsum('td,cde->cte', rows_in, low(qkv_weight), precision=highest) + bias_rows[:, None, :]
    qkv = low_back(low(qkv))
    outputs = []
    for bucket, offset, extent in bucket_list():
        block_qkv = qkv[:, offset:offset + UTT * extent].reshape(3, UTT, extent, HEADS, HEAD_DIM)
        inside = jnp.arange(extent)[None, :] < lengths[:, bucket][:, None]
        outputs.append(jax.checkpoint(attend_slots)(block_qkv, inside).reshape(UTT * extent, D))
    attn = low_back(low(jnp.concatenate(outputs, 0)))
    branch = low_back(jnp.dot(attn, low(out_weight), precision=highest))
    first = layer_norm(branch + norm_vectors[0] + rows_in, norm_vectors[2], norm_vectors[3])
    pre = low_back(jnp.dot(low(first), low(up_weight), precision=highest) + up_bias)
    hidden = low(jax.nn.gelu(pre, approximate=False))
    ffn = low_back(jnp.dot(hidden, low(down_weight), precision=highest))
    second = layer_norm(ffn + norm_vectors[1] + first, norm_vectors[4], norm_vectors[5])
    return second * row_valid(lengths)[:, None]

def reference(tokens, lengths, cotangent, qkv_weight, out_weight, up_weight, down_weight, head_bias, up_bias, norm_vectors, qkv_moment, out_moment, up_moment, down_moment, head_bias_moment, up_bias_moment, norm_moment, qkv_average, out_average, up_average, down_average, head_bias_average, up_bias_average, norm_average):
    params = (qkv_weight, out_weight, up_weight, down_weight, head_bias, up_bias, norm_vectors)
    moments = (qkv_moment, out_moment, up_moment, down_moment, head_bias_moment, up_bias_moment, norm_moment)
    averages = (qkv_average, out_average, up_average, down_average, head_bias_average, up_bias_average, norm_average)
    inputs = tokens.astype(jnp.float32).reshape(N_DP, GROUP, D)
    length_groups = lengths.reshape(N_DP, UTT, 3)

    def run_all(params_in, inputs_in):

        def one_group(pair):
            return jax.checkpoint(group_forward)(params_in, pair[0], pair[1])
        return lax.map(one_group, (inputs_in, length_groups))
    result, pullback = jax.vjp(run_all, params, inputs)
    grads, input_grads = pullback(cotangent.astype(jnp.float32).reshape(N_DP, GROUP, D))
    divisor = math.sqrt(1000.0 * N_DP * UTT)
    nexts, moment_nexts, average_nexts = ([], [], [])
    for weight, grad, moment, average, scale_one in zip(params, grads, moments, averages, RATE_SCALES):
        rate = scale_one / divisor
        moment_next = MOMENTUM * moment + grad
        weight_next = weight - rate * (grad + MOMENTUM * moment_next)
        nexts.append(weight_next)
        moment_nexts.append(moment_next)
        average_nexts.append(DECAY * average + (1.0 - DECAY) * weight_next)
    layer_out = result.reshape(TOKENS, D).astype(jnp.bfloat16)
    tokens_grad = input_grads.reshape(TOKENS, D)
    return (layer_out, tokens_grad, grads[0], grads[1], grads[2], grads[3], grads[4], grads[5], grads[6], nexts[0], nexts[1], nexts[2], nexts[3], nexts[4], nexts[5], nexts[6], moment_nexts[0], moment_nexts[1], moment_nexts[2], moment_nexts[3], moment_nexts[4], moment_nexts[5], moment_nexts[6], average_nexts[0], average_nexts[1], average_nexts[2], average_nexts[3], average_nexts[4], average_nexts[5], average_nexts[6])
```

```python
import math

import jax
import jax.numpy as jnp
from jax import lax
from jax.sharding import PartitionSpec as P

HEAD_DIM = 64
UTT = 1
LENS = (256, 512, 896)
MOSTS = (200, 400, 781)

EPS = 1e-05
MOMENTUM = 0.5
DECAY = 0.5
RATE_SCALES = (0.02, 0.16, 0.02, 0.02, 0.02, 0.32, 0.16)
NEG_FILL = -1000000000.0
BF16 = jnp.bfloat16
F32 = jnp.float32


def dot(a, b, dims):
    return lax.dot_general(a, b, (dims, ((), ())), preferred_element_type=F32)


CORE_SWAP = [(0, 1), (1, 0), (2, 3), (3, 2)]
HALF_SWAP = [(0, 2), (2, 0), (1, 3), (3, 1)]


def core_swap(value):
    return lax.ppermute(value, "mp", CORE_SWAP)


def half_swap(value):
    return lax.ppermute(value, "mp", HALF_SWAP)


def dp_dims(size):
    dims = []
    while size % 4 == 0:
        dims.append(4)
        size //= 4
    if size > 1:
        dims.append(size)
    return tuple(dims)


class Grid:
    def __init__(self, size):
        self.dims = dp_dims(size)
        self.size = size
        rank = lax.axis_index("dp")
        self.strides = []
        stride = size
        for extent in self.dims:
            stride //= extent
            self.strides.append(stride)
        self.coords = [lax.rem(rank // s, e) for s, e in zip(self.strides, self.dims)]

    def send(self, value, stage, ahead):
        extent, stride = self.dims[stage], self.strides[stage]
        pairs = []
        for source in range(self.size):
            at = source // stride % extent
            pairs.append((source, source + ((at + ahead) % extent - at) * stride))
        return lax.ppermute(value, "dp", pairs)


def put(buffer, piece, axis, index):
    starts = [0] * buffer.ndim
    starts[axis] = index
    return lax.dynamic_update_slice(buffer, jnp.expand_dims(piece, axis), tuple(starts))


def take(buffer, axis, index):
    return lax.dynamic_index_in_dim(buffer, index, axis, keepdims=False)


def gather_half(grid, shard, half_stage):
    rows, columns = shard.shape
    value = shard[None]
    done = 0
    order = list(range(len(grid.dims)))
    for stage in order:
        if done == half_stage:
            value = jnp.concatenate([value, half_swap(value)], 0)
        extent, coord = grid.dims[stage], grid.coords[stage]
        axis = 1 + done
        shape = value.shape[:axis] + (extent,) + value.shape[axis:]
        buffer = put(jnp.zeros(shape, value.dtype), value, axis, coord)
        for ahead in range(1, extent):
            source = lax.rem(coord + extent - ahead, extent)
            buffer = put(buffer, grid.send(value, stage, ahead), axis, source)
        value = buffer
        done += 1
    if done == half_stage:
        other = half_swap(value)
        return value.reshape(-1, columns), other.reshape(-1, columns)
    return value[0].reshape(-1, columns), value[1].reshape(-1, columns)


def scatter_sum(grid, mine, theirs, half_first):
    columns = mine.shape[1]
    shape = grid.dims + (mine.shape[0] // grid.size, columns)
    order = list(range(len(grid.dims)))[::-1]

    def along(value, stage):
        extent, coord = grid.dims[stage], grid.coords[stage]
        axis = value.ndim - 3
        total = take(value, axis, coord).astype(F32)
        for ahead in range(1, extent):
            piece = take(value, axis, lax.rem(coord + ahead, extent))
            total = total + grid.send(piece.astype(BF16), stage, ahead).astype(F32)
        return total

    mine, theirs = mine.reshape(shape), theirs.reshape(shape)
    if half_first:
        value = mine.astype(F32) + half_swap(theirs.astype(BF16)).astype(F32)
        for stage in order:
            value = along(value, stage)
        return value
    first = order[0]
    mine = along(mine, first)
    theirs = along(theirs, first)
    value = mine + half_swap(theirs.astype(BF16)).astype(F32)
    for stage in order[1:]:
        value = along(value, stage)
    return value


def sum_all(grid, value, over_cores):
    for stage in range(len(grid.dims)):
        total = value
        for ahead in range(1, grid.dims[stage]):
            total = total + grid.send(value, stage, ahead)
        value = total
    value = value + half_swap(value)
    if over_cores:
        value = value + core_swap(value)
    return value


def offsets():
    listing, offset = [], 0
    for extent in LENS:
        listing.append(offset)
        offset += UTT * extent
    return listing


def move_plan(rows_local):
    start = offsets()[2]
    count = 2 * rows_local - start
    free = -(-(start + MOSTS[2] - 3 * rows_local) // 16) * 16
    return rows_local - count, free, count


def row_table(rows_local, member, lengths):
    source, free, count = move_plan(rows_local)
    starts = offsets()
    local = jnp.arange(rows_local)
    row = member * rows_local + local
    slot = (row >= starts[1]).astype(jnp.int32) + (row >= starts[2]).astype(jnp.int32)
    place = row - jnp.where(slot == 0, starts[0], jnp.where(slot == 1, starts[1], starts[2]))
    arrived = (member == 3) & (local >= free) & (local < free + count)
    left = (member == 1) & (local >= source)
    place = jnp.where(arrived, local - free, place)
    length = jnp.where(slot == 0, lengths[0, 0], jnp.where(slot == 1, lengths[0, 1], lengths[0, 2]))
    return slot, (place < length) & ~left


def bring(rows, member):
    source, free, count = move_plan(rows.shape[0])
    moved = lax.ppermute(rows[source:], "mp", [(1, 3)])
    placed = lax.dynamic_update_slice(rows, moved, (free, 0))
    return jnp.where(member == 3, placed, rows)


def send_back(rows, member):
    source, free, count = move_plan(rows.shape[0])
    moved = lax.ppermute(rows[free : free + count], "mp", [(3, 1)])
    placed = lax.dynamic_update_slice(rows, moved, (source, 0))
    cleared = lax.dynamic_update_slice(rows, jnp.zeros_like(moved), (free, 0))
    return jnp.where(member == 1, placed, jnp.where(member == 3, cleared, rows))


def norm_stats(values):
    mean = jnp.mean(values, axis=-1, keepdims=True)
    center = values - mean
    spread = jnp.mean(center * center, axis=-1, keepdims=True)
    inverse = lax.rsqrt(spread + EPS)
    return center * inverse, inverse


def norm_back(grad, unit, inverse, gain):
    scaled = grad * gain
    return inverse * (
        scaled
        - jnp.mean(scaled, axis=-1, keepdims=True)
        - unit * jnp.mean(scaled * unit, axis=-1, keepdims=True)
    )


def attend(query, keys, values, allowed):
    scores = jnp.einsum("qhd,khd->hqk", query, keys, preferred_element_type=F32)
    scores = jnp.where(allowed[None], scores * HEAD_DIM ** (-0.5), NEG_FILL)
    peak = jnp.max(scores, axis=-1, keepdims=True)
    weights = jnp.exp(scores - peak)
    total = jnp.sum(weights, axis=-1, keepdims=True)
    low = (weights / total).astype(BF16)
    out = jnp.einsum("hqk,khd->qhd", low, values, preferred_element_type=F32)
    return out.astype(BF16), peak + jnp.log(total)


def attend_back(query, keys, values, allowed, log_sum, grad):
    scale = HEAD_DIM ** (-0.5)
    scores = jnp.einsum("qhd,khd->hqk", query, keys, preferred_element_type=F32)
    scores = jnp.where(allowed[None], scores * scale, NEG_FILL)
    probs = jnp.exp(scores - log_sum)
    d_values = jnp.einsum("hqk,qhd->khd", probs.astype(BF16), grad, preferred_element_type=F32)
    d_probs = jnp.einsum("qhd,khd->hqk", grad, values, preferred_element_type=F32)
    mean = jnp.sum(probs * d_probs, axis=-1, keepdims=True)
    low = (probs * (d_probs - mean)).astype(BF16)
    d_query = jnp.einsum("hqk,khd->qhd", low, keys, preferred_element_type=F32) * scale
    d_keys = jnp.einsum("hqk,qhd->khd", low, query, preferred_element_type=F32) * scale
    return d_query.astype(BF16), d_keys.astype(BF16), d_values.astype(BF16)


def update_one(rate, weight, grad, moment, average):
    moment_next = MOMENTUM * moment + grad
    weight_next = weight - rate * (grad + MOMENTUM * moment_next)
    return (weight_next, moment_next, DECAY * average + (1.0 - DECAY) * weight_next)


def on_device(
    tokens,
    lengths,
    cotangent,
    qkv_weight,
    out_weight,
    up_weight,
    down_weight,
    head_bias,
    up_bias,
    norm_vectors,
    qkv_moment,
    out_moment,
    up_moment,
    down_moment,
    head_bias_moment,
    up_bias_moment,
    norm_moment,
    qkv_average,
    out_average,
    up_average,
    down_average,
    head_bias_average,
    up_bias_average,
    norm_average,
):
    grid = Grid(lax.axis_size("dp"))
    member = lax.axis_index("mp")
    mate = member + 1 - 2 * lax.rem(member, 2)
    rows_local, width = tokens.shape
    head_width = qkv_weight.shape[2]
    stages = len(grid.dims)

    qkv_shard = jnp.transpose(qkv_weight, (1, 0, 2)).reshape(-1, 3 * head_width).astype(BF16)
    qkv_pair = gather_half(grid, qkv_shard, stages)
    out_pair = gather_half(grid, out_weight.astype(BF16).T, stages - 1)
    up_pair = gather_half(grid, up_weight.astype(BF16), stages)
    down_pair = gather_half(grid, down_weight.astype(BF16).T, stages - 1)
    bias_pair = (head_bias, half_swap(head_bias))
    up_bias_pair = (up_bias, half_swap(up_bias))

    slot_own, valid_own = row_table(rows_local, member, lengths)
    slot_mate, valid_mate = row_table(rows_local, mate, lengths)
    slot = jnp.concatenate([slot_own, slot_mate])
    frame = jnp.concatenate([valid_own, valid_mate])
    allowed = (slot[:, None] == slot[None, :]) & frame[None, :]
    live = valid_own[:, None]

    def share(rows):
        return jnp.concatenate([rows, core_swap(rows)], 0)

    def settle(partial):
        return partial[:rows_local] + core_swap(partial[rows_local:].astype(BF16)).astype(F32)

    own_tokens = bring(tokens, member)
    own_cotangent = bring(cotangent, member)
    tokens_all = share(own_tokens)

    heads = 2 * head_width // HEAD_DIM
    parts = []
    for weight, bias in zip(qkv_pair, bias_pair):
        rows_bias = jnp.concatenate([bias[0], jnp.zeros_like(bias[0]), bias[1]])
        act = (dot(tokens_all, weight, ((1,), (0,))) + rows_bias).astype(BF16)
        parts.append(act.reshape(2 * rows_local, 3, -1, HEAD_DIM))
    act = jnp.concatenate(parts, 2)
    query, keys, values = act[:, 0], act[:, 1], act[:, 2]
    attn, log_sum = attend(query, keys, values, allowed)
    attn = attn.reshape(2 * rows_local, -1)
    out_both = jnp.concatenate(out_pair, 1)
    branch = settle(dot(attn, out_both, ((1,), (1,))))
    unit_one, inverse_one = norm_stats(branch + norm_vectors[0] + own_tokens.astype(F32))
    first = unit_one * norm_vectors[2] + norm_vectors[3]
    first_all = share(first.astype(BF16))

    up_both = jnp.concatenate(up_pair, 1)
    down_both = jnp.concatenate(down_pair, 1)
    pre = dot(first_all, up_both, ((1,), (0,))) + jnp.concatenate(up_bias_pair)
    phi = 0.5 * (1.0 + lax.erf(pre * (0.5**0.5)))
    density = jnp.exp(-0.5 * pre * pre) * (1.0 / math.sqrt(2.0 * math.pi))
    hidden = (pre * phi).astype(BF16)
    slope = (phi + pre * density).astype(BF16)
    ffn = settle(dot(hidden, down_both, ((1,), (1,))))
    unit_two, inverse_two = norm_stats(ffn + norm_vectors[1] + first)
    second = unit_two * norm_vectors[4] + norm_vectors[5]
    layer_out = send_back(jnp.where(live, second, 0.0).astype(BF16), member)

    grad_two = jnp.where(live, own_cotangent.astype(F32), 0.0)
    d_second = norm_back(grad_two, unit_two, inverse_two, norm_vectors[4])
    d_ffn_all = share(d_second.astype(BF16))
    d_hidden = dot(d_ffn_all, down_both, ((1,), (0,)))
    d_pre = (d_hidden * slope.astype(F32)).astype(BF16)
    d_first = settle(dot(d_pre, up_both, ((1,), (1,)))) + d_second
    units = up_weight.shape[1]
    grad_down = [
        dot(d_ffn_all, hidden[:, at : at + units], ((0,), (0,))).astype(BF16) for at in (0, units)
    ]
    sum_down = scatter_sum(grid, *grad_down, True).T
    grad_up = [
        dot(first_all, d_pre[:, at : at + units], ((0,), (0,))).astype(BF16) for at in (0, units)
    ]
    sum_up = scatter_sum(grid, *grad_up, False)
    grad_up_bias = jnp.sum(d_pre, axis=0, dtype=F32)

    d_branch = norm_back(d_first, unit_one, inverse_one, norm_vectors[2])
    d_branch_all = share(d_branch.astype(BF16))
    d_attn = dot(d_branch_all, out_both, ((1,), (0,))).astype(BF16)
    grad_out = [
        dot(d_branch_all, attn[:, at : at + head_width], ((0,), (0,))).astype(BF16)
        for at in (0, head_width)
    ]
    sum_out = scatter_sum(grid, *grad_out, True).T
    d_query, d_keys, d_values = attend_back(
        query, keys, values, allowed, log_sum, d_attn.reshape(2 * rows_local, heads, HEAD_DIM)
    )
    half_heads = heads // 2
    d_parts = []
    for at in (0, half_heads):
        d_parts.append(
            jnp.concatenate(
                [
                    piece[:, at : at + half_heads].reshape(2 * rows_local, -1)
                    for piece in (d_query, d_keys, d_values)
                ],
                1,
            )
        )
    grad_qkv = [dot(tokens_all, part, ((0,), (0,))).astype(BF16) for part in d_parts]
    sum_qkv = scatter_sum(grid, *grad_qkv, True)
    sum_qkv = jnp.transpose(sum_qkv.reshape(-1, 3, head_width), (1, 0, 2))
    grad_bias = [jnp.sum(part, axis=0, dtype=F32) for part in d_parts]
    d_tokens = settle(
        dot(d_parts[0], qkv_pair[0], ((1,), (1,))) + dot(d_parts[1], qkv_pair[1], ((1,), (1,)))
    )
    tokens_grad = send_back(d_tokens + d_branch, member)

    norm_part = jnp.stack(
        [
            jnp.sum(d_branch, axis=0),
            jnp.sum(d_second, axis=0),
            jnp.sum(d_first * unit_one, axis=0),
            jnp.sum(d_first, axis=0),
            jnp.sum(grad_two * unit_two, axis=0),
            jnp.sum(grad_two, axis=0),
        ]
    )
    sum_norm = sum_all(grid, norm_part, True)

    def sum_half(pair):
        value = pair[0] + half_swap(pair[1])
        for stage in range(stages):
            total = value
            for ahead in range(1, grid.dims[stage]):
                total = total + grid.send(value, stage, ahead)
            value = total
        return value

    sum_up_bias = sum_half((grad_up_bias[:units], grad_up_bias[units:]))
    sum_bias = sum_half(grad_bias)
    sum_head_bias = jnp.stack([sum_bias[:head_width], sum_bias[2 * head_width :]])

    divisor = math.sqrt(1000.0 * grid.size * UTT)
    params = (qkv_weight, out_weight, up_weight, down_weight, head_bias, up_bias, norm_vectors)
    grads = (sum_qkv, sum_out, sum_up, sum_down, sum_head_bias, sum_up_bias, sum_norm)
    moments = (
        qkv_moment,
        out_moment,
        up_moment,
        down_moment,
        head_bias_moment,
        up_bias_moment,
        norm_moment,
    )
    averages = (
        qkv_average,
        out_average,
        up_average,
        down_average,
        head_bias_average,
        up_bias_average,
        norm_average,
    )
    nexts, moment_nexts, average_nexts = ([], [], [])
    for weight, grad, moment, average, scale_one in zip(
        params, grads, moments, averages, RATE_SCALES
    ):
        weight_next, moment_next, average_next = update_one(
            scale_one / divisor, weight, grad, moment, average
        )
        nexts.append(weight_next)
        moment_nexts.append(moment_next)
        average_nexts.append(average_next)
    return (layer_out, tokens_grad, *grads, *nexts, *moment_nexts, *average_nexts)


ROWS = P(("dp", "mp"), None)
PARAMS = (
    P(None, "dp", "mp"),
    P("mp", "dp"),
    P("dp", "mp"),
    P("mp", "dp"),
    P(None, "mp"),
    P("mp"),
    P(),
)


def solution(mesh):
    return jax.shard_map(
        on_device,
        mesh=mesh,
        in_specs=(ROWS, P("dp", None), ROWS) + PARAMS * 3,
        out_specs=(ROWS, ROWS) + PARAMS * 4,
        check_vma=False,
    )
```

```python
import math

import jax
import jax.numpy as jnp
from jax import lax
from jax.experimental import pallas as pl
from jax.experimental.pallas import tpu as pltpu
from jax.sharding import PartitionSpec as P

HEAD_DIM = 64
UTT = 1
LENS = (256, 512, 896)
MOSTS = (200, 400, 781)

EPS = 1e-05
MOMENTUM = 0.5
DECAY = 0.5
RATE_SCALES = (0.02, 0.16, 0.02, 0.02, 0.02, 0.32, 0.16)
NEG_FILL = -1000000000.0
BF16 = jnp.bfloat16
F32 = jnp.float32


def dot(a, b, dims):
    return lax.dot_general(a, b, (dims, ((), ())), preferred_element_type=F32)


CORE_SWAP = [(0, 1), (1, 0), (2, 3), (3, 2)]
HALF_SWAP = [(0, 2), (2, 0), (1, 3), (3, 1)]


def core_swap(value):
    return lax.ppermute(value, "mp", CORE_SWAP)


def half_swap(value):
    return lax.ppermute(value, "mp", HALF_SWAP)


def dp_dims(size):
    dims = []
    while size % 4 == 0:
        dims.append(4)
        size //= 4
    if size > 1:
        dims.append(size)
    return tuple(dims)


class Grid:
    def __init__(self, size):
        self.dims = dp_dims(size)
        self.size = size
        rank = lax.axis_index("dp")
        self.strides = []
        stride = size
        for extent in self.dims:
            stride //= extent
            self.strides.append(stride)
        self.coords = [lax.rem(rank // s, e) for s, e in zip(self.strides, self.dims)]

    def send(self, value, stage, ahead):
        extent, stride = self.dims[stage], self.strides[stage]
        pairs = []
        for source in range(self.size):
            at = source // stride % extent
            pairs.append((source, source + ((at + ahead) % extent - at) * stride))
        return lax.ppermute(value, "dp", pairs)


def put(buffer, piece, axis, index):
    starts = [0] * buffer.ndim
    starts[axis] = index
    return lax.dynamic_update_slice(buffer, jnp.expand_dims(piece, axis), tuple(starts))


def take(buffer, axis, index):
    return lax.dynamic_index_in_dim(buffer, index, axis, keepdims=False)


def gather_half(grid, shard, half_stage):
    rows, columns = shard.shape
    value = shard[None]
    done = 0
    order = list(range(len(grid.dims)))
    for stage in order:
        if done == half_stage:
            value = jnp.concatenate([value, half_swap(value)], 0)
        extent, coord = grid.dims[stage], grid.coords[stage]
        axis = 1 + done
        shape = value.shape[:axis] + (extent,) + value.shape[axis:]
        buffer = put(jnp.zeros(shape, value.dtype), value, axis, coord)
        for ahead in range(1, extent):
            source = lax.rem(coord + extent - ahead, extent)
            buffer = put(buffer, grid.send(value, stage, ahead), axis, source)
        value = buffer
        done += 1
    if done == half_stage:
        other = half_swap(value)
        return value.reshape(-1, columns), other.reshape(-1, columns)
    return value[0].reshape(-1, columns), value[1].reshape(-1, columns)


def scatter_sum(grid, mine, theirs, half_first):
    columns = mine.shape[1]
    shape = grid.dims + (mine.shape[0] // grid.size, columns)
    order = list(range(len(grid.dims)))[::-1]

    def along(value, stage):
        extent, coord = grid.dims[stage], grid.coords[stage]
        axis = value.ndim - 3
        total = take(value, axis, coord).astype(F32)
        for ahead in range(1, extent):
            piece = take(value, axis, lax.rem(coord + ahead, extent))
            total = total + grid.send(piece.astype(BF16), stage, ahead).astype(F32)
        return total

    mine, theirs = mine.reshape(shape), theirs.reshape(shape)
    if half_first:
        value = mine.astype(F32) + half_swap(theirs.astype(BF16)).astype(F32)
        for stage in order:
            value = along(value, stage)
        return value
    first = order[0]
    mine = along(mine, first)
    theirs = along(theirs, first)
    value = mine + half_swap(theirs.astype(BF16)).astype(F32)
    for stage in order[1:]:
        value = along(value, stage)
    return value


def sum_half(grid, pair):
    value = pair[0] + half_swap(pair[1])
    for stage in range(len(grid.dims)):
        total = value
        for ahead in range(1, grid.dims[stage]):
            total = total + grid.send(value, stage, ahead)
        value = total
    return value


def sum_all(grid, value, over_cores):
    for stage in range(len(grid.dims)):
        total = value
        for ahead in range(1, grid.dims[stage]):
            total = total + grid.send(value, stage, ahead)
        value = total
    value = value + half_swap(value)
    if over_cores:
        value = value + core_swap(value)
    return value


def offsets():
    listing, offset = [], 0
    for extent in LENS:
        listing.append(offset)
        offset += UTT * extent
    return listing


def move_plan(rows_local):
    start = offsets()[2]
    count = 2 * rows_local - start
    free = -(-(start + MOSTS[2] - 3 * rows_local) // 16) * 16
    return rows_local - count, free, count


def row_table(rows_local, member, lengths):
    source, free, count = move_plan(rows_local)
    starts = offsets()
    local = jnp.arange(rows_local)
    row = member * rows_local + local
    slot = (row >= starts[1]).astype(jnp.int32) + (row >= starts[2]).astype(jnp.int32)
    place = row - jnp.where(slot == 0, starts[0], jnp.where(slot == 1, starts[1], starts[2]))
    arrived = (member == 3) & (local >= free) & (local < free + count)
    left = (member == 1) & (local >= source)
    place = jnp.where(arrived, local - free, place)
    length = jnp.where(slot == 0, lengths[0, 0], jnp.where(slot == 1, lengths[0, 1], lengths[0, 2]))
    return slot, (place < length) & ~left


def bring(rows, member):
    source, free, count = move_plan(rows.shape[0])
    moved = lax.ppermute(rows[source:], "mp", [(1, 3)])
    placed = lax.dynamic_update_slice(rows, moved, (free, 0))
    return jnp.where(member == 3, placed, rows)


def put_back(rows, moved, member):
    source, free, count = move_plan(rows.shape[0])
    placed = lax.dynamic_update_slice(rows, moved, (source, 0))
    cleared = lax.dynamic_update_slice(rows, jnp.zeros_like(moved), (free, 0))
    return jnp.where(member == 1, placed, jnp.where(member == 3, cleared, rows))


def send_back(rows, member):
    source, free, count = move_plan(rows.shape[0])
    return put_back(rows, lax.ppermute(rows[free : free + count], "mp", [(3, 1)]), member)


CHAIN = 4
X_FIRST = (False, True, True, False)
WHERE = [(0, 0)] + [(step, sign) for step in range(1, CHAIN) for sign in (1, -1)]


class Place:
    def __init__(self):
        self.dp = lax.axis_index("dp")
        self.mp = lax.axis_index("mp")
        self.z = self.dp // 2
        self.x = lax.rem(self.dp, 2)
        self.up = (self.dp + 2, self.mp)
        self.down = (self.dp - 2, self.mp)
        self.across = (self.dp + 1 - 2 * self.x, self.mp)
        self.other = (self.dp, lax.rem(self.mp + 2, 4))
        self.mate = (self.dp, self.mp + 1 - 2 * lax.rem(self.mp, 2))
        self.has_up = self.z < CHAIN - 1
        self.has_down = self.z > 0

    def ring(self, ahead):
        return (lax.rem(self.dp + 2 * ahead, 2 * CHAIN), self.mp)

    def greet(self, peers):
        barrier = pltpu.get_barrier_semaphore()
        for peer in peers:
            pl.semaphore_signal(
                barrier, inc=1, device_id=peer, device_id_type=pl.DeviceIdType.MESH
            )
        pl.semaphore_wait(barrier, len(peers))


def remote(source, target, sends, arrivals, index, device):
    return pltpu.make_async_remote_copy(
        source,
        target,
        sends.at[index],
        arrivals.at[index],
        device_id=device,
        device_id_type=pl.DeviceIdType.MESH,
    )


def gather_kernel(row_plan, *refs):
    shards, (rows_ref, cot_ref, vec_ref) = refs[0:4], refs[4:7]
    fulls, (rows_out, cot_out, vec_out) = refs[7:11], refs[11:14]
    sends, arrivals, side_send, side_arrive, local = refs[14:19]
    here = Place()
    source, free, count = row_plan
    n_rows = rows_ref.shape[0]
    here.greet([here.ring(1), here.ring(2), here.ring(3), here.across, here.other, here.mate,
                (here.dp, 3 - here.mp)])

    def z_of(where):
        step, sign = where
        return here.z - step * sign

    def held(where):
        step, sign = where
        if step == 0:
            return None
        return here.z >= step if sign > 0 else here.z + step < CHAIN

    def maybe(condition, action):
        if condition is None:
            action()
        else:
            pl.when(condition)(action)

    def block(w, where, far, half):
        x = 1 - here.x if far else here.x
        return fulls[w].at[half, z_of(where) * 2 + x]

    def chain(w, where):
        step, sign = where
        origin = shards[w] if step == 0 else block(w, where, False, 0)
        jobs = []
        for way in (1, -1) if step == 0 else (sign,):
            index = step + (0 if way > 0 else 3)
            device = here.up if way > 0 else here.down
            go = here.has_up if way > 0 else here.has_down
            if step < CHAIN - 1:
                jobs.append((go, remote(origin, block_to(w, where), sends.at[w], arrivals.at[w], index, device)))
        return jobs

    def block_to(w, where):
        return fulls[w].at[0, z_of(where) * 2 + here.x]

    def second(w, where):
        origin = shards[w] if where[0] == 0 else block(w, where, False, 0)
        index = 6 + WHERE.index(where)
        if X_FIRST[w]:
            return remote(origin, block(w, where, False, 0), sends.at[w], arrivals.at[w], index, here.across)
        return remote(origin, block(w, where, False, 1), sends.at[w], arrivals.at[w], index, here.other)

    def third(w, where, arrived):
        index = 13 + WHERE.index(where) + (len(WHERE) if arrived else 0)
        if X_FIRST[w]:
            origin = shards[w] if where[0] == 0 and not arrived else block(w, where, arrived, 0)
            return remote(origin, block(w, where, arrived, 1), sends.at[w], arrivals.at[w], index, here.other)
        origin = shards[w] if where[0] == 0 and not arrived else block(w, where, False, int(arrived))
        return remote(origin, block(w, where, False, int(arrived)), sends.at[w], arrivals.at[w], index, here.across)

    def landing(w, where, stage, arrived=False):
        if stage == 2:
            index = 6 + WHERE.index(where)
            target = block(w, where, True, 0) if X_FIRST[w] else block(w, where, False, 1)
            device = here.across if X_FIRST[w] else here.other
        else:
            index = 13 + WHERE.index(where) + (len(WHERE) if arrived else 0)
            if X_FIRST[w]:
                target, device = block(w, where, arrived, 1), here.other
            else:
                target, device = block(w, where, True, int(arrived)), here.across
        return remote(target, target, sends.at[w], arrivals.at[w], index, device)

    def chain_landing(w, where):
        step, sign = where
        index = step - 1 + (0 if sign > 0 else 3)
        target = block(w, where, False, 0)
        return remote(target, target, sends.at[w], arrivals.at[w], index, here.down if sign > 0 else here.up)

    order = (0, 1, 3, 2)
    by_step = [[p for p in WHERE if p[0] == step] for step in range(CHAIN)]

    low, high = pl.ds(0, free), pl.ds(free + count, n_rows - free - count)
    middle, tail = pl.ds(free, count), pl.ds(source, count)
    locals_ = [(None, pltpu.make_async_copy(shards[w], fulls[w].at[0, here.dp], local.at[w])) for w in order]
    not_last, second_core = here.mp != 3, here.mp == 1
    for n, (given, taken) in enumerate(((rows_ref, rows_out.at[0]), (cot_ref, cot_out))):
        for m, part in enumerate((low, high, middle)):
            copy = pltpu.make_async_copy(given.at[part], taken.at[part], local.at[4 + 3 * n + m])
            locals_.append((not_last if m == 2 else None, copy))
    for condition, copy in locals_:
        maybe(condition, copy.start)

    def to_mate(m, part):
        return remote(rows_ref.at[part], rows_out.at[1, part], side_send, side_arrive, m, here.mate)

    side = [(None, to_mate(0, low)), (None, to_mate(1, high)), (not_last, to_mate(2, middle))]
    side.append((None, remote(vec_ref, vec_out, side_send, side_arrive, 3, here.other)))
    moved = [
        remote(rows_ref.at[tail], rows_out.at[0, middle], side_send, side_arrive, 4, here.other),
        remote(cot_ref.at[tail], cot_out.at[middle], side_send, side_arrive, 5, here.other),
        remote(rows_ref.at[tail], rows_out.at[1, middle], side_send, side_arrive, 6, (here.dp, 3 - here.mp)),
    ]
    side += [(second_core, copy) for copy in moved]

    started = []

    def start(condition, copy):
        maybe(condition, copy.start)
        started.append((condition, copy))

    for condition, copy in side:
        start(condition, copy)
    for step in range(CHAIN):
        for where in by_step[step]:
            for w in order:
                if step > 0:
                    maybe(held(where), chain_landing(w, where).wait_recv)
                for go, copy in chain(w, where):
                    both = go if held(where) is None else jnp.logical_and(go, held(where))
                    start(both, copy)
                start(held(where), second(w, where))
                start(held(where), third(w, where, False))
        for where in by_step[step - 1] if step > 0 else ():
            for w in order:
                maybe(held(where), landing(w, where, 2).wait_recv)
                start(held(where), third(w, where, True))
    for where in by_step[CHAIN - 1]:
        for w in order:
            maybe(held(where), landing(w, where, 2).wait_recv)
            start(held(where), third(w, where, True))
    for where in WHERE:
        for w in order:
            for arrived in (False, True):
                maybe(held(where), landing(w, where, 3, arrived).wait_recv)
    to_mate(0, low).wait_recv()
    to_mate(1, high).wait_recv()
    pl.when(here.mp != 2)(to_mate(2, middle).wait_recv)
    side[3][1].wait_recv()
    pl.when(here.mp == 3)(moved[0].wait_recv)
    pl.when(here.mp == 3)(moved[1].wait_recv)
    pl.when(here.mp == 2)(moved[2].wait_recv)
    for condition, copy in started:
        maybe(condition, copy.wait_send)
    for condition, copy in locals_:
        maybe(condition, copy.wait)


def gather_all(shards, rows, cotangent, vectors):
    rows_local, width = rows.shape
    vmem, anywhere = pl.BlockSpec(memory_space=pltpu.VMEM), pl.BlockSpec(memory_space=pl.ANY)
    shapes = [jax.ShapeDtypeStruct((2, 2 * CHAIN) + s.shape, s.dtype) for s in shards]
    shapes += [
        jax.ShapeDtypeStruct((2, rows_local, width), rows.dtype),
        jax.ShapeDtypeStruct((rows_local, width), rows.dtype),
        jax.ShapeDtypeStruct(vectors.shape, vectors.dtype),
    ]
    plan = move_plan(rows_local)
    return pl.pallas_call(
        lambda *refs: gather_kernel(plan, *refs),
        out_shape=shapes,
        in_specs=[vmem] * 7,
        out_specs=[anywhere] * 6 + [vmem],
        scratch_shapes=[
            pltpu.SemaphoreType.DMA((4, 27)),
            pltpu.SemaphoreType.DMA((4, 27)),
            pltpu.SemaphoreType.DMA((7,)),
            pltpu.SemaphoreType.DMA((7,)),
            pltpu.SemaphoreType.DMA((10,)),
        ],
        compiler_params=pltpu.CompilerParams(
            collective_id=0, has_side_effects=True, vmem_limit_bytes=16 * 2**20
        ),
        name="gather_all",
    )(*shards, rows, cotangent, vectors)


def scatter_kernel(*refs):
    mine, theirs = refs[0:4], refs[4:8]
    vec_ref, out_edge, grad_edge = refs[8:11]
    sums, (vec_out, out_back, grad_back) = refs[11:15], refs[15:18]
    firsts, seconds, rises, falls = refs[18:22], refs[22:26], refs[26:30], refs[30:34]
    vec_in, sends, arrivals, side_send, side_arrive = refs[34:39]
    here = Place()
    here.greet([here.ring(1), here.ring(2), here.ring(3), here.across, here.other, here.mate])
    order = (2, 3, 1, 0)
    targets = (3, 0, 2, 1)
    far = 1 - here.x
    started = []

    def start(copy, condition=None):
        if condition is None:
            copy.start()
        else:
            pl.when(condition)(copy.start)
        started.append((condition, copy))
        return copy

    def add(target, more):
        target[...] = (target[...].astype(F32) + more[...].astype(F32)).astype(BF16)

    edges = []
    for index, (given, taken) in enumerate(((out_edge, out_back), (grad_edge, grad_back))):
        copy = remote(given, taken, side_send, side_arrive, 6 + index, here.other)
        edges.append(start(copy, here.mp == 3))

    def vec_send(index, device):
        copy = remote(vec_out, vec_in.at[index], side_send, side_arrive, index, device)
        copy.start()
        return copy

    vec_out[...] = vec_ref[...]
    sent = vec_send(0, here.other)

    first_jobs, second_jobs = {}, {}
    for target in targets:
        for w in order:
            for part in (0, 1):
                if X_FIRST[w]:
                    origin, device = theirs[w].at[target, part], here.other
                else:
                    origin, device = (mine, theirs)[part][w].at[target, far], here.across
                landed = firsts[w].at[target, part]
                first_jobs[w, target, part] = start(
                    remote(origin, landed, sends.at[w], arrivals.at[w], 2 * target + part, device)
                )
    sent.wait()
    vec_out[0:6] = vec_out[0:6] + vec_in[0, 0:6]
    vec_out[6:8] = vec_out[6:8] + vec_in[0, 8:10]
    sent = vec_send(1, here.across)

    for target in targets:
        for w in order:
            for part in (0, 1):
                first_jobs[w, target, part].wait_recv()
                if X_FIRST[w]:
                    add(firsts[w].at[target, part], mine[w].at[target, part])
                else:
                    add(firsts[w].at[target, part], (mine, theirs)[part][w].at[target, here.x])
            if X_FIRST[w]:
                origin, device = firsts[w].at[target, far], here.across
            else:
                origin, device = firsts[w].at[target, 1], here.other
            landed = seconds[w].at[target]
            second_jobs[w, target] = start(
                remote(origin, landed, sends.at[w], arrivals.at[w], 8 + target, device)
            )
    sent.wait()
    vec_out[...] = vec_out[...] + vec_in[1]
    ring = [vec_send(1 + ahead, here.ring(ahead)) for ahead in (1, 2, 3)]

    def lane(w, target, up):
        at = target - 1 if up else target
        return (rises if up else falls)[w].at[at], (12 if up else 15) + at

    def receive(w, target, up):
        slot, index = lane(w, target, up)
        device = here.down if up else here.up
        return remote(slot, slot, sends.at[w], arrivals.at[w], index, device)

    def pass_on(w, target, up):
        slot, index = lane(w, target, up)
        device = here.up if up else here.down
        return remote(seconds[w].at[target], slot, sends.at[w], arrivals.at[w], index, device)

    def take_in(w, target, up):
        receive(w, target, up).wait_recv()
        add(seconds[w].at[target], lane(w, target, up)[0])

    for target in targets:
        for w in order:
            second_jobs[w, target].wait_recv()
            kept = firsts[w].at[target, here.x] if X_FIRST[w] else firsts[w].at[target, 0]
            add(seconds[w].at[target], kept)
            for up in (True, False):
                if target == (0 if up else CHAIN - 1):
                    continue
                before = here.z < target if up else here.z > target
                inner = here.has_down if up else here.has_up
                pl.when(jnp.logical_and(before, inner))(
                    lambda w=w, target=target, up=up: take_in(w, target, up)
                )
                start(pass_on(w, target, up), before)

    for copy in ring:
        copy.wait()
    slots = [vec_out[...], vec_in[2], vec_in[3], vec_in[4]]
    total = jnp.zeros_like(slots[0])
    for at in range(CHAIN):
        for behind in range(CHAIN):
            same = lax.rem(here.z + CHAIN - behind, CHAIN) == at
            total = total + jnp.where(same, slots[behind], 0.0)
    vec_out[...] = total
    sent = vec_send(5, here.mate)

    def finish(w, target, up):
        receive(w, target, up).wait_recv()
        sums[w][...] += lane(w, target, up)[0][...].astype(F32)

    for w in order:
        sums[w][...] = seconds[w][here.z].astype(F32)
        for up in (True, False):
            for target in range(CHAIN):
                if target != (0 if up else CHAIN - 1):
                    pl.when(here.z == target)(
                        lambda w=w, target=target, up=up: finish(w, target, up)
                    )

    sent.wait()
    vec_out[0:6] = vec_out[0:6] + vec_in[5, 0:6]
    for copy in edges:
        pl.when(here.mp == 1)(copy.wait_recv)
    for condition, copy in started:
        if condition is None:
            copy.wait_send()
        else:
            pl.when(condition)(copy.wait_send)


def scatter_all(mine, theirs, vectors, out_edge, grad_edge):
    rows = mine[0].shape[0] // (2 * CHAIN)
    mine = [m.reshape(CHAIN, 2, rows, -1) for m in mine]
    theirs = [t.reshape(CHAIN, 2, rows, -1) for t in theirs]
    widths = [m.shape[-1] for m in mine]
    vmem = pl.BlockSpec(memory_space=pltpu.VMEM)
    shapes = [jax.ShapeDtypeStruct((rows, n), F32) for n in widths]
    shapes += [jax.ShapeDtypeStruct(v.shape, v.dtype) for v in (vectors, out_edge, grad_edge)]
    scratch = [pltpu.VMEM((CHAIN, 2, rows, n), BF16) for n in widths]
    scratch += [pltpu.VMEM((CHAIN, rows, n), BF16) for n in widths]
    scratch += [pltpu.VMEM((CHAIN - 1, rows, n), BF16) for n in widths] * 2
    scratch += [
        pltpu.VMEM((6,) + vectors.shape, F32),
        pltpu.SemaphoreType.DMA((4, 18)),
        pltpu.SemaphoreType.DMA((4, 18)),
        pltpu.SemaphoreType.DMA((8,)),
        pltpu.SemaphoreType.DMA((8,)),
    ]
    return pl.pallas_call(
        scatter_kernel,
        out_shape=shapes,
        in_specs=[vmem] * 11,
        out_specs=[vmem] * 7,
        scratch_shapes=scratch,
        compiler_params=pltpu.CompilerParams(
            collective_id=1, has_side_effects=True, vmem_limit_bytes=48 * 2**20
        ),
        name="scatter_all",
    )(*mine, *theirs, vectors, out_edge, grad_edge)


def norm_stats(values):
    mean = jnp.mean(values, axis=-1, keepdims=True)
    center = values - mean
    spread = jnp.mean(center * center, axis=-1, keepdims=True)
    inverse = lax.rsqrt(spread + EPS)
    return center * inverse, inverse


def norm_back(grad, unit, inverse, gain):
    scaled = grad * gain
    return inverse * (
        scaled
        - jnp.mean(scaled, axis=-1, keepdims=True)
        - unit * jnp.mean(scaled * unit, axis=-1, keepdims=True)
    )


def attend(query, keys, values, allowed):
    scores = jnp.einsum("qhd,khd->hqk", query, keys, preferred_element_type=F32)
    scores = jnp.where(allowed[None], scores * HEAD_DIM ** (-0.5), NEG_FILL)
    peak = jnp.max(scores, axis=-1, keepdims=True)
    weights = jnp.exp(scores - peak)
    total = jnp.sum(weights, axis=-1, keepdims=True)
    low = (weights / total).astype(BF16)
    out = jnp.einsum("hqk,khd->qhd", low, values, preferred_element_type=F32)
    return out.astype(BF16), peak + jnp.log(total)


def attend_back(query, keys, values, allowed, log_sum, grad):
    scale = HEAD_DIM ** (-0.5)
    scores = jnp.einsum("qhd,khd->hqk", query, keys, preferred_element_type=F32)
    scores = jnp.where(allowed[None], scores * scale, NEG_FILL)
    probs = jnp.exp(scores - log_sum)
    d_values = jnp.einsum("hqk,qhd->khd", probs.astype(BF16), grad, preferred_element_type=F32)
    d_probs = jnp.einsum("qhd,khd->hqk", grad, values, preferred_element_type=F32)
    mean = jnp.sum(probs * d_probs, axis=-1, keepdims=True)
    low = (probs * (d_probs - mean)).astype(BF16)
    d_query = jnp.einsum("hqk,khd->qhd", low, keys, preferred_element_type=F32) * scale
    d_keys = jnp.einsum("hqk,qhd->khd", low, query, preferred_element_type=F32) * scale
    return d_query.astype(BF16), d_keys.astype(BF16), d_values.astype(BF16)


def update_one(rate, weight, grad, moment, average):
    moment_next = MOMENTUM * moment + grad
    weight_next = weight - rate * (grad + MOMENTUM * moment_next)
    return (weight_next, moment_next, DECAY * average + (1.0 - DECAY) * weight_next)


def on_device(
    tokens,
    lengths,
    cotangent,
    qkv_weight,
    out_weight,
    up_weight,
    down_weight,
    head_bias,
    up_bias,
    norm_vectors,
    qkv_moment,
    out_moment,
    up_moment,
    down_moment,
    head_bias_moment,
    up_bias_moment,
    norm_moment,
    qkv_average,
    out_average,
    up_average,
    down_average,
    head_bias_average,
    up_bias_average,
    norm_average,
):
    grid = Grid(lax.axis_size("dp"))
    member = lax.axis_index("mp")
    mate = member + 1 - 2 * lax.rem(member, 2)
    rows_local, width = tokens.shape
    head_width = qkv_weight.shape[2]
    stages = len(grid.dims)

    qkv_shard = jnp.transpose(qkv_weight, (1, 0, 2)).reshape(-1, 3 * head_width).astype(BF16)
    shards = (
        qkv_shard,
        out_weight.astype(BF16).T,
        up_weight.astype(BF16),
        down_weight.astype(BF16).T,
    )
    units = up_weight.shape[1]
    kernels = grid.size == 2 * CHAIN and units == width
    if kernels:
        flat = jnp.pad(head_bias.reshape(-1), (0, width - 2 * head_width))
        vectors = jnp.zeros((8, width), F32).at[0].set(up_bias).at[1].set(flat)
        *fulls, rows_both, own_cotangent, far_vectors = gather_all(
            shards, tokens, cotangent, vectors
        )
        pairs = [[full[at].reshape(width, -1) for at in (0, 1)] for full in fulls]
        qkv_pair, out_pair, up_pair, down_pair = pairs
        far_bias = far_vectors[1, : 2 * head_width].reshape(2, head_width)
        bias_pair, up_bias_pair = (head_bias, far_bias), (up_bias, far_vectors[0])
        tokens_all = rows_both.reshape(2 * rows_local, width)
        own_tokens = rows_both[0]
    else:
        qkv_pair = gather_half(grid, shards[0], stages)
        out_pair = gather_half(grid, shards[1], stages - 1)
        up_pair = gather_half(grid, shards[2], stages)
        down_pair = gather_half(grid, shards[3], stages - 1)
        bias_pair = (head_bias, half_swap(head_bias))
        up_bias_pair = (up_bias, half_swap(up_bias))
        own_tokens = bring(tokens, member)
        own_cotangent = bring(cotangent, member)
        tokens_all = jnp.concatenate([own_tokens, core_swap(own_tokens)], 0)

    slot_own, valid_own = row_table(rows_local, member, lengths)
    slot_mate, valid_mate = row_table(rows_local, mate, lengths)
    slot = jnp.concatenate([slot_own, slot_mate])
    frame = jnp.concatenate([valid_own, valid_mate])
    allowed = (slot[:, None] == slot[None, :]) & frame[None, :]
    live = valid_own[:, None]

    def share(rows):
        return jnp.concatenate([rows, core_swap(rows)], 0)

    def settle(partial):
        return partial[:rows_local] + core_swap(partial[rows_local:].astype(BF16)).astype(F32)

    heads = 2 * head_width // HEAD_DIM
    parts = []
    for weight, bias in zip(qkv_pair, bias_pair):
        rows_bias = jnp.concatenate([bias[0], jnp.zeros_like(bias[0]), bias[1]])
        act = (dot(tokens_all, weight, ((1,), (0,))) + rows_bias).astype(BF16)
        parts.append(act.reshape(2 * rows_local, 3, -1, HEAD_DIM))
    act = jnp.concatenate(parts, 2)
    query, keys, values = act[:, 0], act[:, 1], act[:, 2]
    attn, log_sum = attend(query, keys, values, allowed)
    attn = attn.reshape(2 * rows_local, -1)
    out_both = jnp.concatenate(out_pair, 1)
    branch = settle(dot(attn, out_both, ((1,), (1,))))
    unit_one, inverse_one = norm_stats(branch + norm_vectors[0] + own_tokens.astype(F32))
    first = unit_one * norm_vectors[2] + norm_vectors[3]
    first_all = share(first.astype(BF16))

    hiddens, slopes = [], []
    for weight, bias in zip(up_pair, up_bias_pair):
        pre = dot(first_all, weight, ((1,), (0,))) + bias
        phi = 0.5 * (1.0 + lax.erf(pre * (0.5**0.5)))
        density = jnp.exp(-0.5 * pre * pre) * (1.0 / math.sqrt(2.0 * math.pi))
        hiddens.append((pre * phi).astype(BF16))
        slopes.append((phi + pre * density).astype(BF16))
    ffn = settle(
        dot(hiddens[0], down_pair[0], ((1,), (1,))) + dot(hiddens[1], down_pair[1], ((1,), (1,)))
    )
    unit_two, inverse_two = norm_stats(ffn + norm_vectors[1] + first)
    second = unit_two * norm_vectors[4] + norm_vectors[5]
    layer_out = jnp.where(live, second, 0.0).astype(BF16)

    grad_two = jnp.where(live, own_cotangent.astype(F32), 0.0)
    d_second = norm_back(grad_two, unit_two, inverse_two, norm_vectors[4])
    d_ffn_all = share(d_second.astype(BF16))
    d_pres = [
        (dot(d_ffn_all, weight, ((1,), (0,))) * slope.astype(F32)).astype(BF16)
        for weight, slope in zip(down_pair, slopes)
    ]
    d_first = d_second + settle(
        dot(d_pres[0], up_pair[0], ((1,), (1,))) + dot(d_pres[1], up_pair[1], ((1,), (1,)))
    )
    grad_down = [dot(d_ffn_all, hidden, ((0,), (0,))).astype(BF16) for hidden in hiddens]
    grad_up = [dot(first_all, d_pre, ((0,), (0,))).astype(BF16) for d_pre in d_pres]
    grad_up_bias = [jnp.sum(d_pre, axis=0, dtype=F32) for d_pre in d_pres]

    d_branch = norm_back(d_first, unit_one, inverse_one, norm_vectors[2])
    d_branch_all = share(d_branch.astype(BF16))
    d_attn = dot(d_branch_all, out_both, ((1,), (0,))).astype(BF16)
    grad_out = [
        dot(d_branch_all, attn[:, at : at + head_width], ((0,), (0,))).astype(BF16)
        for at in (0, head_width)
    ]
    d_query, d_keys, d_values = attend_back(
        query, keys, values, allowed, log_sum, d_attn.reshape(2 * rows_local, heads, HEAD_DIM)
    )
    half_heads = heads // 2
    d_parts = []
    for at in (0, half_heads):
        d_parts.append(
            jnp.concatenate(
                [
                    piece[:, at : at + half_heads].reshape(2 * rows_local, -1)
                    for piece in (d_query, d_keys, d_values)
                ],
                1,
            )
        )
    grad_qkv = [dot(tokens_all, part, ((0,), (0,))).astype(BF16) for part in d_parts]
    grad_bias = [jnp.sum(part, axis=0, dtype=F32) for part in d_parts]
    d_tokens = settle(
        dot(d_parts[0], qkv_pair[0], ((1,), (1,))) + dot(d_parts[1], qkv_pair[1], ((1,), (1,)))
    )
    tokens_grad = d_tokens + d_branch

    norm_part = jnp.stack(
        [
            jnp.sum(d_branch, axis=0),
            jnp.sum(d_second, axis=0),
            jnp.sum(d_first * unit_one, axis=0),
            jnp.sum(d_first, axis=0),
            jnp.sum(grad_two * unit_two, axis=0),
            jnp.sum(grad_two, axis=0),
        ]
    )
    if kernels:
        pad = jnp.zeros((width - 3 * head_width,), F32)
        vectors = jnp.concatenate(
            [
                norm_part,
                jnp.stack(
                    [
                        grad_up_bias[0],
                        jnp.concatenate([grad_bias[0], pad]),
                        grad_up_bias[1],
                        jnp.concatenate([grad_bias[1], pad]),
                    ]
                ),
                jnp.zeros((6, width), F32),
            ]
        )
        source, free, count = move_plan(rows_local)
        near = (grad_qkv[0], grad_out[0], grad_up[0], grad_down[0])
        distant = (grad_qkv[1], grad_out[1], grad_up[1], grad_down[1])
        *sums, vectors, out_back, grad_back = scatter_all(
            near,
            distant,
            vectors,
            layer_out[free : free + count],
            tokens_grad[free : free + count],
        )
        sum_qkv, sum_out, sum_up, sum_down = sums
        layer_out = put_back(layer_out, out_back, member)
        tokens_grad = put_back(tokens_grad, grad_back, member)
        sum_norm, sum_up_bias, sum_bias = vectors[:6], vectors[6], vectors[7]
        sum_bias = sum_bias[: 3 * head_width]
    else:
        sum_qkv = scatter_sum(grid, *grad_qkv, True)
        sum_out = scatter_sum(grid, *grad_out, True)
        sum_up = scatter_sum(grid, *grad_up, False)
        sum_down = scatter_sum(grid, *grad_down, True)
        layer_out = send_back(layer_out, member)
        tokens_grad = send_back(tokens_grad, member)
        sum_norm = sum_all(grid, norm_part, True)
        sum_up_bias = sum_half(grid, grad_up_bias)
        sum_bias = sum_half(grid, grad_bias)
    sum_qkv = jnp.transpose(sum_qkv.reshape(-1, 3, head_width), (1, 0, 2))
    sum_out, sum_down = sum_out.T, sum_down.T
    sum_head_bias = jnp.stack([sum_bias[:head_width], sum_bias[2 * head_width :]])

    divisor = math.sqrt(1000.0 * grid.size * UTT)
    params = (qkv_weight, out_weight, up_weight, down_weight, head_bias, up_bias, norm_vectors)
    grads = (sum_qkv, sum_out, sum_up, sum_down, sum_head_bias, sum_up_bias, sum_norm)
    moments = (
        qkv_moment,
        out_moment,
        up_moment,
        down_moment,
        head_bias_moment,
        up_bias_moment,
        norm_moment,
    )
    averages = (
        qkv_average,
        out_average,
        up_average,
        down_average,
        head_bias_average,
        up_bias_average,
        norm_average,
    )
    nexts, moment_nexts, average_nexts = ([], [], [])
    for weight, grad, moment, average, scale_one in zip(
        params, grads, moments, averages, RATE_SCALES
    ):
        weight_next, moment_next, average_next = update_one(
            scale_one / divisor, weight, grad, moment, average
        )
        nexts.append(weight_next)
        moment_nexts.append(moment_next)
        average_nexts.append(average_next)
    return (layer_out, tokens_grad, *grads, *nexts, *moment_nexts, *average_nexts)


ROWS = P(("dp", "mp"), None)
PARAMS = (
    P(None, "dp", "mp"),
    P("mp", "dp"),
    P("dp", "mp"),
    P("mp", "dp"),
    P(None, "mp"),
    P("mp"),
    P(),
)


def solution(mesh):
    return jax.shard_map(
        on_device,
        mesh=mesh,
        in_specs=(ROWS, P("dp", None), ROWS) + PARAMS * 3,
        out_specs=(ROWS, ROWS) + PARAMS * 4,
        check_vma=False,
    )
```

```python
import math

import jax
import jax.numpy as jnp
from jax import lax
from jax.experimental import pallas as pl
from jax.experimental.pallas import tpu as pltpu
from jax.sharding import PartitionSpec as P

HEAD_DIM = 64
UTT = 1
LENS = (256, 512, 896)
MOSTS = (200, 400, 781)

EPS = 1e-05
MOMENTUM = 0.5
DECAY = 0.5
RATE_SCALES = (0.02, 0.16, 0.02, 0.02, 0.02, 0.32, 0.16)
NEG_FILL = -1000000000.0
BF16 = jnp.bfloat16
F32 = jnp.float32


def dot(a, b, dims):
    return lax.dot_general(a, b, (dims, ((), ())), preferred_element_type=F32)


CORE_SWAP = [(0, 1), (1, 0), (2, 3), (3, 2)]
HALF_SWAP = [(0, 2), (2, 0), (1, 3), (3, 1)]


def core_swap(value):
    return lax.ppermute(value, "mp", CORE_SWAP)


def half_swap(value):
    return lax.ppermute(value, "mp", HALF_SWAP)


def dp_dims(size):
    dims = []
    while size % 4 == 0:
        dims.append(4)
        size //= 4
    if size > 1:
        dims.append(size)
    return tuple(dims)


class Grid:
    def __init__(self, size):
        self.dims = dp_dims(size)
        self.size = size
        rank = lax.axis_index("dp")
        self.strides = []
        stride = size
        for extent in self.dims:
            stride //= extent
            self.strides.append(stride)
        self.coords = [lax.rem(rank // s, e) for s, e in zip(self.strides, self.dims)]

    def send(self, value, stage, ahead):
        extent, stride = self.dims[stage], self.strides[stage]
        pairs = []
        for source in range(self.size):
            at = source // stride % extent
            pairs.append((source, source + ((at + ahead) % extent - at) * stride))
        return lax.ppermute(value, "dp", pairs)


def put(buffer, piece, axis, index):
    starts = [0] * buffer.ndim
    starts[axis] = index
    return lax.dynamic_update_slice(buffer, jnp.expand_dims(piece, axis), tuple(starts))


def take(buffer, axis, index):
    return lax.dynamic_index_in_dim(buffer, index, axis, keepdims=False)


def gather_half(grid, shard, half_stage):
    rows, columns = shard.shape
    value = shard[None]
    done = 0
    order = list(range(len(grid.dims)))
    for stage in order:
        if done == half_stage:
            value = jnp.concatenate([value, half_swap(value)], 0)
        extent, coord = grid.dims[stage], grid.coords[stage]
        axis = 1 + done
        shape = value.shape[:axis] + (extent,) + value.shape[axis:]
        buffer = put(jnp.zeros(shape, value.dtype), value, axis, coord)
        for ahead in range(1, extent):
            source = lax.rem(coord + extent - ahead, extent)
            buffer = put(buffer, grid.send(value, stage, ahead), axis, source)
        value = buffer
        done += 1
    if done == half_stage:
        other = half_swap(value)
        return value.reshape(-1, columns), other.reshape(-1, columns)
    return value[0].reshape(-1, columns), value[1].reshape(-1, columns)


def scatter_sum(grid, mine, theirs, half_first):
    columns = mine.shape[1]
    shape = grid.dims + (mine.shape[0] // grid.size, columns)
    order = list(range(len(grid.dims)))[::-1]

    def along(value, stage):
        extent, coord = grid.dims[stage], grid.coords[stage]
        axis = value.ndim - 3
        total = take(value, axis, coord).astype(F32)
        for ahead in range(1, extent):
            piece = take(value, axis, lax.rem(coord + ahead, extent))
            total = total + grid.send(piece.astype(BF16), stage, ahead).astype(F32)
        return total

    mine, theirs = mine.reshape(shape), theirs.reshape(shape)
    if half_first:
        value = mine.astype(F32) + half_swap(theirs.astype(BF16)).astype(F32)
        for stage in order:
            value = along(value, stage)
        return value
    first = order[0]
    mine = along(mine, first)
    theirs = along(theirs, first)
    value = mine + half_swap(theirs.astype(BF16)).astype(F32)
    for stage in order[1:]:
        value = along(value, stage)
    return value


def sum_half(grid, pair):
    value = pair[0] + half_swap(pair[1])
    for stage in range(len(grid.dims)):
        total = value
        for ahead in range(1, grid.dims[stage]):
            total = total + grid.send(value, stage, ahead)
        value = total
    return value


def sum_all(grid, value, over_cores):
    for stage in range(len(grid.dims)):
        total = value
        for ahead in range(1, grid.dims[stage]):
            total = total + grid.send(value, stage, ahead)
        value = total
    value = value + half_swap(value)
    if over_cores:
        value = value + core_swap(value)
    return value


def offsets():
    listing, offset = [], 0
    for extent in LENS:
        listing.append(offset)
        offset += UTT * extent
    return listing


def move_plan(rows_local):
    start = offsets()[2]
    count = 2 * rows_local - start
    free = -(-(start + MOSTS[2] - 3 * rows_local) // 16) * 16
    return rows_local - count, free, count


def row_table(rows_local, member, lengths):
    source, free, count = move_plan(rows_local)
    starts = offsets()
    local = jnp.arange(rows_local)
    row = member * rows_local + local
    slot = (row >= starts[1]).astype(jnp.int32) + (row >= starts[2]).astype(jnp.int32)
    place = row - jnp.where(slot == 0, starts[0], jnp.where(slot == 1, starts[1], starts[2]))
    arrived = (member == 3) & (local >= free) & (local < free + count)
    left = (member == 1) & (local >= source)
    place = jnp.where(arrived, local - free, place)
    length = jnp.where(slot == 0, lengths[0, 0], jnp.where(slot == 1, lengths[0, 1], lengths[0, 2]))
    return slot, (place < length) & ~left


def bring(rows, member):
    source, free, count = move_plan(rows.shape[0])
    moved = lax.ppermute(rows[source:], "mp", [(1, 3)])
    placed = lax.dynamic_update_slice(rows, moved, (free, 0))
    return jnp.where(member == 3, placed, rows)


def put_back(rows, moved, member):
    source, free, count = move_plan(rows.shape[0])
    placed = lax.dynamic_update_slice(rows, moved, (source, 0))
    cleared = lax.dynamic_update_slice(rows, jnp.zeros_like(moved), (free, 0))
    return jnp.where(member == 1, placed, jnp.where(member == 3, cleared, rows))


def send_back(rows, member):
    source, free, count = move_plan(rows.shape[0])
    return put_back(rows, lax.ppermute(rows[free : free + count], "mp", [(3, 1)]), member)


CHAIN = 4
X_FIRST = (False, True, True, False)
WHERE = [(0, 0)] + [(step, sign) for step in range(1, CHAIN) for sign in (1, -1)]


class Place:
    def __init__(self):
        self.dp = lax.axis_index("dp")
        self.mp = lax.axis_index("mp")
        self.z = self.dp // 2
        self.x = lax.rem(self.dp, 2)
        self.up = (self.dp + 2, self.mp)
        self.down = (self.dp - 2, self.mp)
        self.across = (self.dp + 1 - 2 * self.x, self.mp)
        self.other = (self.dp, lax.rem(self.mp + 2, 4))
        self.mate = (self.dp, self.mp + 1 - 2 * lax.rem(self.mp, 2))
        self.has_up = self.z < CHAIN - 1
        self.has_down = self.z > 0

    def ring(self, ahead):
        return (lax.rem(self.dp + 2 * ahead, 2 * CHAIN), self.mp)

    def greet(self, peers):
        barrier = pltpu.get_barrier_semaphore()
        for peer in peers:
            pl.semaphore_signal(
                barrier, inc=1, device_id=peer, device_id_type=pl.DeviceIdType.MESH
            )
        pl.semaphore_wait(barrier, len(peers))


def remote(source, target, sends, arrivals, index, device):
    return pltpu.make_async_remote_copy(
        source,
        target,
        sends.at[index],
        arrivals.at[index],
        device_id=device,
        device_id_type=pl.DeviceIdType.MESH,
    )


def gather_kernel(row_plan, *refs):
    shards, (rows_ref, cot_ref, vec_ref) = refs[0:4], refs[4:7]
    fulls, (rows_out, cot_out, vec_out) = refs[7:11], refs[11:14]
    sends, arrivals, side_send, side_arrive, local = refs[14:19]
    here = Place()
    source, free, count = row_plan
    n_rows = rows_ref.shape[0]
    here.greet([here.ring(1), here.ring(2), here.ring(3), here.across, here.other, here.mate,
                (here.dp, 3 - here.mp)])

    def z_of(where):
        step, sign = where
        return here.z - step * sign

    def held(where):
        step, sign = where
        if step == 0:
            return None
        return here.z >= step if sign > 0 else here.z + step < CHAIN

    def maybe(condition, action):
        if condition is None:
            action()
        else:
            pl.when(condition)(action)

    def block(w, where, far, half):
        x = 1 - here.x if far else here.x
        return fulls[w].at[half, z_of(where) * 2 + x]

    def chain(w, where):
        step, sign = where
        origin = shards[w] if step == 0 else block(w, where, False, 0)
        jobs = []
        for way in (1, -1) if step == 0 else (sign,):
            index = step + (0 if way > 0 else 3)
            device = here.up if way > 0 else here.down
            go = here.has_up if way > 0 else here.has_down
            if step < CHAIN - 1:
                jobs.append((go, remote(origin, block_to(w, where), sends.at[w], arrivals.at[w], index, device)))
        return jobs

    def block_to(w, where):
        return fulls[w].at[0, z_of(where) * 2 + here.x]

    def second(w, where):
        origin = shards[w] if where[0] == 0 else block(w, where, False, 0)
        index = 6 + WHERE.index(where)
        if X_FIRST[w]:
            return remote(origin, block(w, where, False, 0), sends.at[w], arrivals.at[w], index, here.across)
        return remote(origin, block(w, where, False, 1), sends.at[w], arrivals.at[w], index, here.other)

    def third(w, where, arrived):
        index = 13 + WHERE.index(where) + (len(WHERE) if arrived else 0)
        if X_FIRST[w]:
            origin = shards[w] if where[0] == 0 and not arrived else block(w, where, arrived, 0)
            return remote(origin, block(w, where, arrived, 1), sends.at[w], arrivals.at[w], index, here.other)
        origin = shards[w] if where[0] == 0 and not arrived else block(w, where, False, int(arrived))
        return remote(origin, block(w, where, False, int(arrived)), sends.at[w], arrivals.at[w], index, here.across)

    def landing(w, where, stage, arrived=False):
        if stage == 2:
            index = 6 + WHERE.index(where)
            target = block(w, where, True, 0) if X_FIRST[w] else block(w, where, False, 1)
            device = here.across if X_FIRST[w] else here.other
        else:
            index = 13 + WHERE.index(where) + (len(WHERE) if arrived else 0)
            if X_FIRST[w]:
                target, device = block(w, where, arrived, 1), here.other
            else:
                target, device = block(w, where, True, int(arrived)), here.across
        return remote(target, target, sends.at[w], arrivals.at[w], index, device)

    def chain_landing(w, where):
        step, sign = where
        index = step - 1 + (0 if sign > 0 else 3)
        target = block(w, where, False, 0)
        return remote(target, target, sends.at[w], arrivals.at[w], index, here.down if sign > 0 else here.up)

    order = (0, 1, 3, 2)
    by_step = [[p for p in WHERE if p[0] == step] for step in range(CHAIN)]

    low, high = pl.ds(0, free), pl.ds(free + count, n_rows - free - count)
    middle, tail = pl.ds(free, count), pl.ds(source, count)
    locals_ = [(None, pltpu.make_async_copy(shards[w], fulls[w].at[0, here.dp], local.at[w])) for w in order]
    not_last, second_core = here.mp != 3, here.mp == 1
    for n, (given, taken) in enumerate(((rows_ref, rows_out.at[0]), (cot_ref, cot_out))):
        for m, part in enumerate((low, high, middle)):
            copy = pltpu.make_async_copy(given.at[part], taken.at[part], local.at[4 + 3 * n + m])
            locals_.append((not_last if m == 2 else None, copy))
    for condition, copy in locals_:
        maybe(condition, copy.start)

    def to_mate(m, part):
        return remote(rows_ref.at[part], rows_out.at[1, part], side_send, side_arrive, m, here.mate)

    side = [(None, to_mate(0, low)), (None, to_mate(1, high)), (not_last, to_mate(2, middle))]
    side.append((None, remote(vec_ref, vec_out, side_send, side_arrive, 3, here.other)))
    moved = [
        remote(rows_ref.at[tail], rows_out.at[0, middle], side_send, side_arrive, 4, here.other),
        remote(cot_ref.at[tail], cot_out.at[middle], side_send, side_arrive, 5, here.other),
        remote(rows_ref.at[tail], rows_out.at[1, middle], side_send, side_arrive, 6, (here.dp, 3 - here.mp)),
    ]
    side += [(second_core, copy) for copy in moved]

    started = []

    def start(condition, copy):
        maybe(condition, copy.start)
        started.append((condition, copy))

    for condition, copy in side:
        start(condition, copy)
    for step in range(CHAIN):
        for where in by_step[step]:
            for w in order:
                if step > 0:
                    maybe(held(where), chain_landing(w, where).wait_recv)
                for go, copy in chain(w, where):
                    both = go if held(where) is None else jnp.logical_and(go, held(where))
                    start(both, copy)
                start(held(where), second(w, where))
                start(held(where), third(w, where, False))
        for where in by_step[step - 1] if step > 0 else ():
            for w in order:
                maybe(held(where), landing(w, where, 2).wait_recv)
                start(held(where), third(w, where, True))
    for where in by_step[CHAIN - 1]:
        for w in order:
            maybe(held(where), landing(w, where, 2).wait_recv)
            start(held(where), third(w, where, True))
    for where in WHERE:
        for w in order:
            for arrived in (False, True):
                maybe(held(where), landing(w, where, 3, arrived).wait_recv)
    to_mate(0, low).wait_recv()
    to_mate(1, high).wait_recv()
    pl.when(here.mp != 2)(to_mate(2, middle).wait_recv)
    side[3][1].wait_recv()
    pl.when(here.mp == 3)(moved[0].wait_recv)
    pl.when(here.mp == 3)(moved[1].wait_recv)
    pl.when(here.mp == 2)(moved[2].wait_recv)
    for condition, copy in started:
        maybe(condition, copy.wait_send)
    for condition, copy in locals_:
        maybe(condition, copy.wait)


def gather_all(shards, rows, cotangent, vectors):
    rows_local, width = rows.shape
    vmem, anywhere = pl.BlockSpec(memory_space=pltpu.VMEM), pl.BlockSpec(memory_space=pl.ANY)
    shapes = [jax.ShapeDtypeStruct((2, 2 * CHAIN) + s.shape, s.dtype) for s in shards]
    shapes += [
        jax.ShapeDtypeStruct((2, rows_local, width), rows.dtype),
        jax.ShapeDtypeStruct((rows_local, width), rows.dtype),
        jax.ShapeDtypeStruct(vectors.shape, vectors.dtype),
    ]
    plan = move_plan(rows_local)
    return pl.pallas_call(
        lambda *refs: gather_kernel(plan, *refs),
        out_shape=shapes,
        in_specs=[vmem] * 7,
        out_specs=[anywhere] * 6 + [vmem],
        scratch_shapes=[
            pltpu.SemaphoreType.DMA((4, 27)),
            pltpu.SemaphoreType.DMA((4, 27)),
            pltpu.SemaphoreType.DMA((7,)),
            pltpu.SemaphoreType.DMA((7,)),
            pltpu.SemaphoreType.DMA((10,)),
        ],
        compiler_params=pltpu.CompilerParams(
            collective_id=0, has_side_effects=True, vmem_limit_bytes=16 * 2**20
        ),
        name="gather_all",
    )(*shards, rows, cotangent, vectors)


def scatter_kernel(*refs):
    mine, theirs = refs[0:4], refs[4:8]
    vec_ref, out_edge, grad_edge = refs[8:11]
    sums, (vec_out, out_back, grad_back) = refs[11:15], refs[15:18]
    firsts, seconds, rises, falls = refs[18:22], refs[22:26], refs[26:30], refs[30:34]
    vec_in, sends, arrivals, side_send, side_arrive = refs[34:39]
    here = Place()
    here.greet([here.ring(1), here.ring(2), here.ring(3), here.across, here.other, here.mate])
    order = (2, 3, 1, 0)
    targets = (3, 0, 2, 1)
    far = 1 - here.x
    started = []

    def start(copy, condition=None):
        if condition is None:
            copy.start()
        else:
            pl.when(condition)(copy.start)
        started.append((condition, copy))
        return copy

    def add(target, more):
        target[...] = (target[...].astype(F32) + more[...].astype(F32)).astype(BF16)

    edges = []
    for index, (given, taken) in enumerate(((out_edge, out_back), (grad_edge, grad_back))):
        copy = remote(given, taken, side_send, side_arrive, 6 + index, here.other)
        edges.append(start(copy, here.mp == 3))

    def vec_send(index, device):
        copy = remote(vec_out, vec_in.at[index], side_send, side_arrive, index, device)
        copy.start()
        return copy

    vec_out[...] = vec_ref[...]
    sent = vec_send(0, here.other)

    first_jobs, second_jobs = {}, {}
    for target in targets:
        for w in order:
            for part in (0, 1):
                if X_FIRST[w]:
                    origin, device = theirs[w].at[target, part], here.other
                else:
                    origin, device = (mine, theirs)[part][w].at[target, far], here.across
                landed = firsts[w].at[target, part]
                first_jobs[w, target, part] = start(
                    remote(origin, landed, sends.at[w], arrivals.at[w], 2 * target + part, device)
                )
    sent.wait()
    vec_out[0:6] = vec_out[0:6] + vec_in[0, 0:6]
    vec_out[6:8] = vec_out[6:8] + vec_in[0, 8:10]
    sent = vec_send(1, here.across)

    for target in targets:
        for w in order:
            for part in (0, 1):
                first_jobs[w, target, part].wait_recv()
                if X_FIRST[w]:
                    add(firsts[w].at[target, part], mine[w].at[target, part])
                else:
                    add(firsts[w].at[target, part], (mine, theirs)[part][w].at[target, here.x])
            if X_FIRST[w]:
                origin, device = firsts[w].at[target, far], here.across
            else:
                origin, device = firsts[w].at[target, 1], here.other
            landed = seconds[w].at[target]
            second_jobs[w, target] = start(
                remote(origin, landed, sends.at[w], arrivals.at[w], 8 + target, device)
            )
    sent.wait()
    vec_out[...] = vec_out[...] + vec_in[1]
    ring = [vec_send(1 + ahead, here.ring(ahead)) for ahead in (1, 2, 3)]

    def lane(w, target, up):
        at = target - 1 if up else target
        return (rises if up else falls)[w].at[at], (12 if up else 15) + at

    def receive(w, target, up):
        slot, index = lane(w, target, up)
        device = here.down if up else here.up
        return remote(slot, slot, sends.at[w], arrivals.at[w], index, device)

    def pass_on(w, target, up):
        slot, index = lane(w, target, up)
        device = here.up if up else here.down
        return remote(seconds[w].at[target], slot, sends.at[w], arrivals.at[w], index, device)

    def take_in(w, target, up):
        receive(w, target, up).wait_recv()
        add(seconds[w].at[target], lane(w, target, up)[0])

    for target in targets:
        for w in order:
            second_jobs[w, target].wait_recv()
            kept = firsts[w].at[target, here.x] if X_FIRST[w] else firsts[w].at[target, 0]
            add(seconds[w].at[target], kept)
            for up in (True, False):
                if target == (0 if up else CHAIN - 1):
                    continue
                before = here.z < target if up else here.z > target
                inner = here.has_down if up else here.has_up
                pl.when(jnp.logical_and(before, inner))(
                    lambda w=w, target=target, up=up: take_in(w, target, up)
                )
                start(pass_on(w, target, up), before)

    for copy in ring:
        copy.wait()
    slots = [vec_out[...], vec_in[2], vec_in[3], vec_in[4]]
    total = jnp.zeros_like(slots[0])
    for at in range(CHAIN):
        for behind in range(CHAIN):
            same = lax.rem(here.z + CHAIN - behind, CHAIN) == at
            total = total + jnp.where(same, slots[behind], 0.0)
    vec_out[...] = total
    sent = vec_send(5, here.mate)

    def finish(w, target, up):
        receive(w, target, up).wait_recv()
        sums[w][...] += lane(w, target, up)[0][...].astype(F32)

    for w in order:
        sums[w][...] = seconds[w][here.z].astype(F32)
        for up in (True, False):
            for target in range(CHAIN):
                if target != (0 if up else CHAIN - 1):
                    pl.when(here.z == target)(
                        lambda w=w, target=target, up=up: finish(w, target, up)
                    )

    sent.wait()
    vec_out[0:6] = vec_out[0:6] + vec_in[5, 0:6]
    for copy in edges:
        pl.when(here.mp == 1)(copy.wait_recv)
    for condition, copy in started:
        if condition is None:
            copy.wait_send()
        else:
            pl.when(condition)(copy.wait_send)


def scatter_all(mine, theirs, vectors, out_edge, grad_edge):
    rows = mine[0].shape[0] // (2 * CHAIN)
    mine = [m.reshape(CHAIN, 2, rows, -1) for m in mine]
    theirs = [t.reshape(CHAIN, 2, rows, -1) for t in theirs]
    widths = [m.shape[-1] for m in mine]
    vmem = pl.BlockSpec(memory_space=pltpu.VMEM)
    shapes = [jax.ShapeDtypeStruct((rows, n), F32) for n in widths]
    shapes += [jax.ShapeDtypeStruct(v.shape, v.dtype) for v in (vectors, out_edge, grad_edge)]
    scratch = [pltpu.VMEM((CHAIN, 2, rows, n), BF16) for n in widths]
    scratch += [pltpu.VMEM((CHAIN, rows, n), BF16) for n in widths]
    scratch += [pltpu.VMEM((CHAIN - 1, rows, n), BF16) for n in widths] * 2
    scratch += [
        pltpu.VMEM((6,) + vectors.shape, F32),
        pltpu.SemaphoreType.DMA((4, 18)),
        pltpu.SemaphoreType.DMA((4, 18)),
        pltpu.SemaphoreType.DMA((8,)),
        pltpu.SemaphoreType.DMA((8,)),
    ]
    return pl.pallas_call(
        scatter_kernel,
        out_shape=shapes,
        in_specs=[vmem] * 11,
        out_specs=[vmem] * 7,
        scratch_shapes=scratch,
        compiler_params=pltpu.CompilerParams(
            collective_id=1, has_side_effects=True, vmem_limit_bytes=48 * 2**20
        ),
        name="scatter_all",
    )(*mine, *theirs, vectors, out_edge, grad_edge)

def split_parts(value, count):
    parts = []
    for _ in range(count):
        part = value.astype(BF16).astype(F32)
        parts.append(part)
        value = value - part
    return parts


def lane_fill(base, parts, first):
    lane = lax.broadcasted_iota(jnp.int32, base.shape, 1)
    for index, part in enumerate(parts):
        base = jnp.where(lane == first + index, part, base)
    return base


def head_columns(head, part, per_half):
    half, index = divmod(head, per_half)
    at = (part * per_half + index) * HEAD_DIM
    return half, slice(at, at + HEAD_DIM)


def attend_kernel(block, near_ref, far_ref, slot_ref, mask_ref, attn_ref, q_ref, k_ref, v_ref, out_ref):
    acts = (near_ref, far_ref)
    heads, rows = q_ref.shape[:2]
    ones = lane_fill(jnp.zeros((rows, HEAD_DIM), F32), (1.0, 1.0), 0).astype(BF16)
    for head in range(heads):
        for part, (ref, more) in enumerate(((q_ref, slot_ref), (k_ref, mask_ref), (v_ref, None))):
            half, columns = head_columns(head, part, heads // 2)
            piece = acts[half][:, columns]
            if part == 0:
                piece = (piece.astype(F32) * HEAD_DIM ** (-0.5)).astype(BF16)
            ref[head, :, 0:HEAD_DIM] = piece
            ref[head, :, HEAD_DIM : 2 * HEAD_DIM] = ones if more is None else more[...]

    def step(index, carry):
        head, at = index // (rows // block), lax.rem(index, rows // block)
        span = pl.ds(pl.multiple_of(at * block, 16), block)
        query = q_ref[head, span, :]
        scores = dot(query, k_ref[head], ((1,), (1,)))
        peak = jnp.max(scores, axis=-1, keepdims=True)
        weights = jnp.exp(scores - peak)
        both = dot(weights.astype(BF16), v_ref[head], ((1,), (0,)))
        total = both[:, HEAD_DIM : HEAD_DIM + 1]
        out_ref[head, span, :] = (both * (1.0 / total)).astype(BF16)
        log_sum = peak + jnp.log(total)
        parts = [-p for p in split_parts(log_sum, 3)]
        q_ref[head, span, :] = lane_fill(query.astype(F32), parts, HEAD_DIM + 3).astype(BF16)
        return carry

    lax.fori_loop(0, heads * (rows // block), step, 0, unroll=6)
    for head in range(heads):
        attn_ref[:, head * HEAD_DIM : (head + 1) * HEAD_DIM] = out_ref[head, :, 0:HEAD_DIM]


def attend_back_kernel(block, attn_ref, grad_ref, q_ref, k_ref, v_ref, near_ref, far_ref, g_ref, dq_ref, dk_ref, dv_ref):
    heads, rows = q_ref.shape[:2]
    for head in range(heads):
        columns = slice(head * HEAD_DIM, (head + 1) * HEAD_DIM)
        grad = grad_ref[:, columns]
        mean = jnp.sum(grad.astype(F32) * attn_ref[:, columns].astype(F32), axis=-1, keepdims=True)
        parts = [-p for p in split_parts(mean, 2)]
        g_ref[head, :, 0:HEAD_DIM] = grad
        g_ref[head, :, HEAD_DIM : 2 * HEAD_DIM] = lane_fill(
            jnp.zeros((rows, HEAD_DIM), F32), parts, 0
        ).astype(BF16)
    dk_ref[...] = jnp.zeros_like(dk_ref)
    dv_ref[...] = jnp.zeros_like(dv_ref)

    def step(index, carry):
        head, at = index // (rows // block), lax.rem(index, rows // block)
        span = pl.ds(pl.multiple_of(at * block, 16), block)
        query, grad = q_ref[head, span, :], g_ref[head, span, :]
        keys = k_ref[head]
        probs = jnp.exp(dot(keys, query, ((1,), (1,))))
        change = (probs * dot(v_ref[head], grad, ((1,), (1,)))).astype(BF16)
        dv_ref[head] += dot(probs.astype(BF16), grad, ((1,), (0,)))
        dk_ref[head] += dot(change, query, ((1,), (0,)))
        dq_ref[head, span, :] = (dot(change, keys, ((0,), (0,))) * HEAD_DIM ** (-0.5)).astype(BF16)
        return carry

    lax.fori_loop(0, heads * (rows // block), step, 0, unroll=6)
    outs = (near_ref, far_ref)
    for head in range(heads):
        for part, ref in enumerate((dq_ref, dk_ref, dv_ref)):
            half, columns = head_columns(head, part, heads // 2)
            outs[half][:, columns] = ref[head, :, 0:HEAD_DIM].astype(BF16)


def attend_cost(heads, rows, products):
    return pl.CostEstimate(
        flops=2 * products * heads * rows * rows * 128,
        bytes_accessed=8 * heads * rows * 128,
        transcendentals=heads * rows * rows,
    )


def attend(near, far, slots, masks, block):
    rows = near.shape[0]
    heads = 2 * near.shape[1] // (3 * HEAD_DIM)
    vmem = pl.BlockSpec(memory_space=pltpu.VMEM)
    wide = jax.ShapeDtypeStruct((heads, rows, 2 * HEAD_DIM), BF16)
    return pl.pallas_call(
        lambda *refs: attend_kernel(block, *refs),
        out_shape=[jax.ShapeDtypeStruct((rows, heads * HEAD_DIM), BF16), wide, wide, wide],
        in_specs=[vmem] * 4,
        out_specs=[vmem] * 4,
        scratch_shapes=[pltpu.VMEM(wide.shape, BF16)],
        compiler_params=pltpu.CompilerParams(vmem_limit_bytes=40 * 2**20),
        cost_estimate=attend_cost(heads, rows, 2),
        name="attend",
    )(near, far, slots, masks)


def attend_back(attn, grad, query, keys, values, block):
    heads, rows = query.shape[:2]
    vmem = pl.BlockSpec(memory_space=pltpu.VMEM)
    out = jax.ShapeDtypeStruct((rows, 3 * heads // 2 * HEAD_DIM), BF16)
    return pl.pallas_call(
        lambda *refs: attend_back_kernel(block, *refs),
        out_shape=[out, out],
        in_specs=[vmem] * 5,
        out_specs=[vmem] * 2,
        scratch_shapes=[pltpu.VMEM(query.shape, BF16)] * 2 + [pltpu.VMEM(query.shape, F32)] * 2,
        compiler_params=pltpu.CompilerParams(vmem_limit_bytes=40 * 2**20),
        cost_estimate=attend_cost(heads, rows, 5),
        name="attend_back",
    )(attn, grad, query, keys, values)


def norm_stats(values):
    mean = jnp.mean(values, axis=-1, keepdims=True)
    center = values - mean
    spread = jnp.mean(center * center, axis=-1, keepdims=True)
    inverse = lax.rsqrt(spread + EPS)
    return center * inverse, inverse


def norm_back(grad, unit, inverse, gain):
    scaled = grad * gain
    return inverse * (
        scaled
        - jnp.mean(scaled, axis=-1, keepdims=True)
        - unit * jnp.mean(scaled * unit, axis=-1, keepdims=True)
    )


def update_one(rate, weight, grad, moment, average):
    moment_next = MOMENTUM * moment + grad
    weight_next = weight - rate * (grad + MOMENTUM * moment_next)
    return (weight_next, moment_next, DECAY * average + (1.0 - DECAY) * weight_next)


def on_device(
    tokens,
    lengths,
    cotangent,
    qkv_weight,
    out_weight,
    up_weight,
    down_weight,
    head_bias,
    up_bias,
    norm_vectors,
    qkv_moment,
    out_moment,
    up_moment,
    down_moment,
    head_bias_moment,
    up_bias_moment,
    norm_moment,
    qkv_average,
    out_average,
    up_average,
    down_average,
    head_bias_average,
    up_bias_average,
    norm_average,
):
    grid = Grid(lax.axis_size("dp"))
    member = lax.axis_index("mp")
    mate = member + 1 - 2 * lax.rem(member, 2)
    rows_local, width = tokens.shape
    head_width = qkv_weight.shape[2]
    stages = len(grid.dims)

    qkv_shard = jnp.transpose(qkv_weight, (1, 0, 2)).reshape(-1, 3 * head_width).astype(BF16)
    shards = (
        qkv_shard,
        out_weight.astype(BF16).T,
        up_weight.astype(BF16),
        down_weight.astype(BF16).T,
    )
    units = up_weight.shape[1]
    kernels = grid.size == 2 * CHAIN and units == width
    if kernels:
        flat = jnp.pad(head_bias.reshape(-1), (0, width - 2 * head_width))
        vectors = jnp.zeros((8, width), F32).at[0].set(up_bias).at[1].set(flat)
        *fulls, rows_both, own_cotangent, far_vectors = gather_all(
            shards, tokens, cotangent, vectors
        )
        pairs = [[full[at].reshape(width, -1) for at in (0, 1)] for full in fulls]
        qkv_pair, out_pair, up_pair, down_pair = pairs
        far_bias = far_vectors[1, : 2 * head_width].reshape(2, head_width)
        bias_pair, up_bias_pair = (head_bias, far_bias), (up_bias, far_vectors[0])
        tokens_all = rows_both.reshape(2 * rows_local, width)
        own_tokens = rows_both[0]
    else:
        qkv_pair = gather_half(grid, shards[0], stages)
        out_pair = gather_half(grid, shards[1], stages - 1)
        up_pair = gather_half(grid, shards[2], stages)
        down_pair = gather_half(grid, shards[3], stages - 1)
        bias_pair = (head_bias, half_swap(head_bias))
        up_bias_pair = (up_bias, half_swap(up_bias))
        own_tokens = bring(tokens, member)
        own_cotangent = bring(cotangent, member)
        tokens_all = jnp.concatenate([own_tokens, core_swap(own_tokens)], 0)

    slot_own, valid_own = row_table(rows_local, member, lengths)
    slot_mate, valid_mate = row_table(rows_local, mate, lengths)
    slot = jnp.concatenate([slot_own, slot_mate])
    frame = jnp.concatenate([valid_own, valid_mate])
    column = jnp.arange(HEAD_DIM)[None, :]
    here_slot = slot[:, None] == column
    slot_lanes = here_slot.astype(BF16)
    mask_lanes = jnp.where(
        column < len(LENS),
        jnp.where(here_slot & frame[:, None], 0.0, NEG_FILL),
        jnp.where(column < len(LENS) + 3, 1.0, 0.0),
    ).astype(BF16)
    live = valid_own[:, None]

    def share(rows):
        return jnp.concatenate([rows, core_swap(rows)], 0)

    def settle(partial):
        return partial[:rows_local] + core_swap(partial[rows_local:].astype(BF16)).astype(F32)

    block = 2 * rows_local
    parts = []
    for weight, bias in zip(qkv_pair, bias_pair):
        rows_bias = jnp.concatenate([bias[0], jnp.zeros_like(bias[0]), bias[1]])
        parts.append((dot(tokens_all, weight, ((1,), (0,))) + rows_bias).astype(BF16))
    attn, query, keys, values = attend(*parts, slot_lanes, mask_lanes, block)
    out_both = jnp.concatenate(out_pair, 1)
    branch = settle(dot(attn, out_both, ((1,), (1,))))
    unit_one, inverse_one = norm_stats(branch + norm_vectors[0] + own_tokens.astype(F32))
    first = unit_one * norm_vectors[2] + norm_vectors[3]
    first_all = share(first.astype(BF16))

    hiddens, slopes = [], []
    for weight, bias in zip(up_pair, up_bias_pair):
        pre = dot(first_all, weight, ((1,), (0,))) + bias
        phi = 0.5 * (1.0 + lax.erf(pre * (0.5**0.5)))
        density = jnp.exp(-0.5 * pre * pre) * (1.0 / math.sqrt(2.0 * math.pi))
        hiddens.append((pre * phi).astype(BF16))
        slopes.append((phi + pre * density).astype(BF16))
    ffn = settle(
        dot(hiddens[0], down_pair[0], ((1,), (1,))) + dot(hiddens[1], down_pair[1], ((1,), (1,)))
    )
    unit_two, inverse_two = norm_stats(ffn + norm_vectors[1] + first)
    second = unit_two * norm_vectors[4] + norm_vectors[5]
    layer_out = jnp.where(live, second, 0.0).astype(BF16)

    grad_two = jnp.where(live, own_cotangent.astype(F32), 0.0)
    d_second = norm_back(grad_two, unit_two, inverse_two, norm_vectors[4])
    d_ffn_all = share(d_second.astype(BF16))
    d_pres = [
        (dot(d_ffn_all, weight, ((1,), (0,))) * slope.astype(F32)).astype(BF16)
        for weight, slope in zip(down_pair, slopes)
    ]
    d_first = d_second + settle(
        dot(d_pres[0], up_pair[0], ((1,), (1,))) + dot(d_pres[1], up_pair[1], ((1,), (1,)))
    )
    grad_down = [dot(d_ffn_all, hidden, ((0,), (0,))).astype(BF16) for hidden in hiddens]
    grad_up = [dot(first_all, d_pre, ((0,), (0,))).astype(BF16) for d_pre in d_pres]
    grad_up_bias = [jnp.sum(d_pre, axis=0, dtype=F32) for d_pre in d_pres]

    d_branch = norm_back(d_first, unit_one, inverse_one, norm_vectors[2])
    d_branch_all = share(d_branch.astype(BF16))
    d_attn = dot(d_branch_all, out_both, ((1,), (0,))).astype(BF16)
    grad_out = [
        dot(d_branch_all, attn[:, at : at + head_width], ((0,), (0,))).astype(BF16)
        for at in (0, head_width)
    ]
    d_parts = attend_back(attn, d_attn, query, keys, values, block)
    grad_qkv = [dot(tokens_all, part, ((0,), (0,))).astype(BF16) for part in d_parts]
    grad_bias = [jnp.sum(part, axis=0, dtype=F32) for part in d_parts]
    d_tokens = settle(
        dot(d_parts[0], qkv_pair[0], ((1,), (1,))) + dot(d_parts[1], qkv_pair[1], ((1,), (1,)))
    )
    tokens_grad = d_tokens + d_branch

    norm_part = jnp.stack(
        [
            jnp.sum(d_branch, axis=0),
            jnp.sum(d_second, axis=0),
            jnp.sum(d_first * unit_one, axis=0),
            jnp.sum(d_first, axis=0),
            jnp.sum(grad_two * unit_two, axis=0),
            jnp.sum(grad_two, axis=0),
        ]
    )
    if kernels:
        pad = jnp.zeros((width - 3 * head_width,), F32)
        vectors = jnp.concatenate(
            [
                norm_part,
                jnp.stack(
                    [
                        grad_up_bias[0],
                        jnp.concatenate([grad_bias[0], pad]),
                        grad_up_bias[1],
                        jnp.concatenate([grad_bias[1], pad]),
                    ]
                ),
                jnp.zeros((6, width), F32),
            ]
        )
        source, free, count = move_plan(rows_local)
        near = (grad_qkv[0], grad_out[0], grad_up[0], grad_down[0])
        distant = (grad_qkv[1], grad_out[1], grad_up[1], grad_down[1])
        *sums, vectors, out_back, grad_back = scatter_all(
            near,
            distant,
            vectors,
            layer_out[free : free + count],
            tokens_grad[free : free + count],
        )
        sum_qkv, sum_out, sum_up, sum_down = sums
        layer_out = put_back(layer_out, out_back, member)
        tokens_grad = put_back(tokens_grad, grad_back, member)
        sum_norm, sum_up_bias, sum_bias = vectors[:6], vectors[6], vectors[7]
        sum_bias = sum_bias[: 3 * head_width]
    else:
        sum_qkv = scatter_sum(grid, *grad_qkv, True)
        sum_out = scatter_sum(grid, *grad_out, True)
        sum_up = scatter_sum(grid, *grad_up, False)
        sum_down = scatter_sum(grid, *grad_down, True)
        layer_out = send_back(layer_out, member)
        tokens_grad = send_back(tokens_grad, member)
        sum_norm = sum_all(grid, norm_part, True)
        sum_up_bias = sum_half(grid, grad_up_bias)
        sum_bias = sum_half(grid, grad_bias)
    sum_qkv = jnp.transpose(sum_qkv.reshape(-1, 3, head_width), (1, 0, 2))
    sum_out, sum_down = sum_out.T, sum_down.T
    sum_head_bias = jnp.stack([sum_bias[:head_width], sum_bias[2 * head_width :]])

    divisor = math.sqrt(1000.0 * grid.size * UTT)
    params = (qkv_weight, out_weight, up_weight, down_weight, head_bias, up_bias, norm_vectors)
    grads = (sum_qkv, sum_out, sum_up, sum_down, sum_head_bias, sum_up_bias, sum_norm)
    moments = (
        qkv_moment,
        out_moment,
        up_moment,
        down_moment,
        head_bias_moment,
        up_bias_moment,
        norm_moment,
    )
    averages = (
        qkv_average,
        out_average,
        up_average,
        down_average,
        head_bias_average,
        up_bias_average,
        norm_average,
    )
    nexts, moment_nexts, average_nexts = ([], [], [])
    for weight, grad, moment, average, scale_one in zip(
        params, grads, moments, averages, RATE_SCALES
    ):
        weight_next, moment_next, average_next = update_one(
            scale_one / divisor, weight, grad, moment, average
        )
        nexts.append(weight_next)
        moment_nexts.append(moment_next)
        average_nexts.append(average_next)
    return (layer_out, tokens_grad, *grads, *nexts, *moment_nexts, *average_nexts)


ROWS = P(("dp", "mp"), None)
PARAMS = (
    P(None, "dp", "mp"),
    P("mp", "dp"),
    P("dp", "mp"),
    P("mp", "dp"),
    P(None, "mp"),
    P("mp"),
    P(),
)


def solution(mesh):
    return jax.shard_map(
        on_device,
        mesh=mesh,
        in_specs=(ROWS, P("dp", None), ROWS) + PARAMS * 3,
        out_specs=(ROWS, ROWS) + PARAMS * 4,
        check_vma=False,
    )
```

```python
import math

import jax
import jax.numpy as jnp
from jax import lax
from jax.experimental import pallas as pl
from jax.experimental.pallas import tpu as pltpu
from jax.sharding import PartitionSpec as P

HEAD_DIM = 64
LANES = 128
UTT = 1
LENS = (256, 512, 896)
MOSTS = (200, 400, 781)

EPS = 1e-05
MOMENTUM = 0.5
DECAY = 0.5
RATE_SCALES = (0.02, 0.16, 0.02, 0.02, 0.02, 0.32, 0.16)
NEG_FILL = -1000000000.0
BF16 = jnp.bfloat16
F32 = jnp.float32


def dot(a, b, dims):
    return lax.dot_general(a, b, (dims, ((), ())), preferred_element_type=F32)


CORE_SWAP = [(0, 1), (1, 0), (2, 3), (3, 2)]
HALF_SWAP = [(0, 2), (2, 0), (1, 3), (3, 1)]


def core_swap(value):
    return lax.ppermute(value, "mp", CORE_SWAP)


def half_swap(value):
    return lax.ppermute(value, "mp", HALF_SWAP)


def dp_dims(size):
    dims = []
    while size % 4 == 0:
        dims.append(4)
        size //= 4
    if size > 1:
        dims.append(size)
    return tuple(dims)


class Grid:
    def __init__(self, size):
        self.dims = dp_dims(size)
        self.size = size
        rank = lax.axis_index("dp")
        self.strides = []
        stride = size
        for extent in self.dims:
            stride //= extent
            self.strides.append(stride)
        self.coords = [lax.rem(rank // s, e) for s, e in zip(self.strides, self.dims)]

    def send(self, value, stage, ahead):
        extent, stride = self.dims[stage], self.strides[stage]
        pairs = []
        for source in range(self.size):
            at = source // stride % extent
            pairs.append((source, source + ((at + ahead) % extent - at) * stride))
        return lax.ppermute(value, "dp", pairs)


def put(buffer, piece, axis, index):
    starts = [0] * buffer.ndim
    starts[axis] = index
    return lax.dynamic_update_slice(buffer, jnp.expand_dims(piece, axis), tuple(starts))


def take(buffer, axis, index):
    return lax.dynamic_index_in_dim(buffer, index, axis, keepdims=False)


def gather_half(grid, shard, half_stage):
    rows, columns = shard.shape
    value = shard[None]
    done = 0
    order = list(range(len(grid.dims)))
    for stage in order:
        if done == half_stage:
            value = jnp.concatenate([value, half_swap(value)], 0)
        extent, coord = grid.dims[stage], grid.coords[stage]
        axis = 1 + done
        shape = value.shape[:axis] + (extent,) + value.shape[axis:]
        buffer = put(jnp.zeros(shape, value.dtype), value, axis, coord)
        for ahead in range(1, extent):
            source = lax.rem(coord + extent - ahead, extent)
            buffer = put(buffer, grid.send(value, stage, ahead), axis, source)
        value = buffer
        done += 1
    if done == half_stage:
        other = half_swap(value)
        return value.reshape(-1, columns), other.reshape(-1, columns)
    return value[0].reshape(-1, columns), value[1].reshape(-1, columns)


def scatter_sum(grid, mine, theirs, half_first):
    columns = mine.shape[1]
    shape = grid.dims + (mine.shape[0] // grid.size, columns)
    order = list(range(len(grid.dims)))[::-1]

    def along(value, stage):
        extent, coord = grid.dims[stage], grid.coords[stage]
        axis = value.ndim - 3
        total = take(value, axis, coord).astype(F32)
        for ahead in range(1, extent):
            piece = take(value, axis, lax.rem(coord + ahead, extent))
            total = total + grid.send(piece.astype(BF16), stage, ahead).astype(F32)
        return total

    mine, theirs = mine.reshape(shape), theirs.reshape(shape)
    if half_first:
        value = mine.astype(F32) + half_swap(theirs.astype(BF16)).astype(F32)
        for stage in order:
            value = along(value, stage)
        return value
    first = order[0]
    mine = along(mine, first)
    theirs = along(theirs, first)
    value = mine + half_swap(theirs.astype(BF16)).astype(F32)
    for stage in order[1:]:
        value = along(value, stage)
    return value


def sum_half(grid, pair):
    value = pair[0] + half_swap(pair[1])
    for stage in range(len(grid.dims)):
        total = value
        for ahead in range(1, grid.dims[stage]):
            total = total + grid.send(value, stage, ahead)
        value = total
    return value


def sum_all(grid, value, over_cores):
    for stage in range(len(grid.dims)):
        total = value
        for ahead in range(1, grid.dims[stage]):
            total = total + grid.send(value, stage, ahead)
        value = total
    value = value + half_swap(value)
    if over_cores:
        value = value + core_swap(value)
    return value


def offsets():
    listing, offset = [], 0
    for extent in LENS:
        listing.append(offset)
        offset += UTT * extent
    return listing


def move_plan(rows_local):
    start = offsets()[2]
    count = 2 * rows_local - start
    free = -(-(start + MOSTS[2] - 3 * rows_local) // 16) * 16
    return rows_local - count, free, count


def row_table(rows_local, member, lengths):
    source, free, count = move_plan(rows_local)
    starts = offsets()
    local = jnp.arange(rows_local)
    row = member * rows_local + local
    slot = (row >= starts[1]).astype(jnp.int32) + (row >= starts[2]).astype(jnp.int32)
    place = row - jnp.where(slot == 0, starts[0], jnp.where(slot == 1, starts[1], starts[2]))
    arrived = (member == 3) & (local >= free) & (local < free + count)
    left = (member == 1) & (local >= source)
    place = jnp.where(arrived, local - free, place)
    length = jnp.where(slot == 0, lengths[0, 0], jnp.where(slot == 1, lengths[0, 1], lengths[0, 2]))
    return slot, (place < length) & ~left


def bring(rows, member):
    source, free, count = move_plan(rows.shape[0])
    moved = lax.ppermute(rows[source:], "mp", [(1, 3)])
    placed = lax.dynamic_update_slice(rows, moved, (free, 0))
    return jnp.where(member == 3, placed, rows)


def put_back(rows, moved, member):
    source, free, count = move_plan(rows.shape[0])
    placed = lax.dynamic_update_slice(rows, moved, (source, 0))
    cleared = lax.dynamic_update_slice(rows, jnp.zeros_like(moved), (free, 0))
    return jnp.where(member == 1, placed, jnp.where(member == 3, cleared, rows))


def send_back(rows, member):
    source, free, count = move_plan(rows.shape[0])
    return put_back(rows, lax.ppermute(rows[free : free + count], "mp", [(3, 1)]), member)


CHAIN = 4
X_FIRST = (False, True, True, False)
WHERE = [(0, 0)] + [(step, sign) for step in range(1, CHAIN) for sign in (1, -1)]


class Place:
    def __init__(self):
        self.dp = lax.axis_index("dp")
        self.mp = lax.axis_index("mp")
        self.z = self.dp // 2
        self.x = lax.rem(self.dp, 2)
        self.up = (self.dp + 2, self.mp)
        self.down = (self.dp - 2, self.mp)
        self.across = (self.dp + 1 - 2 * self.x, self.mp)
        self.other = (self.dp, lax.rem(self.mp + 2, 4))
        self.mate = (self.dp, self.mp + 1 - 2 * lax.rem(self.mp, 2))
        self.has_up = self.z < CHAIN - 1
        self.has_down = self.z > 0

    def ring(self, ahead):
        return (lax.rem(self.dp + 2 * ahead, 2 * CHAIN), self.mp)

    def greet(self, peers):
        barrier = pltpu.get_barrier_semaphore()
        for peer in peers:
            pl.semaphore_signal(
                barrier, inc=1, device_id=peer, device_id_type=pl.DeviceIdType.MESH
            )
        pl.semaphore_wait(barrier, len(peers))


def remote(source, target, sends, arrivals, index, device):
    return pltpu.make_async_remote_copy(
        source,
        target,
        sends.at[index],
        arrivals.at[index],
        device_id=device,
        device_id_type=pl.DeviceIdType.MESH,
    )


def gather_kernel(row_plan, *refs):
    shards, (rows_ref, cot_ref, vec_ref) = refs[0:4], refs[4:7]
    fulls, (rows_out, cot_out, vec_out) = refs[7:11], refs[11:14]
    sends, arrivals, side_send, side_arrive, local = refs[14:19]
    here = Place()
    source, free, count = row_plan
    n_rows = rows_ref.shape[0]
    here.greet([here.ring(1), here.ring(2), here.ring(3), here.across, here.other, here.mate,
                (here.dp, 3 - here.mp)])

    def z_of(where):
        step, sign = where
        return here.z - step * sign

    def held(where):
        step, sign = where
        if step == 0:
            return None
        return here.z >= step if sign > 0 else here.z + step < CHAIN

    def maybe(condition, action):
        if condition is None:
            action()
        else:
            pl.when(condition)(action)

    def block(w, where, far, half):
        x = 1 - here.x if far else here.x
        return fulls[w].at[half, z_of(where) * 2 + x]

    def chain(w, where):
        step, sign = where
        origin = shards[w] if step == 0 else block(w, where, False, 0)
        jobs = []
        for way in (1, -1) if step == 0 else (sign,):
            index = step + (0 if way > 0 else 3)
            device = here.up if way > 0 else here.down
            go = here.has_up if way > 0 else here.has_down
            if step < CHAIN - 1:
                jobs.append((go, remote(origin, block_to(w, where), sends.at[w], arrivals.at[w], index, device)))
        return jobs

    def block_to(w, where):
        return fulls[w].at[0, z_of(where) * 2 + here.x]

    def second(w, where):
        origin = shards[w] if where[0] == 0 else block(w, where, False, 0)
        index = 6 + WHERE.index(where)
        if X_FIRST[w]:
            return remote(origin, block(w, where, False, 0), sends.at[w], arrivals.at[w], index, here.across)
        return remote(origin, block(w, where, False, 1), sends.at[w], arrivals.at[w], index, here.other)

    def third(w, where, arrived):
        index = 13 + WHERE.index(where) + (len(WHERE) if arrived else 0)
        if X_FIRST[w]:
            origin = shards[w] if where[0] == 0 and not arrived else block(w, where, arrived, 0)
            return remote(origin, block(w, where, arrived, 1), sends.at[w], arrivals.at[w], index, here.other)
        origin = shards[w] if where[0] == 0 and not arrived else block(w, where, False, int(arrived))
        return remote(origin, block(w, where, False, int(arrived)), sends.at[w], arrivals.at[w], index, here.across)

    def landing(w, where, stage, arrived=False):
        if stage == 2:
            index = 6 + WHERE.index(where)
            target = block(w, where, True, 0) if X_FIRST[w] else block(w, where, False, 1)
            device = here.across if X_FIRST[w] else here.other
        else:
            index = 13 + WHERE.index(where) + (len(WHERE) if arrived else 0)
            if X_FIRST[w]:
                target, device = block(w, where, arrived, 1), here.other
            else:
                target, device = block(w, where, True, int(arrived)), here.across
        return remote(target, target, sends.at[w], arrivals.at[w], index, device)

    def chain_landing(w, where):
        step, sign = where
        index = step - 1 + (0 if sign > 0 else 3)
        target = block(w, where, False, 0)
        return remote(target, target, sends.at[w], arrivals.at[w], index, here.down if sign > 0 else here.up)

    order = (0, 1, 3, 2)
    by_step = [[p for p in WHERE if p[0] == step] for step in range(CHAIN)]

    low, high = pl.ds(0, free), pl.ds(free + count, n_rows - free - count)
    middle, tail = pl.ds(free, count), pl.ds(source, count)
    locals_ = [(None, pltpu.make_async_copy(shards[w], fulls[w].at[0, here.dp], local.at[w])) for w in order]
    not_last, second_core = here.mp != 3, here.mp == 1
    for n, (given, taken) in enumerate(((rows_ref, rows_out.at[0]), (cot_ref, cot_out))):
        for m, part in enumerate((low, high, middle)):
            copy = pltpu.make_async_copy(given.at[part], taken.at[part], local.at[4 + 3 * n + m])
            locals_.append((not_last if m == 2 else None, copy))
    for condition, copy in locals_:
        maybe(condition, copy.start)

    def to_mate(m, part):
        return remote(rows_ref.at[part], rows_out.at[1, part], side_send, side_arrive, m, here.mate)

    side = [(None, to_mate(0, low)), (None, to_mate(1, high)), (not_last, to_mate(2, middle))]
    side.append((None, remote(vec_ref, vec_out, side_send, side_arrive, 3, here.other)))
    moved = [
        remote(rows_ref.at[tail], rows_out.at[0, middle], side_send, side_arrive, 4, here.other),
        remote(cot_ref.at[tail], cot_out.at[middle], side_send, side_arrive, 5, here.other),
        remote(rows_ref.at[tail], rows_out.at[1, middle], side_send, side_arrive, 6, (here.dp, 3 - here.mp)),
    ]
    side += [(second_core, copy) for copy in moved]

    started = []

    def start(condition, copy):
        maybe(condition, copy.start)
        started.append((condition, copy))

    for condition, copy in side:
        start(condition, copy)
    for step in range(CHAIN):
        for where in by_step[step]:
            for w in order:
                if step > 0:
                    maybe(held(where), chain_landing(w, where).wait_recv)
                for go, copy in chain(w, where):
                    both = go if held(where) is None else jnp.logical_and(go, held(where))
                    start(both, copy)
                start(held(where), second(w, where))
                start(held(where), third(w, where, False))
        for where in by_step[step - 1] if step > 0 else ():
            for w in order:
                maybe(held(where), landing(w, where, 2).wait_recv)
                start(held(where), third(w, where, True))
    for where in by_step[CHAIN - 1]:
        for w in order:
            maybe(held(where), landing(w, where, 2).wait_recv)
            start(held(where), third(w, where, True))
    for where in WHERE:
        for w in order:
            for arrived in (False, True):
                maybe(held(where), landing(w, where, 3, arrived).wait_recv)
    to_mate(0, low).wait_recv()
    to_mate(1, high).wait_recv()
    pl.when(here.mp != 2)(to_mate(2, middle).wait_recv)
    side[3][1].wait_recv()
    pl.when(here.mp == 3)(moved[0].wait_recv)
    pl.when(here.mp == 3)(moved[1].wait_recv)
    pl.when(here.mp == 2)(moved[2].wait_recv)
    for condition, copy in started:
        maybe(condition, copy.wait_send)
    for condition, copy in locals_:
        maybe(condition, copy.wait)


def gather_all(shards, rows, cotangent, vectors):
    rows_local, width = rows.shape
    vmem, anywhere = pl.BlockSpec(memory_space=pltpu.VMEM), pl.BlockSpec(memory_space=pl.ANY)
    shapes = [jax.ShapeDtypeStruct((2, 2 * CHAIN) + s.shape, s.dtype) for s in shards]
    shapes += [
        jax.ShapeDtypeStruct((2, rows_local, width), rows.dtype),
        jax.ShapeDtypeStruct((rows_local, width), rows.dtype),
        jax.ShapeDtypeStruct(vectors.shape, vectors.dtype),
    ]
    plan = move_plan(rows_local)
    return pl.pallas_call(
        lambda *refs: gather_kernel(plan, *refs),
        out_shape=shapes,
        in_specs=[vmem] * 7,
        out_specs=[anywhere] * 6 + [vmem],
        scratch_shapes=[
            pltpu.SemaphoreType.DMA((4, 27)),
            pltpu.SemaphoreType.DMA((4, 27)),
            pltpu.SemaphoreType.DMA((7,)),
            pltpu.SemaphoreType.DMA((7,)),
            pltpu.SemaphoreType.DMA((10,)),
        ],
        compiler_params=pltpu.CompilerParams(
            collective_id=0, has_side_effects=True, vmem_limit_bytes=16 * 2**20
        ),
        name="gather_all",
    )(*shards, rows, cotangent, vectors)


def scatter_kernel(*refs):
    mine = (refs[0], refs[2], refs[4].at[0], refs[5].at[0])
    theirs = (refs[1], refs[3], refs[4].at[1], refs[5].at[1])
    vec_ref, out_edge, grad_edge = refs[6:9]
    sums, (vec_out, out_back, grad_back) = refs[9:13], refs[13:16]
    firsts, seconds, rises, falls = refs[16:20], refs[20:24], refs[24:28], refs[28:32]
    finals = refs[32:36]
    vec_in, sends, arrivals, side_send, side_arrive = refs[36:41]
    here = Place()
    here.greet([here.ring(1), here.ring(2), here.ring(3), here.across, here.other, here.mate])
    order = (2, 3, 1, 0)
    targets = (3, 0, 2, 1)
    far = 1 - here.x
    started = []

    def start(copy, condition=None):
        if condition is None:
            copy.start()
        else:
            pl.when(condition)(copy.start)
        started.append((condition, copy))
        return copy

    def add(target, more):
        target[...] = (target[...].astype(F32) + more[...].astype(F32)).astype(BF16)

    edges = []
    for index, (given, taken) in enumerate(((out_edge, out_back), (grad_edge, grad_back))):
        copy = remote(given, taken, side_send, side_arrive, 6 + index, here.other)
        edges.append(start(copy, here.mp == 3))

    def vec_send(index, device):
        copy = remote(vec_out, vec_in.at[index], side_send, side_arrive, index, device)
        copy.start()
        return copy

    vec_out[...] = vec_ref[...]
    sent = vec_send(0, here.other)

    first_jobs, second_jobs = {}, {}
    for target in targets:
        for w in order:
            for part in (0, 1):
                if X_FIRST[w]:
                    origin, device = theirs[w].at[target, part], here.other
                else:
                    origin, device = (mine, theirs)[part][w].at[target, far], here.across
                landed = firsts[w].at[target, part]
                first_jobs[w, target, part] = start(
                    remote(origin, landed, sends.at[w], arrivals.at[w], 2 * target + part, device)
                )
    sent.wait()
    vec_out[0:6] = vec_out[0:6] + vec_in[0, 0:6]
    vec_out[6:8] = vec_out[6:8] + vec_in[0, 8:10]
    sent = vec_send(1, here.across)

    for target in targets:
        for w in order:
            for part in (0, 1):
                first_jobs[w, target, part].wait_recv()
                if X_FIRST[w]:
                    add(firsts[w].at[target, part], mine[w].at[target, part])
                else:
                    add(firsts[w].at[target, part], (mine, theirs)[part][w].at[target, here.x])
            if X_FIRST[w]:
                origin, device = firsts[w].at[target, far], here.across
            else:
                origin, device = firsts[w].at[target, 1], here.other
            landed = seconds[w].at[target]
            second_jobs[w, target] = start(
                remote(origin, landed, sends.at[w], arrivals.at[w], 8 + target, device)
            )
    sent.wait()
    vec_out[...] = vec_out[...] + vec_in[1]
    ring = [vec_send(1 + ahead, here.ring(ahead)) for ahead in (1, 2, 3)]

    def lane(w, target, up):
        at = target - 1 if up else target
        return (rises if up else falls)[w].at[at], (12 if up else 15) + at

    def receive(w, target, up):
        slot, index = lane(w, target, up)
        device = here.down if up else here.up
        return remote(slot, slot, sends.at[w], arrivals.at[w], index, device)

    def pass_on(w, target, up):
        slot, index = lane(w, target, up)
        device = here.up if up else here.down
        return remote(seconds[w].at[target], slot, sends.at[w], arrivals.at[w], index, device)

    def take_in(w, target, up):
        receive(w, target, up).wait_recv()
        add(seconds[w].at[target], lane(w, target, up)[0])

    for target in targets:
        for w in order:
            second_jobs[w, target].wait_recv()
            kept = firsts[w].at[target, here.x] if X_FIRST[w] else firsts[w].at[target, 0]
            add(seconds[w].at[target], kept)
            for up in (True, False):
                if target == (0 if up else CHAIN - 1):
                    continue
                before = here.z < target if up else here.z > target
                inner = here.has_down if up else here.has_up
                pl.when(jnp.logical_and(before, inner))(
                    lambda w=w, target=target, up=up: take_in(w, target, up)
                )
                start(pass_on(w, target, up), before)

    for copy in ring:
        copy.wait()
    slots = [vec_out[...], vec_in[2], vec_in[3], vec_in[4]]
    total = jnp.zeros_like(slots[0])
    for at in range(CHAIN):
        for behind in range(CHAIN):
            same = lax.rem(here.z + CHAIN - behind, CHAIN) == at
            total = total + jnp.where(same, slots[behind], 0.0)
    vec_out[...] = total
    sent = vec_send(5, here.mate)

    def finish(w, target, up):
        receive(w, target, up).wait_recv()
        finals[w][...] += lane(w, target, up)[0][...].astype(F32)

    for w in order:
        finals[w][...] = seconds[w][here.z].astype(F32)
        for up in (True, False):
            for target in range(CHAIN):
                if target != (0 if up else CHAIN - 1):
                    pl.when(here.z == target)(
                        lambda w=w, target=target, up=up: finish(w, target, up)
                    )

    for c in range(sums[0].shape[0]):
        sums[0][c] = finals[0][:, c * sums[0].shape[2] : (c + 1) * sums[0].shape[2]]
    for w in (2, 3):
        sums[w][...] = finals[w][...]
    value = finals[1][...]
    pad = jnp.zeros((LANES - value.shape[0], value.shape[1]), F32)
    sums[1][...] = jnp.concatenate([value, pad], 0).T[:, : value.shape[0]]

    sent.wait()
    vec_out[0:6] = vec_out[0:6] + vec_in[5, 0:6]
    for copy in edges:
        pl.when(here.mp == 1)(copy.wait_recv)
    for condition, copy in started:
        if condition is None:
            copy.wait_send()
        else:
            pl.when(condition)(copy.wait_send)


def scatter_all(qkv, out, up, down, vectors, out_edge, grad_edge):
    rows = up.shape[1] // (2 * CHAIN)
    qkv, out = [[g.reshape(CHAIN, 2, rows, -1) for g in pair] for pair in (qkv, out)]
    up, down = [g.reshape(2, CHAIN, 2, rows, -1) for g in (up, down)]
    widths = [g.shape[-1] for g in (qkv[0], out[0], up, down)]
    vmem = pl.BlockSpec(memory_space=pltpu.VMEM)
    shapes = [(3, rows, widths[0] // 3), (widths[1], rows), (rows, widths[2]), (rows, widths[3])]
    shapes = [jax.ShapeDtypeStruct(shape, F32) for shape in shapes]
    shapes += [jax.ShapeDtypeStruct(v.shape, v.dtype) for v in (vectors, out_edge, grad_edge)]
    scratch = [pltpu.VMEM((CHAIN, 2, rows, n), BF16) for n in widths]
    scratch += [pltpu.VMEM((CHAIN, rows, n), BF16) for n in widths]
    scratch += [pltpu.VMEM((CHAIN - 1, rows, n), BF16) for n in widths] * 2
    scratch += [pltpu.VMEM((rows, n), F32) for n in widths]
    scratch += [
        pltpu.VMEM((6,) + vectors.shape, F32),
        pltpu.SemaphoreType.DMA((4, 18)),
        pltpu.SemaphoreType.DMA((4, 18)),
        pltpu.SemaphoreType.DMA((8,)),
        pltpu.SemaphoreType.DMA((8,)),
    ]
    return pl.pallas_call(
        scatter_kernel,
        out_shape=shapes,
        in_specs=[vmem] * 9,
        out_specs=[vmem] * 7,
        scratch_shapes=scratch,
        compiler_params=pltpu.CompilerParams(
            collective_id=1, has_side_effects=True, vmem_limit_bytes=48 * 2**20
        ),
        name="scatter_all",
    )(*qkv, *out, up, down, vectors, out_edge, grad_edge)

def split_parts(value, count):
    parts = []
    for _ in range(count):
        part = value.astype(BF16).astype(F32)
        parts.append(part)
        value = value - part
    return parts


def lane_fill(base, parts, first):
    lane = lax.broadcasted_iota(jnp.int32, base.shape, 1)
    for index, part in enumerate(parts):
        base = jnp.where(lane == first + index, part, base)
    return base


def head_columns(head, part, per_half):
    half, index = divmod(head, per_half)
    at = (part * per_half + index) * HEAD_DIM
    return half, slice(at, at + HEAD_DIM)


def attend_kernel(block, near_ref, far_ref, slot_ref, mask_ref, attn_ref, q_ref, k_ref, v_ref, out_ref):
    acts = (near_ref, far_ref)
    heads, rows = q_ref.shape[:2]
    ones = lane_fill(jnp.zeros((rows, HEAD_DIM), F32), (1.0, 1.0), 0).astype(BF16)
    for head in range(heads):
        for part, (ref, more) in enumerate(((q_ref, slot_ref), (k_ref, mask_ref), (v_ref, None))):
            half, columns = head_columns(head, part, heads // 2)
            piece = acts[half][:, columns]
            if part == 0:
                piece = (piece.astype(F32) * HEAD_DIM ** (-0.5)).astype(BF16)
            ref[head, :, 0:HEAD_DIM] = piece
            ref[head, :, HEAD_DIM : 2 * HEAD_DIM] = ones if more is None else more[...]

    def step(index, carry):
        head, at = index // (rows // block), lax.rem(index, rows // block)
        span = pl.ds(pl.multiple_of(at * block, 16), block)
        query = q_ref[head, span, :]
        scores = dot(query, k_ref[head], ((1,), (1,)))
        peak = jnp.max(scores, axis=-1, keepdims=True)
        weights = jnp.exp(scores - peak)
        both = dot(weights.astype(BF16), v_ref[head], ((1,), (0,)))
        total = both[:, HEAD_DIM : HEAD_DIM + 1]
        out_ref[head, span, :] = (both * (1.0 / total)).astype(BF16)
        log_sum = peak + jnp.log(total)
        parts = [-p for p in split_parts(log_sum, 3)]
        q_ref[head, span, :] = lane_fill(query.astype(F32), parts, HEAD_DIM + 3).astype(BF16)
        return carry

    lax.fori_loop(0, heads * (rows // block), step, 0, unroll=6)
    for head in range(heads):
        attn_ref[:, head * HEAD_DIM : (head + 1) * HEAD_DIM] = out_ref[head, :, 0:HEAD_DIM]


def attend_back_kernel(block, attn_ref, grad_ref, q_ref, k_ref, v_ref, near_ref, far_ref, g_ref, dq_ref, dk_ref, dv_ref):
    heads, rows = q_ref.shape[:2]
    for head in range(heads):
        columns = slice(head * HEAD_DIM, (head + 1) * HEAD_DIM)
        grad = grad_ref[:, columns]
        mean = jnp.sum(grad.astype(F32) * attn_ref[:, columns].astype(F32), axis=-1, keepdims=True)
        parts = [-p for p in split_parts(mean, 2)]
        g_ref[head, :, 0:HEAD_DIM] = grad
        g_ref[head, :, HEAD_DIM : 2 * HEAD_DIM] = lane_fill(
            jnp.zeros((rows, HEAD_DIM), F32), parts, 0
        ).astype(BF16)
    dk_ref[...] = jnp.zeros_like(dk_ref)
    dv_ref[...] = jnp.zeros_like(dv_ref)

    def step(index, carry):
        head, at = index // (rows // block), lax.rem(index, rows // block)
        span = pl.ds(pl.multiple_of(at * block, 16), block)
        query, grad = q_ref[head, span, :], g_ref[head, span, :]
        keys = k_ref[head]
        probs = jnp.exp(dot(keys, query, ((1,), (1,))))
        change = (probs * dot(v_ref[head], grad, ((1,), (1,)))).astype(BF16)
        dv_ref[head] += dot(probs.astype(BF16), grad, ((1,), (0,)))
        dk_ref[head] += dot(change, query, ((1,), (0,)))
        dq_ref[head, span, :] = (dot(change, keys, ((0,), (0,))) * HEAD_DIM ** (-0.5)).astype(BF16)
        return carry

    lax.fori_loop(0, heads * (rows // block), step, 0, unroll=6)
    outs = (near_ref, far_ref)
    for head in range(heads):
        for part, ref in enumerate((dq_ref, dk_ref, dv_ref)):
            half, columns = head_columns(head, part, heads // 2)
            outs[half][:, columns] = ref[head, :, 0:HEAD_DIM].astype(BF16)


def attend_cost(heads, rows, products):
    return pl.CostEstimate(
        flops=2 * products * heads * rows * rows * 128,
        bytes_accessed=8 * heads * rows * 128,
        transcendentals=heads * rows * rows,
    )


def attend(near, far, slots, masks, block):
    rows = near.shape[0]
    heads = 2 * near.shape[1] // (3 * HEAD_DIM)
    vmem = pl.BlockSpec(memory_space=pltpu.VMEM)
    wide = jax.ShapeDtypeStruct((heads, rows, 2 * HEAD_DIM), BF16)
    return pl.pallas_call(
        lambda *refs: attend_kernel(block, *refs),
        out_shape=[jax.ShapeDtypeStruct((rows, heads * HEAD_DIM), BF16), wide, wide, wide],
        in_specs=[vmem] * 4,
        out_specs=[vmem] * 4,
        scratch_shapes=[pltpu.VMEM(wide.shape, BF16)],
        compiler_params=pltpu.CompilerParams(vmem_limit_bytes=40 * 2**20),
        cost_estimate=attend_cost(heads, rows, 2),
        name="attend",
    )(near, far, slots, masks)


def attend_back(attn, grad, query, keys, values, block):
    heads, rows = query.shape[:2]
    vmem = pl.BlockSpec(memory_space=pltpu.VMEM)
    out = jax.ShapeDtypeStruct((rows, 3 * heads // 2 * HEAD_DIM), BF16)
    return pl.pallas_call(
        lambda *refs: attend_back_kernel(block, *refs),
        out_shape=[out, out],
        in_specs=[vmem] * 5,
        out_specs=[vmem] * 2,
        scratch_shapes=[pltpu.VMEM(query.shape, BF16)] * 2 + [pltpu.VMEM(query.shape, F32)] * 2,
        compiler_params=pltpu.CompilerParams(vmem_limit_bytes=40 * 2**20),
        cost_estimate=attend_cost(heads, rows, 5),
        name="attend_back",
    )(attn, grad, query, keys, values)


def norm_stats(values):
    mean = jnp.mean(values, axis=-1, keepdims=True)
    center = values - mean
    spread = jnp.mean(center * center, axis=-1, keepdims=True)
    inverse = lax.rsqrt(spread + EPS)
    return center * inverse, inverse


def norm_back(grad, unit, inverse, gain):
    scaled = grad * gain
    return inverse * (
        scaled
        - jnp.mean(scaled, axis=-1, keepdims=True)
        - unit * jnp.mean(scaled * unit, axis=-1, keepdims=True)
    )


def feed_back_kernel(n_rows, first_ref, grad_ref, up_ref, down_ref, near_hidden, far_hidden,
                     near_slope, far_slope, g_up_ref, g_down_ref, g_bias_ref, own_ref, mate_ref, total_ref, first_t, grad_t):
    step = pl.program_id(0)

    @pl.when(step == 0)
    def _():
        first_t[...] = first_ref[...].T
        grad_t[...] = grad_ref[...].T
        total_ref[...] = jnp.zeros_like(total_ref)

    near = step < pl.num_programs(0) // 2
    hidden = jnp.where(near, near_hidden[...], far_hidden[...])
    slope = jnp.where(near, near_slope[...], far_slope[...])
    d_hidden = dot(grad_ref[...], down_ref[0], ((1,), (0,)))
    d_pre = (d_hidden * slope.astype(F32)).astype(BF16)
    total_ref[...] += dot(d_pre, up_ref[0], ((1,), (1,)))
    g_bias_ref[0] = jnp.sum(d_pre.astype(F32), axis=0, keepdims=True)
    g_up_ref[0] = dot(first_t[...], d_pre, ((1,), (0,))).astype(BF16)
    g_down_ref[0] = dot(grad_t[...], hidden, ((1,), (0,))).astype(BF16)

    @pl.when(step == pl.num_programs(0) - 1)
    def _():
        own_ref[...] = total_ref[0:n_rows, :]
        mate_ref[...] = total_ref[n_rows:, :].astype(BF16)


def feed_specs(rows, width, units, tile):
    blocks = units // tile
    whole = pl.BlockSpec((rows, width), lambda i: (0, 0))
    half = pl.BlockSpec((rows // 2, width), lambda i: (0, 0))

    def split(count):
        return pl.BlockSpec((1, count, tile), lambda i: (i // blocks, 0, lax.rem(i, blocks)))

    halves = [jax.ShapeDtypeStruct((rows // 2, width), kind) for kind in (F32, BF16)]
    return (2 * blocks,), whole, half, split, halves


def feed_back(first, grad, up, down, hiddens, slopes, tile):
    (rows, width), units = first.shape, up.shape[2]
    grid, whole, half, split, halves = feed_specs(rows, width, units, tile)
    last = units // tile - 1
    near = pl.BlockSpec((rows, tile), lambda i: (0, jnp.minimum(i, last)))
    far = pl.BlockSpec((rows, tile), lambda i: (0, jnp.maximum(i - last - 1, 0)))
    wide = jax.ShapeDtypeStruct((2, width, units), BF16)
    return pl.pallas_call(
        lambda *refs: feed_back_kernel(rows // 2, *refs),
        grid=grid,
        out_shape=[wide, wide, jax.ShapeDtypeStruct((2, 1, units), F32)] + halves,
        in_specs=[whole, whole, split(width), split(width), near, far, near, far],
        out_specs=[split(width), split(width), split(1), half, half],
        scratch_shapes=[
            pltpu.VMEM((rows, width), F32),
            pltpu.VMEM((width, rows), BF16),
            pltpu.VMEM((width, rows), BF16),
        ],
        compiler_params=pltpu.CompilerParams(vmem_limit_bytes=48 * 2**20),
        cost_estimate=pl.CostEstimate(
            flops=16 * rows * width * units,
            bytes_accessed=16 * width * units + 8 * rows * units,
            transcendentals=0,
        ),
        name="feed_back",
    )(first, grad, up, down, *hiddens, *slopes)


def update_one(rate, weight, grad, moment, average):
    moment_next = MOMENTUM * moment + grad
    weight_next = weight - rate * (grad + MOMENTUM * moment_next)
    return (weight_next, moment_next, DECAY * average + (1.0 - DECAY) * weight_next)


def on_device(
    tokens,
    lengths,
    cotangent,
    qkv_weight,
    out_weight,
    up_weight,
    down_weight,
    head_bias,
    up_bias,
    norm_vectors,
    qkv_moment,
    out_moment,
    up_moment,
    down_moment,
    head_bias_moment,
    up_bias_moment,
    norm_moment,
    qkv_average,
    out_average,
    up_average,
    down_average,
    head_bias_average,
    up_bias_average,
    norm_average,
):
    grid = Grid(lax.axis_size("dp"))
    member = lax.axis_index("mp")
    mate = member + 1 - 2 * lax.rem(member, 2)
    rows_local, width = tokens.shape
    head_width = qkv_weight.shape[2]
    stages = len(grid.dims)
    units = up_weight.shape[1]

    qkv_shard = jnp.transpose(qkv_weight, (1, 0, 2)).reshape(-1, 3 * head_width).astype(BF16)
    shards = (
        qkv_shard,
        out_weight.astype(BF16).T,
        up_weight.astype(BF16),
        down_weight.astype(BF16).T,
    )
    kernels = grid.size == 2 * CHAIN and units == width
    if kernels:
        flat = jnp.pad(head_bias.reshape(-1), (0, width - 2 * head_width))
        vectors = jnp.zeros((8, width), F32).at[0].set(up_bias).at[1].set(flat)
        *fulls, rows_both, own_cotangent, far_vectors = gather_all(
            shards, tokens, cotangent, vectors
        )
        qkv_pair, out_pair, up_pair, down_pair = [full.reshape(2, width, -1) for full in fulls]
        far_bias = far_vectors[1, : 2 * head_width].reshape(2, head_width)
        bias_pair, up_bias_pair = (head_bias, far_bias), (up_bias, far_vectors[0])
        tokens_all = rows_both.reshape(2 * rows_local, width)
        own_tokens = rows_both[0]
    else:
        qkv_pair = gather_half(grid, shards[0], stages)
        out_pair = gather_half(grid, shards[1], stages - 1)
        up_pair = jnp.stack(gather_half(grid, shards[2], stages))
        down_pair = jnp.stack(gather_half(grid, shards[3], stages - 1))
        bias_pair = (head_bias, half_swap(head_bias))
        up_bias_pair = (up_bias, half_swap(up_bias))
        own_tokens = bring(tokens, member)
        own_cotangent = bring(cotangent, member)
        tokens_all = jnp.concatenate([own_tokens, core_swap(own_tokens)], 0)

    slot_own, valid_own = row_table(rows_local, member, lengths)
    slot_mate, valid_mate = row_table(rows_local, mate, lengths)
    slot = jnp.concatenate([slot_own, slot_mate])
    frame = jnp.concatenate([valid_own, valid_mate])
    column = jnp.arange(HEAD_DIM)[None, :]
    here_slot = slot[:, None] == column
    slot_lanes = here_slot.astype(BF16)
    mask_lanes = jnp.where(
        column < len(LENS),
        jnp.where(here_slot & frame[:, None], 0.0, NEG_FILL),
        jnp.where(column < len(LENS) + 3, 1.0, 0.0),
    ).astype(BF16)
    live = valid_own[:, None]

    def share(rows):
        return jnp.concatenate([rows, core_swap(rows)], 0)

    def settle(partial):
        return partial[:rows_local] + core_swap(partial[rows_local:].astype(BF16)).astype(F32)

    block = 2 * rows_local
    parts = []
    for weight, bias in zip(qkv_pair, bias_pair):
        rows_bias = jnp.concatenate([bias[0], jnp.zeros_like(bias[0]), bias[1]])
        parts.append((dot(tokens_all, weight, ((1,), (0,))) + rows_bias).astype(BF16))
    attn, query, keys, values = attend(*parts, slot_lanes, mask_lanes, block)
    out_both = jnp.concatenate([out_pair[0], out_pair[1]], 1)
    branch = settle(dot(attn, out_both, ((1,), (1,))))
    unit_one, inverse_one = norm_stats(branch + norm_vectors[0] + own_tokens.astype(F32))
    first = unit_one * norm_vectors[2] + norm_vectors[3]
    first_all = share(first.astype(BF16))

    hiddens, slopes = [], []
    for at in (0, 1):
        pre = dot(first_all, up_pair[at], ((1,), (0,))) + up_bias_pair[at]
        phi = 0.5 * (1.0 + lax.erf(pre * (0.5**0.5)))
        density = jnp.exp(-0.5 * pre * pre) * (1.0 / math.sqrt(2.0 * math.pi))
        hiddens.append((pre * phi).astype(BF16))
        slopes.append((phi + pre * density).astype(BF16))
    ffn = settle(
        dot(hiddens[0], down_pair[0], ((1,), (1,))) + dot(hiddens[1], down_pair[1], ((1,), (1,)))
    )
    unit_two, inverse_two = norm_stats(ffn + norm_vectors[1] + first)
    second = unit_two * norm_vectors[4] + norm_vectors[5]
    layer_out = jnp.where(live, second, 0.0).astype(BF16)

    grad_two = jnp.where(live, own_cotangent.astype(F32), 0.0)
    d_second = norm_back(grad_two, unit_two, inverse_two, norm_vectors[4])
    d_ffn_all = share(d_second.astype(BF16))
    tile = 2 * LANES if units % (2 * LANES) == 0 else units
    grad_up, grad_down, grad_up_bias, d_first_own, d_first_mate = feed_back(
        first_all, d_ffn_all, up_pair, down_pair, hiddens, slopes, tile
    )
    grad_up_bias = grad_up_bias[:, 0, :]
    d_first = d_second + (d_first_own + core_swap(d_first_mate).astype(F32))

    d_branch = norm_back(d_first, unit_one, inverse_one, norm_vectors[2])
    d_branch_all = share(d_branch.astype(BF16))
    d_attn = dot(d_branch_all, out_both, ((1,), (0,))).astype(BF16)
    grad_out = [
        dot(d_branch_all, attn[:, at : at + head_width], ((0,), (0,))).astype(BF16)
        for at in (0, head_width)
    ]
    d_parts = attend_back(attn, d_attn, query, keys, values, block)
    grad_qkv = [dot(tokens_all, part, ((0,), (0,))).astype(BF16) for part in d_parts]
    grad_bias = [jnp.sum(part, axis=0, dtype=F32) for part in d_parts]
    d_tokens = settle(
        dot(d_parts[0], qkv_pair[0], ((1,), (1,))) + dot(d_parts[1], qkv_pair[1], ((1,), (1,)))
    )
    tokens_grad = d_tokens + d_branch

    norm_part = jnp.stack(
        [
            jnp.sum(d_branch, axis=0),
            jnp.sum(d_second, axis=0),
            jnp.sum(d_first * unit_one, axis=0),
            jnp.sum(d_first, axis=0),
            jnp.sum(grad_two * unit_two, axis=0),
            jnp.sum(grad_two, axis=0),
        ]
    )
    if kernels:
        pad = jnp.zeros((width - 3 * head_width,), F32)
        vectors = jnp.concatenate(
            [
                norm_part,
                jnp.stack(
                    [
                        grad_up_bias[0],
                        jnp.concatenate([grad_bias[0], pad]),
                        grad_up_bias[1],
                        jnp.concatenate([grad_bias[1], pad]),
                    ]
                ),
                jnp.zeros((6, width), F32),
            ]
        )
        source, free, count = move_plan(rows_local)
        *sums, vectors, out_back, grad_back = scatter_all(
            grad_qkv,
            grad_out,
            grad_up,
            grad_down,
            vectors,
            layer_out[free : free + count],
            tokens_grad[free : free + count],
        )
        sum_qkv, sum_out, sum_up, sum_down = sums
        sum_down = sum_down.T
        layer_out = put_back(layer_out, out_back, member)
        tokens_grad = put_back(tokens_grad, grad_back, member)
        sum_norm, sum_up_bias, sum_bias = vectors[:6], vectors[6], vectors[7]
        sum_bias = sum_bias[: 3 * head_width]
    else:
        sum_qkv = scatter_sum(grid, *grad_qkv, True)
        sum_out = scatter_sum(grid, *grad_out, True)
        sum_up = scatter_sum(grid, *grad_up, False)
        sum_down = scatter_sum(grid, *grad_down, True)
        layer_out = send_back(layer_out, member)
        tokens_grad = send_back(tokens_grad, member)
        sum_norm = sum_all(grid, norm_part, True)
        sum_up_bias = sum_half(grid, grad_up_bias)
        sum_bias = sum_half(grid, grad_bias)
        sum_qkv = jnp.transpose(sum_qkv.reshape(-1, 3, head_width), (1, 0, 2))
        sum_out, sum_down = sum_out.T, sum_down.T
    sum_head_bias = jnp.stack([sum_bias[:head_width], sum_bias[2 * head_width :]])

    divisor = math.sqrt(1000.0 * grid.size * UTT)
    params = (qkv_weight, out_weight, up_weight, down_weight, head_bias, up_bias, norm_vectors)
    grads = (sum_qkv, sum_out, sum_up, sum_down, sum_head_bias, sum_up_bias, sum_norm)
    moments = (
        qkv_moment,
        out_moment,
        up_moment,
        down_moment,
        head_bias_moment,
        up_bias_moment,
        norm_moment,
    )
    averages = (
        qkv_average,
        out_average,
        up_average,
        down_average,
        head_bias_average,
        up_bias_average,
        norm_average,
    )
    nexts, moment_nexts, average_nexts = ([], [], [])
    for weight, grad, moment, average, scale_one in zip(
        params, grads, moments, averages, RATE_SCALES
    ):
        weight_next, moment_next, average_next = update_one(
            scale_one / divisor, weight, grad, moment, average
        )
        nexts.append(weight_next)
        moment_nexts.append(moment_next)
        average_nexts.append(average_next)
    return (layer_out, tokens_grad, *grads, *nexts, *moment_nexts, *average_nexts)


ROWS = P(("dp", "mp"), None)
PARAMS = (
    P(None, "dp", "mp"),
    P("mp", "dp"),
    P("dp", "mp"),
    P("mp", "dp"),
    P(None, "mp"),
    P("mp"),
    P(),
)


def solution(mesh):
    return jax.shard_map(
        on_device,
        mesh=mesh,
        in_specs=(ROWS, P("dp", None), ROWS) + PARAMS * 3,
        out_specs=(ROWS, ROWS) + PARAMS * 4,
        check_vma=False,
    )
```

```python
import math

import jax
import jax.numpy as jnp
from jax import lax
from jax.experimental import pallas as pl
from jax.experimental.pallas import tpu as pltpu
from jax.sharding import PartitionSpec as P

HEAD_DIM = 64
LANES = 128
UTT = 1
LENS = (256, 512, 896)
MOSTS = (200, 400, 781)

EPS = 1e-05
MOMENTUM = 0.5
DECAY = 0.5
RATE_SCALES = (0.02, 0.16, 0.02, 0.02, 0.02, 0.32, 0.16)
NEG_FILL = -1000000000.0
BF16 = jnp.bfloat16
F32 = jnp.float32


def dot(a, b, dims):
    return lax.dot_general(a, b, (dims, ((), ())), preferred_element_type=F32)


CORE_SWAP = [(0, 1), (1, 0), (2, 3), (3, 2)]
HALF_SWAP = [(0, 2), (2, 0), (1, 3), (3, 1)]


def core_swap(value):
    return lax.ppermute(value, "mp", CORE_SWAP)


def half_swap(value):
    return lax.ppermute(value, "mp", HALF_SWAP)


def dp_dims(size):
    dims = []
    while size % 4 == 0:
        dims.append(4)
        size //= 4
    if size > 1:
        dims.append(size)
    return tuple(dims)


class Grid:
    def __init__(self, size):
        self.dims = dp_dims(size)
        self.size = size
        rank = lax.axis_index("dp")
        self.strides = []
        stride = size
        for extent in self.dims:
            stride //= extent
            self.strides.append(stride)
        self.coords = [lax.rem(rank // s, e) for s, e in zip(self.strides, self.dims)]

    def send(self, value, stage, ahead):
        extent, stride = self.dims[stage], self.strides[stage]
        pairs = []
        for source in range(self.size):
            at = source // stride % extent
            pairs.append((source, source + ((at + ahead) % extent - at) * stride))
        return lax.ppermute(value, "dp", pairs)


def put(buffer, piece, axis, index):
    starts = [0] * buffer.ndim
    starts[axis] = index
    return lax.dynamic_update_slice(buffer, jnp.expand_dims(piece, axis), tuple(starts))


def take(buffer, axis, index):
    return lax.dynamic_index_in_dim(buffer, index, axis, keepdims=False)


def gather_half(grid, shard, half_stage):
    rows, columns = shard.shape
    value = shard[None]
    done = 0
    order = list(range(len(grid.dims)))
    for stage in order:
        if done == half_stage:
            value = jnp.concatenate([value, half_swap(value)], 0)
        extent, coord = grid.dims[stage], grid.coords[stage]
        axis = 1 + done
        shape = value.shape[:axis] + (extent,) + value.shape[axis:]
        buffer = put(jnp.zeros(shape, value.dtype), value, axis, coord)
        for ahead in range(1, extent):
            source = lax.rem(coord + extent - ahead, extent)
            buffer = put(buffer, grid.send(value, stage, ahead), axis, source)
        value = buffer
        done += 1
    if done == half_stage:
        other = half_swap(value)
        return value.reshape(-1, columns), other.reshape(-1, columns)
    return value[0].reshape(-1, columns), value[1].reshape(-1, columns)


def scatter_sum(grid, mine, theirs, half_first):
    columns = mine.shape[1]
    shape = grid.dims + (mine.shape[0] // grid.size, columns)
    order = list(range(len(grid.dims)))[::-1]

    def along(value, stage):
        extent, coord = grid.dims[stage], grid.coords[stage]
        axis = value.ndim - 3
        total = take(value, axis, coord).astype(F32)
        for ahead in range(1, extent):
            piece = take(value, axis, lax.rem(coord + ahead, extent))
            total = total + grid.send(piece.astype(BF16), stage, ahead).astype(F32)
        return total

    mine, theirs = mine.reshape(shape), theirs.reshape(shape)
    if half_first:
        value = mine.astype(F32) + half_swap(theirs.astype(BF16)).astype(F32)
        for stage in order:
            value = along(value, stage)
        return value
    first = order[0]
    mine = along(mine, first)
    theirs = along(theirs, first)
    value = mine + half_swap(theirs.astype(BF16)).astype(F32)
    for stage in order[1:]:
        value = along(value, stage)
    return value


def sum_half(grid, pair):
    value = pair[0] + half_swap(pair[1])
    for stage in range(len(grid.dims)):
        total = value
        for ahead in range(1, grid.dims[stage]):
            total = total + grid.send(value, stage, ahead)
        value = total
    return value


def sum_all(grid, value, over_cores):
    for stage in range(len(grid.dims)):
        total = value
        for ahead in range(1, grid.dims[stage]):
            total = total + grid.send(value, stage, ahead)
        value = total
    value = value + half_swap(value)
    if over_cores:
        value = value + core_swap(value)
    return value


def offsets():
    listing, offset = [], 0
    for extent in LENS:
        listing.append(offset)
        offset += UTT * extent
    return listing


def move_plan(rows_local):
    start = offsets()[2]
    count = 2 * rows_local - start
    free = -(-(start + MOSTS[2] - 3 * rows_local) // 16) * 16
    return rows_local - count, free, count


def row_table(rows_local, member, lengths):
    source, free, count = move_plan(rows_local)
    starts = offsets()
    local = jnp.arange(rows_local)
    row = member * rows_local + local
    slot = (row >= starts[1]).astype(jnp.int32) + (row >= starts[2]).astype(jnp.int32)
    place = row - jnp.where(slot == 0, starts[0], jnp.where(slot == 1, starts[1], starts[2]))
    arrived = (member == 3) & (local >= free) & (local < free + count)
    left = (member == 1) & (local >= source)
    place = jnp.where(arrived, local - free, place)
    length = jnp.where(slot == 0, lengths[0, 0], jnp.where(slot == 1, lengths[0, 1], lengths[0, 2]))
    return slot, (place < length) & ~left


def bring(rows, member):
    source, free, count = move_plan(rows.shape[0])
    moved = lax.ppermute(rows[source:], "mp", [(1, 3)])
    placed = lax.dynamic_update_slice(rows, moved, (free, 0))
    return jnp.where(member == 3, placed, rows)


def put_back(rows, moved, member):
    source, free, count = move_plan(rows.shape[0])
    placed = lax.dynamic_update_slice(rows, moved, (source, 0))
    cleared = lax.dynamic_update_slice(rows, jnp.zeros_like(moved), (free, 0))
    return jnp.where(member == 1, placed, jnp.where(member == 3, cleared, rows))


def send_back(rows, member):
    source, free, count = move_plan(rows.shape[0])
    return put_back(rows, lax.ppermute(rows[free : free + count], "mp", [(3, 1)]), member)


CHAIN = 4
X_FIRST = (False, True, True, False)
WHERE = [(0, 0)] + [(step, sign) for step in range(1, CHAIN) for sign in (1, -1)]


class Place:
    def __init__(self):
        self.dp = lax.axis_index("dp")
        self.mp = lax.axis_index("mp")
        self.z = self.dp // 2
        self.x = lax.rem(self.dp, 2)
        self.up = (self.dp + 2, self.mp)
        self.down = (self.dp - 2, self.mp)
        self.across = (self.dp + 1 - 2 * self.x, self.mp)
        self.other = (self.dp, lax.rem(self.mp + 2, 4))
        self.mate = (self.dp, self.mp + 1 - 2 * lax.rem(self.mp, 2))
        self.has_up = self.z < CHAIN - 1
        self.has_down = self.z > 0

    def ring(self, ahead):
        return (lax.rem(self.dp + 2 * ahead, 2 * CHAIN), self.mp)

    def greet(self, peers):
        barrier = pltpu.get_barrier_semaphore()
        for peer in peers:
            pl.semaphore_signal(
                barrier, inc=1, device_id=peer, device_id_type=pl.DeviceIdType.MESH
            )
        pl.semaphore_wait(barrier, len(peers))


def remote(source, target, sends, arrivals, index, device):
    return pltpu.make_async_remote_copy(
        source,
        target,
        sends.at[index],
        arrivals.at[index],
        device_id=device,
        device_id_type=pl.DeviceIdType.MESH,
    )


def gather_kernel(row_plan, *refs):
    shards, (rows_ref, cot_ref, vec_ref) = refs[0:4], refs[4:7]
    fulls, (rows_out, cot_out, vec_out) = refs[7:11], refs[11:14]
    sends, arrivals, side_send, side_arrive, local = refs[14:19]
    here = Place()
    source, free, count = row_plan
    n_rows = rows_ref.shape[0]
    here.greet([here.ring(1), here.ring(2), here.ring(3), here.across, here.other, here.mate,
                (here.dp, 3 - here.mp)])

    def z_of(where):
        step, sign = where
        return here.z - step * sign

    def held(where):
        step, sign = where
        if step == 0:
            return None
        return here.z >= step if sign > 0 else here.z + step < CHAIN

    def maybe(condition, action):
        if condition is None:
            action()
        else:
            pl.when(condition)(action)

    def block(w, where, far, half):
        x = 1 - here.x if far else here.x
        return fulls[w].at[half, z_of(where) * 2 + x]

    def chain(w, where):
        step, sign = where
        origin = shards[w] if step == 0 else block(w, where, False, 0)
        jobs = []
        for way in (1, -1) if step == 0 else (sign,):
            index = step + (0 if way > 0 else 3)
            device = here.up if way > 0 else here.down
            go = here.has_up if way > 0 else here.has_down
            if step < CHAIN - 1:
                jobs.append((go, remote(origin, block_to(w, where), sends.at[w], arrivals.at[w], index, device)))
        return jobs

    def block_to(w, where):
        return fulls[w].at[0, z_of(where) * 2 + here.x]

    def second(w, where):
        origin = shards[w] if where[0] == 0 else block(w, where, False, 0)
        index = 6 + WHERE.index(where)
        if X_FIRST[w]:
            return remote(origin, block(w, where, False, 0), sends.at[w], arrivals.at[w], index, here.across)
        return remote(origin, block(w, where, False, 1), sends.at[w], arrivals.at[w], index, here.other)

    def third(w, where, arrived):
        index = 13 + WHERE.index(where) + (len(WHERE) if arrived else 0)
        if X_FIRST[w]:
            origin = shards[w] if where[0] == 0 and not arrived else block(w, where, arrived, 0)
            return remote(origin, block(w, where, arrived, 1), sends.at[w], arrivals.at[w], index, here.other)
        origin = shards[w] if where[0] == 0 and not arrived else block(w, where, False, int(arrived))
        return remote(origin, block(w, where, False, int(arrived)), sends.at[w], arrivals.at[w], index, here.across)

    def landing(w, where, stage, arrived=False):
        if stage == 2:
            index = 6 + WHERE.index(where)
            target = block(w, where, True, 0) if X_FIRST[w] else block(w, where, False, 1)
            device = here.across if X_FIRST[w] else here.other
        else:
            index = 13 + WHERE.index(where) + (len(WHERE) if arrived else 0)
            if X_FIRST[w]:
                target, device = block(w, where, arrived, 1), here.other
            else:
                target, device = block(w, where, True, int(arrived)), here.across
        return remote(target, target, sends.at[w], arrivals.at[w], index, device)

    def chain_landing(w, where):
        step, sign = where
        index = step - 1 + (0 if sign > 0 else 3)
        target = block(w, where, False, 0)
        return remote(target, target, sends.at[w], arrivals.at[w], index, here.down if sign > 0 else here.up)

    order = (0, 1, 3, 2)
    by_step = [[p for p in WHERE if p[0] == step] for step in range(CHAIN)]

    low, high = pl.ds(0, free), pl.ds(free + count, n_rows - free - count)
    middle, tail = pl.ds(free, count), pl.ds(source, count)
    locals_ = [(None, pltpu.make_async_copy(shards[w], fulls[w].at[0, here.dp], local.at[w])) for w in order]
    not_last, second_core = here.mp != 3, here.mp == 1
    for n, (given, taken) in enumerate(((rows_ref, rows_out.at[0]), (cot_ref, cot_out))):
        for m, part in enumerate((low, high, middle)):
            copy = pltpu.make_async_copy(given.at[part], taken.at[part], local.at[4 + 3 * n + m])
            locals_.append((not_last if m == 2 else None, copy))
    for condition, copy in locals_:
        maybe(condition, copy.start)

    def to_mate(m, part):
        return remote(rows_ref.at[part], rows_out.at[1, part], side_send, side_arrive, m, here.mate)

    side = [(None, to_mate(0, low)), (None, to_mate(1, high)), (not_last, to_mate(2, middle))]
    side.append((None, remote(vec_ref, vec_out, side_send, side_arrive, 3, here.other)))
    moved = [
        remote(rows_ref.at[tail], rows_out.at[0, middle], side_send, side_arrive, 4, here.other),
        remote(cot_ref.at[tail], cot_out.at[middle], side_send, side_arrive, 5, here.other),
        remote(rows_ref.at[tail], rows_out.at[1, middle], side_send, side_arrive, 6, (here.dp, 3 - here.mp)),
    ]
    side += [(second_core, copy) for copy in moved]

    started = []

    def start(condition, copy):
        maybe(condition, copy.start)
        started.append((condition, copy))

    for condition, copy in side:
        start(condition, copy)
    for step in range(CHAIN):
        for where in by_step[step]:
            for w in order:
                if step > 0:
                    maybe(held(where), chain_landing(w, where).wait_recv)
                for go, copy in chain(w, where):
                    both = go if held(where) is None else jnp.logical_and(go, held(where))
                    start(both, copy)
                start(held(where), second(w, where))
                start(held(where), third(w, where, False))
        for where in by_step[step - 1] if step > 0 else ():
            for w in order:
                maybe(held(where), landing(w, where, 2).wait_recv)
                start(held(where), third(w, where, True))
    for where in by_step[CHAIN - 1]:
        for w in order:
            maybe(held(where), landing(w, where, 2).wait_recv)
            start(held(where), third(w, where, True))
    for where in WHERE:
        for w in order:
            for arrived in (False, True):
                maybe(held(where), landing(w, where, 3, arrived).wait_recv)
    to_mate(0, low).wait_recv()
    to_mate(1, high).wait_recv()
    pl.when(here.mp != 2)(to_mate(2, middle).wait_recv)
    side[3][1].wait_recv()
    pl.when(here.mp == 3)(moved[0].wait_recv)
    pl.when(here.mp == 3)(moved[1].wait_recv)
    pl.when(here.mp == 2)(moved[2].wait_recv)
    for condition, copy in started:
        maybe(condition, copy.wait_send)
    for condition, copy in locals_:
        maybe(condition, copy.wait)


def gather_all(shards, rows, cotangent, vectors):
    rows_local, width = rows.shape
    vmem, anywhere = pl.BlockSpec(memory_space=pltpu.VMEM), pl.BlockSpec(memory_space=pl.ANY)
    shapes = [jax.ShapeDtypeStruct((2, 2 * CHAIN) + s.shape, s.dtype) for s in shards]
    shapes += [
        jax.ShapeDtypeStruct((2, rows_local, width), rows.dtype),
        jax.ShapeDtypeStruct((rows_local, width), rows.dtype),
        jax.ShapeDtypeStruct(vectors.shape, vectors.dtype),
    ]
    plan = move_plan(rows_local)
    return pl.pallas_call(
        lambda *refs: gather_kernel(plan, *refs),
        out_shape=shapes,
        in_specs=[vmem] * 7,
        out_specs=[anywhere] * 6 + [vmem],
        scratch_shapes=[
            pltpu.SemaphoreType.DMA((4, 27)),
            pltpu.SemaphoreType.DMA((4, 27)),
            pltpu.SemaphoreType.DMA((7,)),
            pltpu.SemaphoreType.DMA((7,)),
            pltpu.SemaphoreType.DMA((10,)),
        ],
        compiler_params=pltpu.CompilerParams(
            collective_id=0, has_side_effects=True, vmem_limit_bytes=16 * 2**20
        ),
        name="gather_all",
    )(*shards, rows, cotangent, vectors)


def finish_kernel(block, *refs):
    attn_ref, grad_ref, q_ref, k_ref, v_ref, rows_ref, weight_ref = refs[0:7]
    out_near, out_far, up_ref, down_ref, vec_ref, out_edge, branch_ref = refs[7:14]
    sums, (vec_out, out_back, grad_back, grad_out) = refs[14:18], refs[18:22]
    firsts, seconds, rises, falls, finals = [refs[22 + 4 * i : 26 + 4 * i] for i in range(5)]
    (g_ref, dq_ref, dk_ref, dv_ref, parts_ref, g_qkv, rows_t, to_mate, from_mate, grad_edge) = refs[42:52]
    vec_in, sends, arrivals, side_send, side_arrive = refs[52:57]
    mine = (g_qkv.at[0], out_near, up_ref.at[0], down_ref.at[0])
    theirs = (g_qkv.at[1], out_far, up_ref.at[1], down_ref.at[1])
    n_rows = branch_ref.shape[0]
    _, free, count = move_plan(n_rows)
    here = Place()
    here.greet([here.ring(1), here.ring(2), here.ring(3), here.across, here.other, here.mate])
    early, late = (2, 3, 1), (0,)
    targets = (3, 0, 2, 1)
    far = 1 - here.x
    started = []

    def start(copy, condition=None):
        if condition is None:
            copy.start()
        else:
            pl.when(condition)(copy.start)
        started.append((condition, copy))
        return copy

    def add(target, more):
        target[...] = (target[...].astype(F32) + more[...].astype(F32)).astype(BF16)

    first_jobs, second_jobs = {}, {}

    def first_stage(weights):
        for target in targets:
            for w in weights:
                for part in (0, 1):
                    if X_FIRST[w]:
                        origin, device = theirs[w].at[target, part], here.other
                    else:
                        origin, device = (mine, theirs)[part][w].at[target, far], here.across
                    landed = firsts[w].at[target, part]
                    first_jobs[w, target, part] = start(
                        remote(origin, landed, sends.at[w], arrivals.at[w], 2 * target + part, device)
                    )

    def second_stage(weights):
        for target in targets:
            for w in weights:
                for part in (0, 1):
                    first_jobs[w, target, part].wait_recv()
                    if X_FIRST[w]:
                        add(firsts[w].at[target, part], mine[w].at[target, part])
                    else:
                        add(firsts[w].at[target, part], (mine, theirs)[part][w].at[target, here.x])
                if X_FIRST[w]:
                    origin, device = firsts[w].at[target, far], here.across
                else:
                    origin, device = firsts[w].at[target, 1], here.other
                landed = seconds[w].at[target]
                second_jobs[w, target] = start(
                    remote(origin, landed, sends.at[w], arrivals.at[w], 8 + target, device)
                )

    def lane(w, target, up):
        at = target - 1 if up else target
        return (rises if up else falls)[w].at[at], (12 if up else 15) + at

    def receive(w, target, up):
        slot, index = lane(w, target, up)
        device = here.down if up else here.up
        return remote(slot, slot, sends.at[w], arrivals.at[w], index, device)

    def pass_on(w, target, up):
        slot, index = lane(w, target, up)
        device = here.up if up else here.down
        return remote(seconds[w].at[target], slot, sends.at[w], arrivals.at[w], index, device)

    def take_in(w, target, up):
        receive(w, target, up).wait_recv()
        add(seconds[w].at[target], lane(w, target, up)[0])

    def chain(weights):
        for target in targets:
            for w in weights:
                second_jobs[w, target].wait_recv()
                kept = firsts[w].at[target, here.x] if X_FIRST[w] else firsts[w].at[target, 0]
                add(seconds[w].at[target], kept)
                for up in (True, False):
                    if target == (0 if up else CHAIN - 1):
                        continue
                    before = here.z < target if up else here.z > target
                    inner = here.has_down if up else here.has_up
                    pl.when(jnp.logical_and(before, inner))(
                        lambda w=w, target=target, up=up: take_in(w, target, up)
                    )
                    start(pass_on(w, target, up), before)

    def finish(w, target, up):
        receive(w, target, up).wait_recv()
        finals[w][...] += lane(w, target, up)[0][...].astype(F32)

    def settle_sums(weights):
        for w in weights:
            finals[w][...] = seconds[w][here.z].astype(F32)
            for up in (True, False):
                for target in range(CHAIN):
                    if target != (0 if up else CHAIN - 1):
                        pl.when(here.z == target)(
                            lambda w=w, target=target, up=up: finish(w, target, up)
                        )

    first_stage(early)
    edges = [start(remote(out_edge, out_back, side_send, side_arrive, 6, here.other), here.mp == 3)]

    attend_back_body(
        block, 3, attn_ref, grad_ref, q_ref, k_ref, v_ref, (parts_ref.at[0], parts_ref.at[1]),
        g_ref, dq_ref, dk_ref, dv_ref,
    )
    rows_t[...] = rows_ref[...].T
    d_rows = jnp.zeros(rows_ref.shape, F32)
    vec_out[...] = vec_ref[...]
    depth, columns = g_qkv.shape[3], g_qkv.shape[4]
    for half in (0, 1):
        part = parts_ref[half]
        d_rows = d_rows + dot(part, weight_ref[half], ((1,), (1,)))
        grads = dot(rows_t[...], part, ((1,), (0,))).astype(BF16)
        for at in range(2 * CHAIN):
            g_qkv[half, at // 2, at % 2] = grads[at * depth : (at + 1) * depth, :]
        row = 7 + 2 * half
        vec_out[row : row + 1, 0:columns] = jnp.sum(part.astype(F32), axis=0, keepdims=True)
    to_mate[...] = d_rows[n_rows:, :].astype(BF16)
    grad_out[...] = d_rows[0:n_rows, :] + branch_ref[...]
    mate_job = start(remote(to_mate, from_mate, side_send, side_arrive, 8, here.mate))

    def vec_send(index, device):
        copy = remote(vec_out, vec_in.at[index], side_send, side_arrive, index, device)
        copy.start()
        return copy

    sent = vec_send(0, here.other)
    second_stage(early)
    first_stage(late)
    mate_job.wait_recv()
    grad_out[...] = grad_out[...] + from_mate[...].astype(F32)
    grad_edge[...] = grad_out[free : free + count, :]
    edges.append(start(remote(grad_edge, grad_back, side_send, side_arrive, 7, here.other), here.mp == 3))
    sent.wait()
    vec_out[0:6] = vec_out[0:6] + vec_in[0, 0:6]
    vec_out[6:8] = vec_out[6:8] + vec_in[0, 8:10]
    sent = vec_send(1, here.across)
    chain(early)
    second_stage(late)
    sent.wait()
    vec_out[...] = vec_out[...] + vec_in[1]
    ring = [vec_send(1 + ahead, here.ring(ahead)) for ahead in (1, 2, 3)]
    settle_sums(early)
    chain(late)
    for copy in ring:
        copy.wait()
    slots = [vec_out[...], vec_in[2], vec_in[3], vec_in[4]]
    total = jnp.zeros_like(slots[0])
    for at in range(CHAIN):
        for behind in range(CHAIN):
            same = lax.rem(here.z + CHAIN - behind, CHAIN) == at
            total = total + jnp.where(same, slots[behind], 0.0)
    vec_out[...] = total
    sent = vec_send(5, here.mate)
    for w in (2, 3):
        sums[w][...] = finals[w][...]
    value = finals[1][...]
    pad = jnp.zeros((LANES - value.shape[0], value.shape[1]), F32)
    sums[1][...] = jnp.concatenate([value, pad], 0).T[:, : value.shape[0]]
    settle_sums(late)
    for c in range(sums[0].shape[0]):
        sums[0][c] = finals[0][:, c * sums[0].shape[2] : (c + 1) * sums[0].shape[2]]

    sent.wait()
    vec_out[0:6] = vec_out[0:6] + vec_in[5, 0:6]
    for copy in edges:
        pl.when(here.mp == 1)(copy.wait_recv)
    for condition, copy in started:
        if condition is None:
            copy.wait_send()
        else:
            pl.when(condition)(copy.wait_send)


def finish_all(attn, grad, query, keys, values, rows, weight, out, up, down, vectors, out_edge, branch, block):
    heads, n_all = query.shape[:2]
    width = rows.shape[1]
    depth = width // (2 * CHAIN)
    out = [g.reshape(CHAIN, 2, depth, -1) for g in out]
    up, down = [g.reshape(2, CHAIN, 2, depth, -1) for g in (up, down)]
    columns = weight.shape[2]
    widths = [columns, out[0].shape[-1], up.shape[-1], down.shape[-1]]
    vmem = pl.BlockSpec(memory_space=pltpu.VMEM)
    shapes = [(3, depth, columns // 3), (widths[1], depth), (depth, widths[2]), (depth, widths[3])]
    shapes = [jax.ShapeDtypeStruct(shape, F32) for shape in shapes]
    shapes += [
        jax.ShapeDtypeStruct(vectors.shape, F32),
        jax.ShapeDtypeStruct(out_edge.shape, BF16),
        jax.ShapeDtypeStruct(out_edge.shape, F32),
        jax.ShapeDtypeStruct(branch.shape, F32),
    ]
    scratch = [pltpu.VMEM((CHAIN, 2, depth, n), BF16) for n in widths]
    scratch += [pltpu.VMEM((CHAIN, depth, n), BF16) for n in widths]
    scratch += [pltpu.VMEM((CHAIN - 1, depth, n), BF16) for n in widths] * 2
    scratch += [pltpu.VMEM((depth, n), F32) for n in widths]
    scratch += [pltpu.VMEM(query.shape, BF16)] * 2 + [pltpu.VMEM(query.shape, F32)] * 2
    scratch += [
        pltpu.VMEM((2, n_all, columns), BF16),
        pltpu.VMEM((2, CHAIN, 2, depth, columns), BF16),
        pltpu.VMEM((width, n_all), BF16),
        pltpu.VMEM(branch.shape, BF16),
        pltpu.VMEM(branch.shape, BF16),
        pltpu.VMEM(out_edge.shape, F32),
        pltpu.VMEM((6,) + vectors.shape, F32),
        pltpu.SemaphoreType.DMA((4, 18)),
        pltpu.SemaphoreType.DMA((4, 18)),
        pltpu.SemaphoreType.DMA((9,)),
        pltpu.SemaphoreType.DMA((9,)),
    ]
    return pl.pallas_call(
        lambda *refs: finish_kernel(block, *refs),
        out_shape=shapes,
        in_specs=[vmem] * 14,
        out_specs=[vmem] * 8,
        scratch_shapes=scratch,
        compiler_params=pltpu.CompilerParams(
            collective_id=1, has_side_effects=True, vmem_limit_bytes=62 * 2**20
        ),
        name="finish_all",
    )(attn, grad, query, keys, values, rows, weight, *out, up, down, vectors, out_edge, branch)


def split_parts(value, count):
    parts = []
    for _ in range(count):
        part = value.astype(BF16).astype(F32)
        parts.append(part)
        value = value - part
    return parts


def lane_fill(base, parts, first):
    lane = lax.broadcasted_iota(jnp.int32, base.shape, 1)
    for index, part in enumerate(parts):
        base = jnp.where(lane == first + index, part, base)
    return base


def head_columns(head, part, per_half):
    half, index = divmod(head, per_half)
    at = (part * per_half + index) * HEAD_DIM
    return half, slice(at, at + HEAD_DIM)


def attend_kernel(block, near_ref, far_ref, slot_ref, mask_ref, attn_ref, q_ref, k_ref, v_ref, out_ref):
    acts = (near_ref, far_ref)
    heads, rows = q_ref.shape[:2]
    ones = lane_fill(jnp.zeros((rows, HEAD_DIM), F32), (1.0, 1.0), 0).astype(BF16)
    for head in range(heads):
        for part, (ref, more) in enumerate(((q_ref, slot_ref), (k_ref, mask_ref), (v_ref, None))):
            half, columns = head_columns(head, part, heads // 2)
            piece = acts[half][:, columns]
            if part == 0:
                piece = (piece.astype(F32) * HEAD_DIM ** (-0.5)).astype(BF16)
            ref[head, :, 0:HEAD_DIM] = piece
            ref[head, :, HEAD_DIM : 2 * HEAD_DIM] = ones if more is None else more[...]

    def step(index, carry):
        head, at = index // (rows // block), lax.rem(index, rows // block)
        span = pl.ds(pl.multiple_of(at * block, 16), block)
        query = q_ref[head, span, :]
        scores = dot(query, k_ref[head], ((1,), (1,)))
        peak = jnp.max(scores, axis=-1, keepdims=True)
        weights = jnp.exp(scores - peak)
        both = dot(weights.astype(BF16), v_ref[head], ((1,), (0,)))
        total = both[:, HEAD_DIM : HEAD_DIM + 1]
        out_ref[head, span, :] = (both * (1.0 / total)).astype(BF16)
        log_sum = peak + jnp.log(total)
        parts = [-p for p in split_parts(log_sum, 3)]
        q_ref[head, span, :] = lane_fill(query.astype(F32), parts, HEAD_DIM + 3).astype(BF16)
        return carry

    lax.fori_loop(0, heads * (rows // block), step, 0, unroll=6)
    for head in range(heads):
        attn_ref[:, head * HEAD_DIM : (head + 1) * HEAD_DIM] = out_ref[head, :, 0:HEAD_DIM]


def attend_back_body(block, unroll, attn_ref, grad_ref, q_ref, k_ref, v_ref, outs, g_ref, dq_ref, dk_ref, dv_ref):
    heads, rows = q_ref.shape[:2]
    for head in range(heads):
        columns = slice(head * HEAD_DIM, (head + 1) * HEAD_DIM)
        grad = grad_ref[:, columns]
        mean = jnp.sum(grad.astype(F32) * attn_ref[:, columns].astype(F32), axis=-1, keepdims=True)
        parts = [-p for p in split_parts(mean, 2)]
        g_ref[head, :, 0:HEAD_DIM] = grad
        g_ref[head, :, HEAD_DIM : 2 * HEAD_DIM] = lane_fill(
            jnp.zeros((rows, HEAD_DIM), F32), parts, 0
        ).astype(BF16)
    dk_ref[...] = jnp.zeros_like(dk_ref)
    dv_ref[...] = jnp.zeros_like(dv_ref)

    def step(index, carry):
        head, at = index // (rows // block), lax.rem(index, rows // block)
        span = pl.ds(pl.multiple_of(at * block, 16), block)
        query, grad = q_ref[head, span, :], g_ref[head, span, :]
        keys = k_ref[head]
        probs = jnp.exp(dot(keys, query, ((1,), (1,))))
        change = (probs * dot(v_ref[head], grad, ((1,), (1,)))).astype(BF16)
        dv_ref[head] += dot(probs.astype(BF16), grad, ((1,), (0,)))
        dk_ref[head] += dot(change, query, ((1,), (0,)))
        dq_ref[head, span, :] = (dot(change, keys, ((0,), (0,))) * HEAD_DIM ** (-0.5)).astype(BF16)
        return carry

    lax.fori_loop(0, heads * (rows // block), step, 0, unroll=unroll)
    for head in range(heads):
        for part, ref in enumerate((dq_ref, dk_ref, dv_ref)):
            half, columns = head_columns(head, part, heads // 2)
            outs[half][:, columns] = ref[head, :, 0:HEAD_DIM].astype(BF16)


def attend_back_kernel(block, attn_ref, grad_ref, q_ref, k_ref, v_ref, near_ref, far_ref, *scratch):
    attend_back_body(
        block, 1, attn_ref, grad_ref, q_ref, k_ref, v_ref, (near_ref, far_ref), *scratch
    )


def attend_cost(heads, rows, products):
    return pl.CostEstimate(
        flops=2 * products * heads * rows * rows * 128,
        bytes_accessed=8 * heads * rows * 128,
        transcendentals=heads * rows * rows,
    )


def attend(near, far, slots, masks, block):
    rows = near.shape[0]
    heads = 2 * near.shape[1] // (3 * HEAD_DIM)
    vmem = pl.BlockSpec(memory_space=pltpu.VMEM)
    wide = jax.ShapeDtypeStruct((heads, rows, 2 * HEAD_DIM), BF16)
    return pl.pallas_call(
        lambda *refs: attend_kernel(block, *refs),
        out_shape=[jax.ShapeDtypeStruct((rows, heads * HEAD_DIM), BF16), wide, wide, wide],
        in_specs=[vmem] * 4,
        out_specs=[vmem] * 4,
        scratch_shapes=[pltpu.VMEM(wide.shape, BF16)],
        compiler_params=pltpu.CompilerParams(vmem_limit_bytes=40 * 2**20),
        cost_estimate=attend_cost(heads, rows, 2),
        name="attend",
    )(near, far, slots, masks)


def attend_back(attn, grad, query, keys, values, block):
    heads, rows = query.shape[:2]
    vmem = pl.BlockSpec(memory_space=pltpu.VMEM)
    out = jax.ShapeDtypeStruct((rows, 3 * heads // 2 * HEAD_DIM), BF16)
    return pl.pallas_call(
        lambda *refs: attend_back_kernel(block, *refs),
        out_shape=[out, out],
        in_specs=[vmem] * 5,
        out_specs=[vmem] * 2,
        scratch_shapes=[pltpu.VMEM(query.shape, BF16)] * 2 + [pltpu.VMEM(query.shape, F32)] * 2,
        compiler_params=pltpu.CompilerParams(vmem_limit_bytes=40 * 2**20),
        cost_estimate=attend_cost(heads, rows, 5),
        name="attend_back",
    )(attn, grad, query, keys, values)


def norm_stats(values):
    mean = jnp.mean(values, axis=-1, keepdims=True)
    center = values - mean
    spread = jnp.mean(center * center, axis=-1, keepdims=True)
    inverse = lax.rsqrt(spread + EPS)
    return center * inverse, inverse


def norm_back(grad, unit, inverse, gain):
    scaled = grad * gain
    return inverse * (
        scaled
        - jnp.mean(scaled, axis=-1, keepdims=True)
        - unit * jnp.mean(scaled * unit, axis=-1, keepdims=True)
    )


def feed_back_kernel(n_rows, first_ref, grad_ref, up_ref, down_ref, near_hidden, far_hidden,
                     near_slope, far_slope, g_up_ref, g_down_ref, g_bias_ref, own_ref, mate_ref, total_ref, first_t, grad_t):
    step = pl.program_id(0)

    @pl.when(step == 0)
    def _():
        first_t[...] = first_ref[...].T
        grad_t[...] = grad_ref[...].T
        total_ref[...] = jnp.zeros_like(total_ref)

    near = step < pl.num_programs(0) // 2
    hidden = jnp.where(near, near_hidden[...], far_hidden[...])
    slope = jnp.where(near, near_slope[...], far_slope[...])
    d_hidden = dot(grad_ref[...], down_ref[0], ((1,), (0,)))
    d_pre = (d_hidden * slope.astype(F32)).astype(BF16)
    total_ref[...] += dot(d_pre, up_ref[0], ((1,), (1,)))
    g_bias_ref[0] = jnp.sum(d_pre.astype(F32), axis=0, keepdims=True)
    g_up_ref[0] = dot(first_t[...], d_pre, ((1,), (0,))).astype(BF16)
    g_down_ref[0] = dot(grad_t[...], hidden, ((1,), (0,))).astype(BF16)

    @pl.when(step == pl.num_programs(0) - 1)
    def _():
        own_ref[...] = total_ref[0:n_rows, :]
        mate_ref[...] = total_ref[n_rows:, :].astype(BF16)


def feed_specs(rows, width, units, tile):
    blocks = units // tile
    whole = pl.BlockSpec((rows, width), lambda i: (0, 0))
    half = pl.BlockSpec((rows // 2, width), lambda i: (0, 0))

    def split(count):
        return pl.BlockSpec((1, count, tile), lambda i: (i // blocks, 0, lax.rem(i, blocks)))

    halves = [jax.ShapeDtypeStruct((rows // 2, width), kind) for kind in (F32, BF16)]
    return (2 * blocks,), whole, half, split, halves


def feed_back(first, grad, up, down, hiddens, slopes, tile):
    (rows, width), units = first.shape, up.shape[2]
    grid, whole, half, split, halves = feed_specs(rows, width, units, tile)
    last = units // tile - 1
    near = pl.BlockSpec((rows, tile), lambda i: (0, jnp.minimum(i, last)))
    far = pl.BlockSpec((rows, tile), lambda i: (0, jnp.maximum(i - last - 1, 0)))
    wide = jax.ShapeDtypeStruct((2, width, units), BF16)
    return pl.pallas_call(
        lambda *refs: feed_back_kernel(rows // 2, *refs),
        grid=grid,
        out_shape=[wide, wide, jax.ShapeDtypeStruct((2, 1, units), F32)] + halves,
        in_specs=[whole, whole, split(width), split(width), near, far, near, far],
        out_specs=[split(width), split(width), split(1), half, half],
        scratch_shapes=[
            pltpu.VMEM((rows, width), F32),
            pltpu.VMEM((width, rows), BF16),
            pltpu.VMEM((width, rows), BF16),
        ],
        compiler_params=pltpu.CompilerParams(vmem_limit_bytes=48 * 2**20),
        cost_estimate=pl.CostEstimate(
            flops=16 * rows * width * units,
            bytes_accessed=16 * width * units + 8 * rows * units,
            transcendentals=0,
        ),
        name="feed_back",
    )(first, grad, up, down, *hiddens, *slopes)


def update_one(rate, weight, grad, moment, average):
    moment_next = MOMENTUM * moment + grad
    weight_next = weight - rate * (grad + MOMENTUM * moment_next)
    return (weight_next, moment_next, DECAY * average + (1.0 - DECAY) * weight_next)


def on_device(
    tokens,
    lengths,
    cotangent,
    qkv_weight,
    out_weight,
    up_weight,
    down_weight,
    head_bias,
    up_bias,
    norm_vectors,
    qkv_moment,
    out_moment,
    up_moment,
    down_moment,
    head_bias_moment,
    up_bias_moment,
    norm_moment,
    qkv_average,
    out_average,
    up_average,
    down_average,
    head_bias_average,
    up_bias_average,
    norm_average,
):
    grid = Grid(lax.axis_size("dp"))
    member = lax.axis_index("mp")
    mate = member + 1 - 2 * lax.rem(member, 2)
    rows_local, width = tokens.shape
    head_width = qkv_weight.shape[2]
    stages = len(grid.dims)
    units = up_weight.shape[1]

    qkv_shard = jnp.transpose(qkv_weight, (1, 0, 2)).reshape(-1, 3 * head_width).astype(BF16)
    shards = (
        qkv_shard,
        out_weight.astype(BF16).T,
        up_weight.astype(BF16),
        down_weight.astype(BF16).T,
    )
    kernels = grid.size == 2 * CHAIN and units == width
    if kernels:
        flat = jnp.pad(head_bias.reshape(-1), (0, width - 2 * head_width))
        vectors = jnp.zeros((8, width), F32).at[0].set(up_bias).at[1].set(flat)
        *fulls, rows_both, own_cotangent, far_vectors = gather_all(
            shards, tokens, cotangent, vectors
        )
        qkv_pair, out_pair, up_pair, down_pair = [full.reshape(2, width, -1) for full in fulls]
        far_bias = far_vectors[1, : 2 * head_width].reshape(2, head_width)
        bias_pair, up_bias_pair = (head_bias, far_bias), (up_bias, far_vectors[0])
        tokens_all = rows_both.reshape(2 * rows_local, width)
        own_tokens = rows_both[0]
    else:
        qkv_pair = gather_half(grid, shards[0], stages)
        out_pair = gather_half(grid, shards[1], stages - 1)
        up_pair = jnp.stack(gather_half(grid, shards[2], stages))
        down_pair = jnp.stack(gather_half(grid, shards[3], stages - 1))
        bias_pair = (head_bias, half_swap(head_bias))
        up_bias_pair = (up_bias, half_swap(up_bias))
        own_tokens = bring(tokens, member)
        own_cotangent = bring(cotangent, member)
        tokens_all = jnp.concatenate([own_tokens, core_swap(own_tokens)], 0)

    slot_own, valid_own = row_table(rows_local, member, lengths)
    slot_mate, valid_mate = row_table(rows_local, mate, lengths)
    slot = jnp.concatenate([slot_own, slot_mate])
    frame = jnp.concatenate([valid_own, valid_mate])
    column = jnp.arange(HEAD_DIM)[None, :]
    here_slot = slot[:, None] == column
    slot_lanes = here_slot.astype(BF16)
    mask_lanes = jnp.where(
        column < len(LENS),
        jnp.where(here_slot & frame[:, None], 0.0, NEG_FILL),
        jnp.where(column < len(LENS) + 3, 1.0, 0.0),
    ).astype(BF16)
    live = valid_own[:, None]

    def share(rows):
        return jnp.concatenate([rows, core_swap(rows)], 0)

    def settle(partial):
        return partial[:rows_local] + core_swap(partial[rows_local:].astype(BF16)).astype(F32)

    block = 2 * rows_local
    parts = []
    for weight, bias in zip(qkv_pair, bias_pair):
        rows_bias = jnp.concatenate([bias[0], jnp.zeros_like(bias[0]), bias[1]])
        parts.append((dot(tokens_all, weight, ((1,), (0,))) + rows_bias).astype(BF16))
    attn, query, keys, values = attend(*parts, slot_lanes, mask_lanes, block)
    out_both = jnp.concatenate([out_pair[0], out_pair[1]], 1)
    branch = settle(dot(attn, out_both, ((1,), (1,))))
    unit_one, inverse_one = norm_stats(branch + norm_vectors[0] + own_tokens.astype(F32))
    first = unit_one * norm_vectors[2] + norm_vectors[3]
    first_all = share(first.astype(BF16))

    hiddens, slopes = [], []
    for at in (0, 1):
        pre = dot(first_all, up_pair[at], ((1,), (0,))) + up_bias_pair[at]
        phi = 0.5 * (1.0 + lax.erf(pre * (0.5**0.5)))
        density = jnp.exp(-0.5 * pre * pre) * (1.0 / math.sqrt(2.0 * math.pi))
        hiddens.append((pre * phi).astype(BF16))
        slopes.append((phi + pre * density).astype(BF16))
    ffn = settle(
        dot(hiddens[0], down_pair[0], ((1,), (1,))) + dot(hiddens[1], down_pair[1], ((1,), (1,)))
    )
    unit_two, inverse_two = norm_stats(ffn + norm_vectors[1] + first)
    second = unit_two * norm_vectors[4] + norm_vectors[5]
    layer_out = jnp.where(live, second, 0.0).astype(BF16)

    grad_two = jnp.where(live, own_cotangent.astype(F32), 0.0)
    d_second = norm_back(grad_two, unit_two, inverse_two, norm_vectors[4])
    d_ffn_all = share(d_second.astype(BF16))
    tile = 2 * LANES if units % (2 * LANES) == 0 else units
    grad_up, grad_down, grad_up_bias, d_first_own, d_first_mate = feed_back(
        first_all, d_ffn_all, up_pair, down_pair, hiddens, slopes, tile
    )
    grad_up_bias = grad_up_bias[:, 0, :]
    d_first = d_second + (d_first_own + core_swap(d_first_mate).astype(F32))

    d_branch = norm_back(d_first, unit_one, inverse_one, norm_vectors[2])
    d_branch_all = share(d_branch.astype(BF16))
    d_attn = dot(d_branch_all, out_both, ((1,), (0,))).astype(BF16)
    grad_out = [
        dot(d_branch_all, attn[:, at : at + head_width], ((0,), (0,))).astype(BF16)
        for at in (0, head_width)
    ]
    norm_part = jnp.stack(
        [
            jnp.sum(d_branch, axis=0),
            jnp.sum(d_second, axis=0),
            jnp.sum(d_first * unit_one, axis=0),
            jnp.sum(d_first, axis=0),
            jnp.sum(grad_two * unit_two, axis=0),
            jnp.sum(grad_two, axis=0),
        ]
    )
    if kernels:
        blank = jnp.zeros((1, width), F32)
        vectors = jnp.concatenate(
            [norm_part, grad_up_bias[:1], blank, grad_up_bias[1:], jnp.zeros((7, width), F32)]
        )
        source, free, count = move_plan(rows_local)
        *sums, vectors, out_back, grad_back, tokens_grad = finish_all(
            attn,
            d_attn,
            query,
            keys,
            values,
            tokens_all,
            qkv_pair,
            grad_out,
            grad_up,
            grad_down,
            vectors,
            layer_out[free : free + count],
            d_branch,
            block,
        )
        sum_qkv, sum_out, sum_up, sum_down = sums
        sum_down = sum_down.T
        layer_out = put_back(layer_out, out_back, member)
        tokens_grad = put_back(tokens_grad, grad_back, member)
        sum_norm, sum_up_bias, sum_bias = vectors[:6], vectors[6], vectors[7]
        sum_bias = sum_bias[: 3 * head_width]
    else:
        d_parts = attend_back(attn, d_attn, query, keys, values, block)
        grad_qkv = [dot(tokens_all, part, ((0,), (0,))).astype(BF16) for part in d_parts]
        grad_bias = [jnp.sum(part, axis=0, dtype=F32) for part in d_parts]
        d_tokens = settle(
            dot(d_parts[0], qkv_pair[0], ((1,), (1,))) + dot(d_parts[1], qkv_pair[1], ((1,), (1,)))
        )
        tokens_grad = d_tokens + d_branch
        sum_qkv = scatter_sum(grid, *grad_qkv, True)
        sum_out = scatter_sum(grid, *grad_out, True)
        sum_up = scatter_sum(grid, *grad_up, False)
        sum_down = scatter_sum(grid, *grad_down, True)
        layer_out = send_back(layer_out, member)
        tokens_grad = send_back(tokens_grad, member)
        sum_norm = sum_all(grid, norm_part, True)
        sum_up_bias = sum_half(grid, grad_up_bias)
        sum_bias = sum_half(grid, grad_bias)
        sum_qkv = jnp.transpose(sum_qkv.reshape(-1, 3, head_width), (1, 0, 2))
        sum_out, sum_down = sum_out.T, sum_down.T
    sum_head_bias = jnp.stack([sum_bias[:head_width], sum_bias[2 * head_width :]])

    divisor = math.sqrt(1000.0 * grid.size * UTT)
    params = (qkv_weight, out_weight, up_weight, down_weight, head_bias, up_bias, norm_vectors)
    grads = (sum_qkv, sum_out, sum_up, sum_down, sum_head_bias, sum_up_bias, sum_norm)
    moments = (
        qkv_moment,
        out_moment,
        up_moment,
        down_moment,
        head_bias_moment,
        up_bias_moment,
        norm_moment,
    )
    averages = (
        qkv_average,
        out_average,
        up_average,
        down_average,
        head_bias_average,
        up_bias_average,
        norm_average,
    )
    nexts, moment_nexts, average_nexts = ([], [], [])
    for weight, grad, moment, average, scale_one in zip(
        params, grads, moments, averages, RATE_SCALES
    ):
        weight_next, moment_next, average_next = update_one(
            scale_one / divisor, weight, grad, moment, average
        )
        nexts.append(weight_next)
        moment_nexts.append(moment_next)
        average_nexts.append(average_next)
    return (layer_out, tokens_grad, *grads, *nexts, *moment_nexts, *average_nexts)


ROWS = P(("dp", "mp"), None)
PARAMS = (
    P(None, "dp", "mp"),
    P("mp", "dp"),
    P("dp", "mp"),
    P("mp", "dp"),
    P(None, "mp"),
    P("mp"),
    P(),
)


def solution(mesh):
    return jax.shard_map(
        on_device,
        mesh=mesh,
        in_specs=(ROWS, P("dp", None), ROWS) + PARAMS * 3,
        out_specs=(ROWS, ROWS) + PARAMS * 4,
        check_vma=False,
    )
```

```python
import math

import jax
import jax.numpy as jnp
from jax import lax
from jax.experimental import pallas as pl
from jax.experimental.pallas import tpu as pltpu
from jax.sharding import PartitionSpec as P

HEAD_DIM = 64
LANES = 128
UTT = 1
LENS = (256, 512, 896)
MOSTS = (200, 400, 781)

EPS = 1e-05
MOMENTUM = 0.5
DECAY = 0.5
RATE_SCALES = (0.02, 0.16, 0.02, 0.02, 0.02, 0.32, 0.16)
NEG_FILL = -1000000000.0
BF16 = jnp.bfloat16
F32 = jnp.float32


def dot(a, b, dims):
    return lax.dot_general(a, b, (dims, ((), ())), preferred_element_type=F32)


CORE_SWAP = [(0, 1), (1, 0), (2, 3), (3, 2)]
HALF_SWAP = [(0, 2), (2, 0), (1, 3), (3, 1)]


def core_swap(value):
    return lax.ppermute(value, "mp", CORE_SWAP)


def half_swap(value):
    return lax.ppermute(value, "mp", HALF_SWAP)


def dp_dims(size):
    dims = []
    while size % 4 == 0:
        dims.append(4)
        size //= 4
    if size > 1:
        dims.append(size)
    return tuple(dims)


class Grid:
    def __init__(self, size):
        self.dims = dp_dims(size)
        self.size = size
        rank = lax.axis_index("dp")
        self.strides = []
        stride = size
        for extent in self.dims:
            stride //= extent
            self.strides.append(stride)
        self.coords = [lax.rem(rank // s, e) for s, e in zip(self.strides, self.dims)]

    def send(self, value, stage, ahead):
        extent, stride = self.dims[stage], self.strides[stage]
        pairs = []
        for source in range(self.size):
            at = source // stride % extent
            pairs.append((source, source + ((at + ahead) % extent - at) * stride))
        return lax.ppermute(value, "dp", pairs)


def put(buffer, piece, axis, index):
    starts = [0] * buffer.ndim
    starts[axis] = index
    return lax.dynamic_update_slice(buffer, jnp.expand_dims(piece, axis), tuple(starts))


def take(buffer, axis, index):
    return lax.dynamic_index_in_dim(buffer, index, axis, keepdims=False)


def gather_half(grid, shard, half_stage):
    rows, columns = shard.shape
    value = shard[None]
    done = 0
    order = list(range(len(grid.dims)))
    for stage in order:
        if done == half_stage:
            value = jnp.concatenate([value, half_swap(value)], 0)
        extent, coord = grid.dims[stage], grid.coords[stage]
        axis = 1 + done
        shape = value.shape[:axis] + (extent,) + value.shape[axis:]
        buffer = put(jnp.zeros(shape, value.dtype), value, axis, coord)
        for ahead in range(1, extent):
            source = lax.rem(coord + extent - ahead, extent)
            buffer = put(buffer, grid.send(value, stage, ahead), axis, source)
        value = buffer
        done += 1
    if done == half_stage:
        other = half_swap(value)
        return value.reshape(-1, columns), other.reshape(-1, columns)
    return value[0].reshape(-1, columns), value[1].reshape(-1, columns)


def scatter_sum(grid, mine, theirs, half_first):
    columns = mine.shape[1]
    shape = grid.dims + (mine.shape[0] // grid.size, columns)
    order = list(range(len(grid.dims)))[::-1]

    def along(value, stage):
        extent, coord = grid.dims[stage], grid.coords[stage]
        axis = value.ndim - 3
        total = take(value, axis, coord).astype(F32)
        for ahead in range(1, extent):
            piece = take(value, axis, lax.rem(coord + ahead, extent))
            total = total + grid.send(piece.astype(BF16), stage, ahead).astype(F32)
        return total

    mine, theirs = mine.reshape(shape), theirs.reshape(shape)
    if half_first:
        value = mine.astype(F32) + half_swap(theirs.astype(BF16)).astype(F32)
        for stage in order:
            value = along(value, stage)
        return value
    first = order[0]
    mine = along(mine, first)
    theirs = along(theirs, first)
    value = mine + half_swap(theirs.astype(BF16)).astype(F32)
    for stage in order[1:]:
        value = along(value, stage)
    return value


def sum_half(grid, pair):
    value = pair[0] + half_swap(pair[1])
    for stage in range(len(grid.dims)):
        total = value
        for ahead in range(1, grid.dims[stage]):
            total = total + grid.send(value, stage, ahead)
        value = total
    return value


def sum_all(grid, value, over_cores):
    for stage in range(len(grid.dims)):
        total = value
        for ahead in range(1, grid.dims[stage]):
            total = total + grid.send(value, stage, ahead)
        value = total
    value = value + half_swap(value)
    if over_cores:
        value = value + core_swap(value)
    return value


def offsets():
    listing, offset = [], 0
    for extent in LENS:
        listing.append(offset)
        offset += UTT * extent
    return listing


def move_plan(rows_local):
    start = offsets()[2]
    count = 2 * rows_local - start
    free = -(-(start + MOSTS[2] - 3 * rows_local) // 16) * 16
    return rows_local - count, free, count


def row_table(rows_local, member, lengths):
    source, free, count = move_plan(rows_local)
    starts = offsets()
    local = jnp.arange(rows_local)
    row = member * rows_local + local
    slot = (row >= starts[1]).astype(jnp.int32) + (row >= starts[2]).astype(jnp.int32)
    place = row - jnp.where(slot == 0, starts[0], jnp.where(slot == 1, starts[1], starts[2]))
    arrived = (member == 3) & (local >= free) & (local < free + count)
    left = (member == 1) & (local >= source)
    place = jnp.where(arrived, local - free, place)
    length = jnp.where(slot == 0, lengths[0, 0], jnp.where(slot == 1, lengths[0, 1], lengths[0, 2]))
    return slot, (place < length) & ~left


def bring(rows, member):
    source, free, count = move_plan(rows.shape[0])
    moved = lax.ppermute(rows[source:], "mp", [(1, 3)])
    placed = lax.dynamic_update_slice(rows, moved, (free, 0))
    return jnp.where(member == 3, placed, rows)


def put_back(rows, moved, member):
    source, free, count = move_plan(rows.shape[0])
    placed = lax.dynamic_update_slice(rows, moved, (source, 0))
    cleared = lax.dynamic_update_slice(rows, jnp.zeros_like(moved), (free, 0))
    return jnp.where(member == 1, placed, jnp.where(member == 3, cleared, rows))


def send_back(rows, member):
    source, free, count = move_plan(rows.shape[0])
    return put_back(rows, lax.ppermute(rows[free : free + count], "mp", [(3, 1)]), member)


CHAIN = 4
X_FIRST = (False, True, True, False)
WHERE = [(0, 0)] + [(step, sign) for step in range(1, CHAIN) for sign in (1, -1)]


class Place:
    def __init__(self):
        self.dp = lax.axis_index("dp")
        self.mp = lax.axis_index("mp")
        self.z = self.dp // 2
        self.x = lax.rem(self.dp, 2)
        self.up = (self.dp + 2, self.mp)
        self.down = (self.dp - 2, self.mp)
        self.across = (self.dp + 1 - 2 * self.x, self.mp)
        self.other = (self.dp, lax.rem(self.mp + 2, 4))
        self.mate = (self.dp, self.mp + 1 - 2 * lax.rem(self.mp, 2))
        self.has_up = self.z < CHAIN - 1
        self.has_down = self.z > 0

    def ring(self, ahead):
        return (lax.rem(self.dp + 2 * ahead, 2 * CHAIN), self.mp)

    def greet(self, peers):
        barrier = pltpu.get_barrier_semaphore()
        for peer in peers:
            pl.semaphore_signal(
                barrier, inc=1, device_id=peer, device_id_type=pl.DeviceIdType.MESH
            )
        pl.semaphore_wait(barrier, len(peers))


def remote(source, target, sends, arrivals, index, device):
    return pltpu.make_async_remote_copy(
        source,
        target,
        sends.at[index],
        arrivals.at[index],
        device_id=device,
        device_id_type=pl.DeviceIdType.MESH,
    )


def gather_kernel(row_plan, *refs):
    shards, (rows_ref, cot_ref, vec_ref) = refs[0:4], refs[4:7]
    fulls, (rows_out, cot_out, vec_out) = refs[7:11], refs[11:14]
    sends, arrivals, side_send, side_arrive, local = refs[14:19]
    here = Place()
    source, free, count = row_plan
    n_rows = rows_ref.shape[0]
    here.greet([here.ring(1), here.ring(2), here.ring(3), here.across, here.other, here.mate,
                (here.dp, 3 - here.mp)])

    def z_of(where):
        step, sign = where
        return here.z - step * sign

    def held(where):
        step, sign = where
        if step == 0:
            return None
        return here.z >= step if sign > 0 else here.z + step < CHAIN

    def maybe(condition, action):
        if condition is None:
            action()
        else:
            pl.when(condition)(action)

    def block(w, where, far, half):
        x = 1 - here.x if far else here.x
        return fulls[w].at[half, z_of(where) * 2 + x]

    def chain(w, where):
        step, sign = where
        origin = shards[w] if step == 0 else block(w, where, False, 0)
        jobs = []
        for way in (1, -1) if step == 0 else (sign,):
            index = step + (0 if way > 0 else 3)
            device = here.up if way > 0 else here.down
            go = here.has_up if way > 0 else here.has_down
            if step < CHAIN - 1:
                jobs.append((go, remote(origin, block_to(w, where), sends.at[w], arrivals.at[w], index, device)))
        return jobs

    def block_to(w, where):
        return fulls[w].at[0, z_of(where) * 2 + here.x]

    def second(w, where):
        origin = shards[w] if where[0] == 0 else block(w, where, False, 0)
        index = 6 + WHERE.index(where)
        if X_FIRST[w]:
            return remote(origin, block(w, where, False, 0), sends.at[w], arrivals.at[w], index, here.across)
        return remote(origin, block(w, where, False, 1), sends.at[w], arrivals.at[w], index, here.other)

    def third(w, where, arrived):
        index = 13 + WHERE.index(where) + (len(WHERE) if arrived else 0)
        if X_FIRST[w]:
            origin = shards[w] if where[0] == 0 and not arrived else block(w, where, arrived, 0)
            return remote(origin, block(w, where, arrived, 1), sends.at[w], arrivals.at[w], index, here.other)
        origin = shards[w] if where[0] == 0 and not arrived else block(w, where, False, int(arrived))
        return remote(origin, block(w, where, False, int(arrived)), sends.at[w], arrivals.at[w], index, here.across)

    def landing(w, where, stage, arrived=False):
        if stage == 2:
            index = 6 + WHERE.index(where)
            target = block(w, where, True, 0) if X_FIRST[w] else block(w, where, False, 1)
            device = here.across if X_FIRST[w] else here.other
        else:
            index = 13 + WHERE.index(where) + (len(WHERE) if arrived else 0)
            if X_FIRST[w]:
                target, device = block(w, where, arrived, 1), here.other
            else:
                target, device = block(w, where, True, int(arrived)), here.across
        return remote(target, target, sends.at[w], arrivals.at[w], index, device)

    def chain_landing(w, where):
        step, sign = where
        index = step - 1 + (0 if sign > 0 else 3)
        target = block(w, where, False, 0)
        return remote(target, target, sends.at[w], arrivals.at[w], index, here.down if sign > 0 else here.up)

    order = (0, 1, 3, 2)
    by_step = [[p for p in WHERE if p[0] == step] for step in range(CHAIN)]

    low, high = pl.ds(0, free), pl.ds(free + count, n_rows - free - count)
    middle, tail = pl.ds(free, count), pl.ds(source, count)
    locals_ = [(None, pltpu.make_async_copy(shards[w], fulls[w].at[0, here.dp], local.at[w])) for w in order]
    not_last, second_core = here.mp != 3, here.mp == 1
    for n, (given, taken) in enumerate(((rows_ref, rows_out.at[0]), (cot_ref, cot_out))):
        for m, part in enumerate((low, high, middle)):
            copy = pltpu.make_async_copy(given.at[part], taken.at[part], local.at[4 + 3 * n + m])
            locals_.append((not_last if m == 2 else None, copy))
    for condition, copy in locals_:
        maybe(condition, copy.start)

    def to_mate(m, part):
        return remote(rows_ref.at[part], rows_out.at[1, part], side_send, side_arrive, m, here.mate)

    side = [(None, to_mate(0, low)), (None, to_mate(1, high)), (not_last, to_mate(2, middle))]
    side.append((None, remote(vec_ref, vec_out, side_send, side_arrive, 3, here.other)))
    moved = [
        remote(rows_ref.at[tail], rows_out.at[0, middle], side_send, side_arrive, 4, here.other),
        remote(cot_ref.at[tail], cot_out.at[middle], side_send, side_arrive, 5, here.other),
        remote(rows_ref.at[tail], rows_out.at[1, middle], side_send, side_arrive, 6, (here.dp, 3 - here.mp)),
    ]
    side += [(second_core, copy) for copy in moved]

    started = []

    def start(condition, copy):
        maybe(condition, copy.start)
        started.append((condition, copy))

    for condition, copy in side:
        start(condition, copy)
    for step in range(CHAIN):
        for where in by_step[step]:
            for w in order:
                if step > 0:
                    maybe(held(where), chain_landing(w, where).wait_recv)
                for go, copy in chain(w, where):
                    both = go if held(where) is None else jnp.logical_and(go, held(where))
                    start(both, copy)
                start(held(where), second(w, where))
                start(held(where), third(w, where, False))
        for where in by_step[step - 1] if step > 0 else ():
            for w in order:
                maybe(held(where), landing(w, where, 2).wait_recv)
                start(held(where), third(w, where, True))
    for where in by_step[CHAIN - 1]:
        for w in order:
            maybe(held(where), landing(w, where, 2).wait_recv)
            start(held(where), third(w, where, True))
    for where in WHERE:
        for w in order:
            for arrived in (False, True):
                maybe(held(where), landing(w, where, 3, arrived).wait_recv)
    to_mate(0, low).wait_recv()
    to_mate(1, high).wait_recv()
    pl.when(here.mp != 2)(to_mate(2, middle).wait_recv)
    side[3][1].wait_recv()
    pl.when(here.mp == 3)(moved[0].wait_recv)
    pl.when(here.mp == 3)(moved[1].wait_recv)
    pl.when(here.mp == 2)(moved[2].wait_recv)
    for condition, copy in started:
        maybe(condition, copy.wait_send)
    for condition, copy in locals_:
        maybe(condition, copy.wait)


def gather_all(shards, rows, cotangent, vectors):
    rows_local, width = rows.shape
    vmem, anywhere = pl.BlockSpec(memory_space=pltpu.VMEM), pl.BlockSpec(memory_space=pl.ANY)
    shapes = [jax.ShapeDtypeStruct((2, 2 * CHAIN) + s.shape, s.dtype) for s in shards]
    shapes += [
        jax.ShapeDtypeStruct((2, rows_local, width), rows.dtype),
        jax.ShapeDtypeStruct((rows_local, width), rows.dtype),
        jax.ShapeDtypeStruct(vectors.shape, vectors.dtype),
    ]
    plan = move_plan(rows_local)
    return pl.pallas_call(
        lambda *refs: gather_kernel(plan, *refs),
        out_shape=shapes,
        in_specs=[vmem] * 7,
        out_specs=[anywhere] * 6 + [vmem],
        scratch_shapes=[
            pltpu.SemaphoreType.DMA((4, 27)),
            pltpu.SemaphoreType.DMA((4, 27)),
            pltpu.SemaphoreType.DMA((7,)),
            pltpu.SemaphoreType.DMA((7,)),
            pltpu.SemaphoreType.DMA((10,)),
        ],
        compiler_params=pltpu.CompilerParams(
            collective_id=0, has_side_effects=True, vmem_limit_bytes=16 * 2**20
        ),
        name="gather_all",
    )(*shards, rows, cotangent, vectors)


def finish_kernel(block, *refs):
    attn_ref, grad_ref, q_ref, k_ref, v_ref, rows_ref, weight_ref = refs[0:7]
    out_near, out_far, up_ref, down_ref, vec_ref, out_edge, branch_ref = refs[7:14]
    sums, (vec_out, out_back, grad_back, grad_out) = refs[14:18], refs[18:22]
    firsts, seconds, thirds, finals = [refs[22 + 4 * i : 26 + 4 * i] for i in range(4)]
    (g_ref, dq_ref, dk_ref, dv_ref, parts_ref, g_qkv, rows_t, to_mate, from_mate, grad_edge) = refs[38:48]
    vec_in, sends, arrivals, side_send, side_arrive = refs[48:53]
    mine = (g_qkv.at[0], out_near, up_ref.at[0], down_ref.at[0])
    theirs = (g_qkv.at[1], out_far, up_ref.at[1], down_ref.at[1])
    n_rows = branch_ref.shape[0]
    _, free, count = move_plan(n_rows)
    here = Place()
    here.greet([here.ring(1), here.ring(2), here.ring(3), here.across, here.other, here.mate])
    early, late = (2, 3, 1), (0,)
    order = (2, 1, 3, 0)

    def owner(ahead):
        return lax.rem(here.z + ahead, CHAIN)

    far = 1 - here.x
    started = []

    def start(copy, condition=None):
        if condition is None:
            copy.start()
        else:
            pl.when(condition)(copy.start)
        started.append((condition, copy))
        return copy

    def add(target, more):
        target[...] = (target[...].astype(F32) + more[...].astype(F32)).astype(BF16)

    first_jobs, second_jobs = {}, {}

    def first_stage(weights):
        for ahead in order:
            target = owner(ahead)
            for w in weights:
                for part in (0, 1):
                    if X_FIRST[w]:
                        origin, device = theirs[w].at[target, part], here.other
                    else:
                        origin, device = (mine, theirs)[part][w].at[target, far], here.across
                    landed = firsts[w].at[target, part]
                    first_jobs[w, ahead, part] = start(
                        remote(origin, landed, sends.at[w], arrivals.at[w], 2 * ahead + part, device)
                    )

    def second_stage(weights):
        for ahead in order:
            target = owner(ahead)
            for w in weights:
                for part in (0, 1):
                    first_jobs[w, ahead, part].wait_recv()
                    if X_FIRST[w]:
                        add(firsts[w].at[target, part], mine[w].at[target, part])
                    else:
                        add(firsts[w].at[target, part], (mine, theirs)[part][w].at[target, here.x])
                if X_FIRST[w]:
                    origin, device = firsts[w].at[target, far], here.across
                else:
                    origin, device = firsts[w].at[target, 1], here.other
                landed = seconds[w].at[target]
                second_jobs[w, ahead] = start(
                    remote(origin, landed, sends.at[w], arrivals.at[w], 8 + ahead, device)
                )

    third_jobs = {}

    def third_stage(weights):
        for ahead in order:
            target = owner(ahead)
            for w in weights:
                second_jobs[w, ahead].wait_recv()
                kept = firsts[w].at[target, here.x] if X_FIRST[w] else firsts[w].at[target, 0]
                add(seconds[w].at[target], kept)
                if ahead > 0:
                    third_jobs[w, ahead] = start(
                        remote(
                            seconds[w].at[target],
                            thirds[w].at[ahead - 1],
                            sends.at[w],
                            arrivals.at[w],
                            11 + ahead,
                            here.ring(ahead),
                        )
                    )

    def settle_sums(weights):
        for w in weights:
            total = seconds[w][here.z].astype(F32)
            for ahead in range(1, CHAIN):
                third_jobs[w, ahead].wait_recv()
                total = total + thirds[w][ahead - 1].astype(F32)
            finals[w][...] = total

    first_stage(early)
    edges = [start(remote(out_edge, out_back, side_send, side_arrive, 6, here.other), here.mp == 3)]

    attend_back_body(
        block, 3, attn_ref, grad_ref, q_ref, k_ref, v_ref, (parts_ref.at[0], parts_ref.at[1]),
        g_ref, dq_ref, dk_ref, dv_ref,
    )
    rows_t[...] = rows_ref[...].T
    d_rows = jnp.zeros(rows_ref.shape, F32)
    vec_out[...] = vec_ref[...]
    depth, columns = g_qkv.shape[3], g_qkv.shape[4]
    for half in (0, 1):
        part = parts_ref[half]
        d_rows = d_rows + dot(part, weight_ref[half], ((1,), (1,)))
        grads = dot(rows_t[...], part, ((1,), (0,))).astype(BF16)
        for at in range(2 * CHAIN):
            g_qkv[half, at // 2, at % 2] = grads[at * depth : (at + 1) * depth, :]
        row = 7 + 2 * half
        vec_out[row : row + 1, 0:columns] = jnp.sum(part.astype(F32), axis=0, keepdims=True)
    to_mate[...] = d_rows[n_rows:, :].astype(BF16)
    grad_out[...] = d_rows[0:n_rows, :] + branch_ref[...]
    mate_job = start(remote(to_mate, from_mate, side_send, side_arrive, 8, here.mate))

    def vec_send(index, device):
        copy = remote(vec_out, vec_in.at[index], side_send, side_arrive, index, device)
        copy.start()
        return copy

    sent = vec_send(0, here.other)
    second_stage(early)
    first_stage(late)
    mate_job.wait_recv()
    grad_out[...] = grad_out[...] + from_mate[...].astype(F32)
    grad_edge[...] = grad_out[free : free + count, :]
    edges.append(start(remote(grad_edge, grad_back, side_send, side_arrive, 7, here.other), here.mp == 3))
    sent.wait()
    vec_out[0:6] = vec_out[0:6] + vec_in[0, 0:6]
    vec_out[6:8] = vec_out[6:8] + vec_in[0, 8:10]
    sent = vec_send(1, here.across)
    third_stage(early)
    second_stage(late)
    sent.wait()
    vec_out[...] = vec_out[...] + vec_in[1]
    ring = [vec_send(1 + ahead, here.ring(ahead)) for ahead in (1, 2, 3)]
    third_stage(late)
    settle_sums(early)
    for copy in ring:
        copy.wait()
    slots = [vec_out[...], vec_in[2], vec_in[3], vec_in[4]]
    total = jnp.zeros_like(slots[0])
    for at in range(CHAIN):
        for behind in range(CHAIN):
            same = lax.rem(here.z + CHAIN - behind, CHAIN) == at
            total = total + jnp.where(same, slots[behind], 0.0)
    vec_out[...] = total
    sent = vec_send(5, here.mate)
    for w in (2, 3):
        sums[w][...] = finals[w][...]
    value = finals[1][...]
    pad = jnp.zeros((LANES - value.shape[0], value.shape[1]), F32)
    sums[1][...] = jnp.concatenate([value, pad], 0).T[:, : value.shape[0]]
    settle_sums(late)
    for c in range(sums[0].shape[0]):
        sums[0][c] = finals[0][:, c * sums[0].shape[2] : (c + 1) * sums[0].shape[2]]

    sent.wait()
    vec_out[0:6] = vec_out[0:6] + vec_in[5, 0:6]
    for copy in edges:
        pl.when(here.mp == 1)(copy.wait_recv)
    for condition, copy in started:
        if condition is None:
            copy.wait_send()
        else:
            pl.when(condition)(copy.wait_send)


def finish_all(attn, grad, query, keys, values, rows, weight, out, up, down, vectors, out_edge, branch, block):
    heads, n_all = query.shape[:2]
    width = rows.shape[1]
    depth = width // (2 * CHAIN)
    out = [g.reshape(CHAIN, 2, depth, -1) for g in out]
    up, down = [g.reshape(2, CHAIN, 2, depth, -1) for g in (up, down)]
    columns = weight.shape[2]
    widths = [columns, out[0].shape[-1], up.shape[-1], down.shape[-1]]
    vmem = pl.BlockSpec(memory_space=pltpu.VMEM)
    shapes = [(3, depth, columns // 3), (widths[1], depth), (depth, widths[2]), (depth, widths[3])]
    shapes = [jax.ShapeDtypeStruct(shape, F32) for shape in shapes]
    shapes += [
        jax.ShapeDtypeStruct(vectors.shape, F32),
        jax.ShapeDtypeStruct(out_edge.shape, BF16),
        jax.ShapeDtypeStruct(out_edge.shape, F32),
        jax.ShapeDtypeStruct(branch.shape, F32),
    ]
    scratch = [pltpu.VMEM((CHAIN, 2, depth, n), BF16) for n in widths]
    scratch += [pltpu.VMEM((CHAIN, depth, n), BF16) for n in widths]
    scratch += [pltpu.VMEM((CHAIN - 1, depth, n), BF16) for n in widths]
    scratch += [pltpu.VMEM((depth, n), F32) for n in widths]
    scratch += [pltpu.VMEM(query.shape, BF16)] * 2 + [pltpu.VMEM(query.shape, F32)] * 2
    scratch += [
        pltpu.VMEM((2, n_all, columns), BF16),
        pltpu.VMEM((2, CHAIN, 2, depth, columns), BF16),
        pltpu.VMEM((width, n_all), BF16),
        pltpu.VMEM(branch.shape, BF16),
        pltpu.VMEM(branch.shape, BF16),
        pltpu.VMEM(out_edge.shape, F32),
        pltpu.VMEM((6,) + vectors.shape, F32),
        pltpu.SemaphoreType.DMA((4, 15)),
        pltpu.SemaphoreType.DMA((4, 15)),
        pltpu.SemaphoreType.DMA((9,)),
        pltpu.SemaphoreType.DMA((9,)),
    ]
    return pl.pallas_call(
        lambda *refs: finish_kernel(block, *refs),
        out_shape=shapes,
        in_specs=[vmem] * 14,
        out_specs=[vmem] * 8,
        scratch_shapes=scratch,
        compiler_params=pltpu.CompilerParams(
            collective_id=1, has_side_effects=True, vmem_limit_bytes=62 * 2**20
        ),
        name="finish_all",
    )(attn, grad, query, keys, values, rows, weight, *out, up, down, vectors, out_edge, branch)


def split_parts(value, count):
    parts = []
    for _ in range(count):
        part = value.astype(BF16).astype(F32)
        parts.append(part)
        value = value - part
    return parts


def lane_fill(base, parts, first):
    lane = lax.broadcasted_iota(jnp.int32, base.shape, 1)
    for index, part in enumerate(parts):
        base = jnp.where(lane == first + index, part, base)
    return base


def head_columns(head, part, per_half):
    half, index = divmod(head, per_half)
    at = (part * per_half + index) * HEAD_DIM
    return half, slice(at, at + HEAD_DIM)


def attend_kernel(block, near_ref, far_ref, slot_ref, mask_ref, attn_ref, q_ref, k_ref, v_ref, out_ref):
    acts = (near_ref, far_ref)
    heads, rows = q_ref.shape[:2]
    ones = lane_fill(jnp.zeros((rows, HEAD_DIM), F32), (1.0, 1.0), 0).astype(BF16)
    for head in range(heads):
        for part, (ref, more) in enumerate(((q_ref, slot_ref), (k_ref, mask_ref), (v_ref, None))):
            half, columns = head_columns(head, part, heads // 2)
            piece = acts[half][:, columns]
            if part == 0:
                piece = (piece.astype(F32) * HEAD_DIM ** (-0.5)).astype(BF16)
            ref[head, :, 0:HEAD_DIM] = piece
            ref[head, :, HEAD_DIM : 2 * HEAD_DIM] = ones if more is None else more[...]

    def step(index, carry):
        head, at = index // (rows // block), lax.rem(index, rows // block)
        span = pl.ds(pl.multiple_of(at * block, 16), block)
        query = q_ref[head, span, :]
        scores = dot(query, k_ref[head], ((1,), (1,)))
        peak = jnp.max(scores, axis=-1, keepdims=True)
        weights = jnp.exp(scores - peak)
        both = dot(weights.astype(BF16), v_ref[head], ((1,), (0,)))
        total = both[:, HEAD_DIM : HEAD_DIM + 1]
        out_ref[head, span, :] = (both * (1.0 / total)).astype(BF16)
        log_sum = peak + jnp.log(total)
        parts = [-p for p in split_parts(log_sum, 3)]
        q_ref[head, span, :] = lane_fill(query.astype(F32), parts, HEAD_DIM + 3).astype(BF16)
        return carry

    lax.fori_loop(0, heads * (rows // block), step, 0, unroll=6)
    for head in range(heads):
        attn_ref[:, head * HEAD_DIM : (head + 1) * HEAD_DIM] = out_ref[head, :, 0:HEAD_DIM]


def attend_back_body(block, unroll, attn_ref, grad_ref, q_ref, k_ref, v_ref, outs, g_ref, dq_ref, dk_ref, dv_ref):
    heads, rows = q_ref.shape[:2]
    for head in range(heads):
        columns = slice(head * HEAD_DIM, (head + 1) * HEAD_DIM)
        grad = grad_ref[:, columns]
        mean = jnp.sum(grad.astype(F32) * attn_ref[:, columns].astype(F32), axis=-1, keepdims=True)
        parts = [-p for p in split_parts(mean, 2)]
        g_ref[head, :, 0:HEAD_DIM] = grad
        g_ref[head, :, HEAD_DIM : 2 * HEAD_DIM] = lane_fill(
            jnp.zeros((rows, HEAD_DIM), F32), parts, 0
        ).astype(BF16)
    dk_ref[...] = jnp.zeros_like(dk_ref)
    dv_ref[...] = jnp.zeros_like(dv_ref)

    def step(index, carry):
        head, at = index // (rows // block), lax.rem(index, rows // block)
        span = pl.ds(pl.multiple_of(at * block, 16), block)
        query, grad = q_ref[head, span, :], g_ref[head, span, :]
        keys = k_ref[head]
        probs = jnp.exp(dot(keys, query, ((1,), (1,))))
        change = (probs * dot(v_ref[head], grad, ((1,), (1,)))).astype(BF16)
        dv_ref[head] += dot(probs.astype(BF16), grad, ((1,), (0,)))
        dk_ref[head] += dot(change, query, ((1,), (0,)))
        dq_ref[head, span, :] = (dot(change, keys, ((0,), (0,))) * HEAD_DIM ** (-0.5)).astype(BF16)
        return carry

    lax.fori_loop(0, heads * (rows // block), step, 0, unroll=unroll)
    for head in range(heads):
        for part, ref in enumerate((dq_ref, dk_ref, dv_ref)):
            half, columns = head_columns(head, part, heads // 2)
            outs[half][:, columns] = ref[head, :, 0:HEAD_DIM].astype(BF16)


def attend_back_kernel(block, attn_ref, grad_ref, q_ref, k_ref, v_ref, near_ref, far_ref, *scratch):
    attend_back_body(
        block, 1, attn_ref, grad_ref, q_ref, k_ref, v_ref, (near_ref, far_ref), *scratch
    )


def attend_cost(heads, rows, products):
    return pl.CostEstimate(
        flops=2 * products * heads * rows * rows * 128,
        bytes_accessed=8 * heads * rows * 128,
        transcendentals=heads * rows * rows,
    )


def attend(near, far, slots, masks, block):
    rows = near.shape[0]
    heads = 2 * near.shape[1] // (3 * HEAD_DIM)
    vmem = pl.BlockSpec(memory_space=pltpu.VMEM)
    wide = jax.ShapeDtypeStruct((heads, rows, 2 * HEAD_DIM), BF16)
    return pl.pallas_call(
        lambda *refs: attend_kernel(block, *refs),
        out_shape=[jax.ShapeDtypeStruct((rows, heads * HEAD_DIM), BF16), wide, wide, wide],
        in_specs=[vmem] * 4,
        out_specs=[vmem] * 4,
        scratch_shapes=[pltpu.VMEM(wide.shape, BF16)],
        compiler_params=pltpu.CompilerParams(vmem_limit_bytes=40 * 2**20),
        cost_estimate=attend_cost(heads, rows, 2),
        name="attend",
    )(near, far, slots, masks)


def attend_back(attn, grad, query, keys, values, block):
    heads, rows = query.shape[:2]
    vmem = pl.BlockSpec(memory_space=pltpu.VMEM)
    out = jax.ShapeDtypeStruct((rows, 3 * heads // 2 * HEAD_DIM), BF16)
    return pl.pallas_call(
        lambda *refs: attend_back_kernel(block, *refs),
        out_shape=[out, out],
        in_specs=[vmem] * 5,
        out_specs=[vmem] * 2,
        scratch_shapes=[pltpu.VMEM(query.shape, BF16)] * 2 + [pltpu.VMEM(query.shape, F32)] * 2,
        compiler_params=pltpu.CompilerParams(vmem_limit_bytes=40 * 2**20),
        cost_estimate=attend_cost(heads, rows, 5),
        name="attend_back",
    )(attn, grad, query, keys, values)


def norm_stats(values):
    mean = jnp.mean(values, axis=-1, keepdims=True)
    center = values - mean
    spread = jnp.mean(center * center, axis=-1, keepdims=True)
    inverse = lax.rsqrt(spread + EPS)
    return center * inverse, inverse


def norm_back(grad, unit, inverse, gain):
    scaled = grad * gain
    return inverse * (
        scaled
        - jnp.mean(scaled, axis=-1, keepdims=True)
        - unit * jnp.mean(scaled * unit, axis=-1, keepdims=True)
    )


def feed_back_kernel(n_rows, first_ref, grad_ref, up_ref, down_ref, near_hidden, far_hidden,
                     near_slope, far_slope, g_up_ref, g_down_ref, g_bias_ref, own_ref, mate_ref, total_ref, first_t, grad_t):
    step = pl.program_id(0)

    @pl.when(step == 0)
    def _():
        first_t[...] = first_ref[...].T
        grad_t[...] = grad_ref[...].T
        total_ref[...] = jnp.zeros_like(total_ref)

    near = step < pl.num_programs(0) // 2
    hidden = jnp.where(near, near_hidden[...], far_hidden[...])
    slope = jnp.where(near, near_slope[...], far_slope[...])
    d_hidden = dot(grad_ref[...], down_ref[0], ((1,), (0,)))
    d_pre = (d_hidden * slope.astype(F32)).astype(BF16)
    total_ref[...] += dot(d_pre, up_ref[0], ((1,), (1,)))
    g_bias_ref[0] = jnp.sum(d_pre.astype(F32), axis=0, keepdims=True)
    g_up_ref[0] = dot(first_t[...], d_pre, ((1,), (0,))).astype(BF16)
    g_down_ref[0] = dot(grad_t[...], hidden, ((1,), (0,))).astype(BF16)

    @pl.when(step == pl.num_programs(0) - 1)
    def _():
        own_ref[...] = total_ref[0:n_rows, :]
        mate_ref[...] = total_ref[n_rows:, :].astype(BF16)


def feed_specs(rows, width, units, tile):
    blocks = units // tile
    whole = pl.BlockSpec((rows, width), lambda i: (0, 0))
    half = pl.BlockSpec((rows // 2, width), lambda i: (0, 0))

    def split(count):
        return pl.BlockSpec((1, count, tile), lambda i: (i // blocks, 0, lax.rem(i, blocks)))

    halves = [jax.ShapeDtypeStruct((rows // 2, width), kind) for kind in (F32, BF16)]
    return (2 * blocks,), whole, half, split, halves


def feed_back(first, grad, up, down, hiddens, slopes, tile):
    (rows, width), units = first.shape, up.shape[2]
    grid, whole, half, split, halves = feed_specs(rows, width, units, tile)
    last = units // tile - 1
    near = pl.BlockSpec((rows, tile), lambda i: (0, jnp.minimum(i, last)))
    far = pl.BlockSpec((rows, tile), lambda i: (0, jnp.maximum(i - last - 1, 0)))
    wide = jax.ShapeDtypeStruct((2, width, units), BF16)
    return pl.pallas_call(
        lambda *refs: feed_back_kernel(rows // 2, *refs),
        grid=grid,
        out_shape=[wide, wide, jax.ShapeDtypeStruct((2, 1, units), F32)] + halves,
        in_specs=[whole, whole, split(width), split(width), near, far, near, far],
        out_specs=[split(width), split(width), split(1), half, half],
        scratch_shapes=[
            pltpu.VMEM((rows, width), F32),
            pltpu.VMEM((width, rows), BF16),
            pltpu.VMEM((width, rows), BF16),
        ],
        compiler_params=pltpu.CompilerParams(vmem_limit_bytes=48 * 2**20),
        cost_estimate=pl.CostEstimate(
            flops=16 * rows * width * units,
            bytes_accessed=16 * width * units + 8 * rows * units,
            transcendentals=0,
        ),
        name="feed_back",
    )(first, grad, up, down, *hiddens, *slopes)


def update_one(rate, weight, grad, moment, average):
    moment_next = MOMENTUM * moment + grad
    weight_next = weight - rate * (grad + MOMENTUM * moment_next)
    return (weight_next, moment_next, DECAY * average + (1.0 - DECAY) * weight_next)


def on_device(
    tokens,
    lengths,
    cotangent,
    qkv_weight,
    out_weight,
    up_weight,
    down_weight,
    head_bias,
    up_bias,
    norm_vectors,
    qkv_moment,
    out_moment,
    up_moment,
    down_moment,
    head_bias_moment,
    up_bias_moment,
    norm_moment,
    qkv_average,
    out_average,
    up_average,
    down_average,
    head_bias_average,
    up_bias_average,
    norm_average,
):
    grid = Grid(lax.axis_size("dp"))
    member = lax.axis_index("mp")
    mate = member + 1 - 2 * lax.rem(member, 2)
    rows_local, width = tokens.shape
    head_width = qkv_weight.shape[2]
    stages = len(grid.dims)
    units = up_weight.shape[1]

    qkv_shard = jnp.transpose(qkv_weight, (1, 0, 2)).reshape(-1, 3 * head_width).astype(BF16)
    shards = (
        qkv_shard,
        out_weight.astype(BF16).T,
        up_weight.astype(BF16),
        down_weight.astype(BF16).T,
    )
    kernels = grid.size == 2 * CHAIN and units == width
    if kernels:
        flat = jnp.pad(head_bias.reshape(-1), (0, width - 2 * head_width))
        vectors = jnp.zeros((8, width), F32).at[0].set(up_bias).at[1].set(flat)
        *fulls, rows_both, own_cotangent, far_vectors = gather_all(
            shards, tokens, cotangent, vectors
        )
        qkv_pair, out_pair, up_pair, down_pair = [full.reshape(2, width, -1) for full in fulls]
        far_bias = far_vectors[1, : 2 * head_width].reshape(2, head_width)
        bias_pair, up_bias_pair = (head_bias, far_bias), (up_bias, far_vectors[0])
        tokens_all = rows_both.reshape(2 * rows_local, width)
        own_tokens = rows_both[0]
    else:
        qkv_pair = gather_half(grid, shards[0], stages)
        out_pair = gather_half(grid, shards[1], stages - 1)
        up_pair = jnp.stack(gather_half(grid, shards[2], stages))
        down_pair = jnp.stack(gather_half(grid, shards[3], stages - 1))
        bias_pair = (head_bias, half_swap(head_bias))
        up_bias_pair = (up_bias, half_swap(up_bias))
        own_tokens = bring(tokens, member)
        own_cotangent = bring(cotangent, member)
        tokens_all = jnp.concatenate([own_tokens, core_swap(own_tokens)], 0)

    slot_own, valid_own = row_table(rows_local, member, lengths)
    slot_mate, valid_mate = row_table(rows_local, mate, lengths)
    slot = jnp.concatenate([slot_own, slot_mate])
    frame = jnp.concatenate([valid_own, valid_mate])
    column = jnp.arange(HEAD_DIM)[None, :]
    here_slot = slot[:, None] == column
    slot_lanes = here_slot.astype(BF16)
    mask_lanes = jnp.where(
        column < len(LENS),
        jnp.where(here_slot & frame[:, None], 0.0, NEG_FILL),
        jnp.where(column < len(LENS) + 3, 1.0, 0.0),
    ).astype(BF16)
    live = valid_own[:, None]

    def share(rows):
        return jnp.concatenate([rows, core_swap(rows)], 0)

    def settle(partial):
        return partial[:rows_local] + core_swap(partial[rows_local:].astype(BF16)).astype(F32)

    block = 2 * rows_local
    parts = []
    for weight, bias in zip(qkv_pair, bias_pair):
        rows_bias = jnp.concatenate([bias[0], jnp.zeros_like(bias[0]), bias[1]])
        parts.append((dot(tokens_all, weight, ((1,), (0,))) + rows_bias).astype(BF16))
    attn, query, keys, values = attend(*parts, slot_lanes, mask_lanes, block)
    out_both = jnp.concatenate([out_pair[0], out_pair[1]], 1)
    branch = settle(dot(attn, out_both, ((1,), (1,))))
    unit_one, inverse_one = norm_stats(branch + norm_vectors[0] + own_tokens.astype(F32))
    first = unit_one * norm_vectors[2] + norm_vectors[3]
    first_all = share(first.astype(BF16))

    hiddens, slopes = [], []
    for at in (0, 1):
        pre = dot(first_all, up_pair[at], ((1,), (0,))) + up_bias_pair[at]
        phi = 0.5 * (1.0 + lax.erf(pre * (0.5**0.5)))
        density = jnp.exp(-0.5 * pre * pre) * (1.0 / math.sqrt(2.0 * math.pi))
        hiddens.append((pre * phi).astype(BF16))
        slopes.append((phi + pre * density).astype(BF16))
    ffn = settle(
        dot(hiddens[0], down_pair[0], ((1,), (1,))) + dot(hiddens[1], down_pair[1], ((1,), (1,)))
    )
    unit_two, inverse_two = norm_stats(ffn + norm_vectors[1] + first)
    second = unit_two * norm_vectors[4] + norm_vectors[5]
    layer_out = jnp.where(live, second, 0.0).astype(BF16)

    grad_two = jnp.where(live, own_cotangent.astype(F32), 0.0)
    d_second = norm_back(grad_two, unit_two, inverse_two, norm_vectors[4])
    d_ffn_all = share(d_second.astype(BF16))
    tile = 2 * LANES if units % (2 * LANES) == 0 else units
    grad_up, grad_down, grad_up_bias, d_first_own, d_first_mate = feed_back(
        first_all, d_ffn_all, up_pair, down_pair, hiddens, slopes, tile
    )
    grad_up_bias = grad_up_bias[:, 0, :]
    d_first = d_second + (d_first_own + core_swap(d_first_mate).astype(F32))

    d_branch = norm_back(d_first, unit_one, inverse_one, norm_vectors[2])
    d_branch_all = share(d_branch.astype(BF16))
    d_attn = dot(d_branch_all, out_both, ((1,), (0,))).astype(BF16)
    grad_out = [
        dot(d_branch_all, attn[:, at : at + head_width], ((0,), (0,))).astype(BF16)
        for at in (0, head_width)
    ]
    norm_part = jnp.stack(
        [
            jnp.sum(d_branch, axis=0),
            jnp.sum(d_second, axis=0),
            jnp.sum(d_first * unit_one, axis=0),
            jnp.sum(d_first, axis=0),
            jnp.sum(grad_two * unit_two, axis=0),
            jnp.sum(grad_two, axis=0),
        ]
    )
    if kernels:
        blank = jnp.zeros((1, width), F32)
        vectors = jnp.concatenate(
            [norm_part, grad_up_bias[:1], blank, grad_up_bias[1:], jnp.zeros((7, width), F32)]
        )
        source, free, count = move_plan(rows_local)
        *sums, vectors, out_back, grad_back, tokens_grad = finish_all(
            attn,
            d_attn,
            query,
            keys,
            values,
            tokens_all,
            qkv_pair,
            grad_out,
            grad_up,
            grad_down,
            vectors,
            layer_out[free : free + count],
            d_branch,
            block,
        )
        sum_qkv, sum_out, sum_up, sum_down = sums
        sum_down = sum_down.T
        layer_out = put_back(layer_out, out_back, member)
        tokens_grad = put_back(tokens_grad, grad_back, member)
        sum_norm, sum_up_bias, sum_bias = vectors[:6], vectors[6], vectors[7]
        sum_bias = sum_bias[: 3 * head_width]
    else:
        d_parts = attend_back(attn, d_attn, query, keys, values, block)
        grad_qkv = [dot(tokens_all, part, ((0,), (0,))).astype(BF16) for part in d_parts]
        grad_bias = [jnp.sum(part, axis=0, dtype=F32) for part in d_parts]
        d_tokens = settle(
            dot(d_parts[0], qkv_pair[0], ((1,), (1,))) + dot(d_parts[1], qkv_pair[1], ((1,), (1,)))
        )
        tokens_grad = d_tokens + d_branch
        sum_qkv = scatter_sum(grid, *grad_qkv, True)
        sum_out = scatter_sum(grid, *grad_out, True)
        sum_up = scatter_sum(grid, *grad_up, False)
        sum_down = scatter_sum(grid, *grad_down, True)
        layer_out = send_back(layer_out, member)
        tokens_grad = send_back(tokens_grad, member)
        sum_norm = sum_all(grid, norm_part, True)
        sum_up_bias = sum_half(grid, grad_up_bias)
        sum_bias = sum_half(grid, grad_bias)
        sum_qkv = jnp.transpose(sum_qkv.reshape(-1, 3, head_width), (1, 0, 2))
        sum_out, sum_down = sum_out.T, sum_down.T
    sum_head_bias = jnp.stack([sum_bias[:head_width], sum_bias[2 * head_width :]])

    divisor = math.sqrt(1000.0 * grid.size * UTT)
    params = (qkv_weight, out_weight, up_weight, down_weight, head_bias, up_bias, norm_vectors)
    grads = (sum_qkv, sum_out, sum_up, sum_down, sum_head_bias, sum_up_bias, sum_norm)
    moments = (
        qkv_moment,
        out_moment,
        up_moment,
        down_moment,
        head_bias_moment,
        up_bias_moment,
        norm_moment,
    )
    averages = (
        qkv_average,
        out_average,
        up_average,
        down_average,
        head_bias_average,
        up_bias_average,
        norm_average,
    )
    nexts, moment_nexts, average_nexts = ([], [], [])
    for weight, grad, moment, average, scale_one in zip(
        params, grads, moments, averages, RATE_SCALES
    ):
        weight_next, moment_next, average_next = update_one(
            scale_one / divisor, weight, grad, moment, average
        )
        nexts.append(weight_next)
        moment_nexts.append(moment_next)
        average_nexts.append(average_next)
    return (layer_out, tokens_grad, *grads, *nexts, *moment_nexts, *average_nexts)


ROWS = P(("dp", "mp"), None)
PARAMS = (
    P(None, "dp", "mp"),
    P("mp", "dp"),
    P("dp", "mp"),
    P("mp", "dp"),
    P(None, "mp"),
    P("mp"),
    P(),
)


def solution(mesh):
    return jax.shard_map(
        on_device,
        mesh=mesh,
        in_specs=(ROWS, P("dp", None), ROWS) + PARAMS * 3,
        out_specs=(ROWS, ROWS) + PARAMS * 4,
        check_vma=False,
    )
```

```python
import math

import jax
import jax.numpy as jnp
from jax import lax
from jax.experimental import pallas as pl
from jax.experimental.pallas import tpu as pltpu
from jax.sharding import PartitionSpec as P

HEAD_DIM = 64
LANES = 128
UTT = 1
LENS = (256, 512, 896)
MOSTS = (200, 400, 781)

EPS = 1e-05
MOMENTUM = 0.5
DECAY = 0.5
RATE_SCALES = (0.02, 0.16, 0.02, 0.02, 0.02, 0.32, 0.16)
NEG_FILL = -1000000000.0
BF16 = jnp.bfloat16
F32 = jnp.float32


def dot(a, b, dims):
    return lax.dot_general(a, b, (dims, ((), ())), preferred_element_type=F32)


CORE_SWAP = [(0, 1), (1, 0), (2, 3), (3, 2)]
HALF_SWAP = [(0, 2), (2, 0), (1, 3), (3, 1)]


def core_swap(value):
    return lax.ppermute(value, "mp", CORE_SWAP)


def half_swap(value):
    return lax.ppermute(value, "mp", HALF_SWAP)


def dp_dims(size):
    dims = []
    while size % 4 == 0:
        dims.append(4)
        size //= 4
    if size > 1:
        dims.append(size)
    return tuple(dims)


class Grid:
    def __init__(self, size):
        self.dims = dp_dims(size)
        self.size = size
        rank = lax.axis_index("dp")
        self.strides = []
        stride = size
        for extent in self.dims:
            stride //= extent
            self.strides.append(stride)
        self.coords = [lax.rem(rank // s, e) for s, e in zip(self.strides, self.dims)]

    def send(self, value, stage, ahead):
        extent, stride = self.dims[stage], self.strides[stage]
        pairs = []
        for source in range(self.size):
            at = source // stride % extent
            pairs.append((source, source + ((at + ahead) % extent - at) * stride))
        return lax.ppermute(value, "dp", pairs)


def put(buffer, piece, axis, index):
    starts = [0] * buffer.ndim
    starts[axis] = index
    return lax.dynamic_update_slice(buffer, jnp.expand_dims(piece, axis), tuple(starts))


def take(buffer, axis, index):
    return lax.dynamic_index_in_dim(buffer, index, axis, keepdims=False)


def gather_half(grid, shard, half_stage):
    rows, columns = shard.shape
    value = shard[None]
    done = 0
    order = list(range(len(grid.dims)))
    for stage in order:
        if done == half_stage:
            value = jnp.concatenate([value, half_swap(value)], 0)
        extent, coord = grid.dims[stage], grid.coords[stage]
        axis = 1 + done
        shape = value.shape[:axis] + (extent,) + value.shape[axis:]
        buffer = put(jnp.zeros(shape, value.dtype), value, axis, coord)
        for ahead in range(1, extent):
            source = lax.rem(coord + extent - ahead, extent)
            buffer = put(buffer, grid.send(value, stage, ahead), axis, source)
        value = buffer
        done += 1
    if done == half_stage:
        other = half_swap(value)
        return value.reshape(-1, columns), other.reshape(-1, columns)
    return value[0].reshape(-1, columns), value[1].reshape(-1, columns)


def scatter_sum(grid, mine, theirs, half_first):
    columns = mine.shape[1]
    shape = grid.dims + (mine.shape[0] // grid.size, columns)
    order = list(range(len(grid.dims)))[::-1]

    def along(value, stage):
        extent, coord = grid.dims[stage], grid.coords[stage]
        axis = value.ndim - 3
        total = take(value, axis, coord).astype(F32)
        for ahead in range(1, extent):
            piece = take(value, axis, lax.rem(coord + ahead, extent))
            total = total + grid.send(piece.astype(BF16), stage, ahead).astype(F32)
        return total

    mine, theirs = mine.reshape(shape), theirs.reshape(shape)
    if half_first:
        value = mine.astype(F32) + half_swap(theirs.astype(BF16)).astype(F32)
        for stage in order:
            value = along(value, stage)
        return value
    first = order[0]
    mine = along(mine, first)
    theirs = along(theirs, first)
    value = mine + half_swap(theirs.astype(BF16)).astype(F32)
    for stage in order[1:]:
        value = along(value, stage)
    return value


def sum_half(grid, pair):
    value = pair[0] + half_swap(pair[1])
    for stage in range(len(grid.dims)):
        total = value
        for ahead in range(1, grid.dims[stage]):
            total = total + grid.send(value, stage, ahead)
        value = total
    return value


def sum_all(grid, value, over_cores):
    for stage in range(len(grid.dims)):
        total = value
        for ahead in range(1, grid.dims[stage]):
            total = total + grid.send(value, stage, ahead)
        value = total
    value = value + half_swap(value)
    if over_cores:
        value = value + core_swap(value)
    return value


def offsets():
    listing, offset = [], 0
    for extent in LENS:
        listing.append(offset)
        offset += UTT * extent
    return listing


def move_plan(rows_local):
    start = offsets()[2]
    count = 2 * rows_local - start
    free = -(-(start + MOSTS[2] - 3 * rows_local) // 16) * 16
    return rows_local - count, free, count


def row_table(rows_local, member, lengths):
    source, free, count = move_plan(rows_local)
    starts = offsets()
    local = jnp.arange(rows_local)
    row = member * rows_local + local
    slot = (row >= starts[1]).astype(jnp.int32) + (row >= starts[2]).astype(jnp.int32)
    place = row - jnp.where(slot == 0, starts[0], jnp.where(slot == 1, starts[1], starts[2]))
    arrived = (member == 3) & (local >= free) & (local < free + count)
    left = (member == 1) & (local >= source)
    place = jnp.where(arrived, local - free, place)
    length = jnp.where(slot == 0, lengths[0, 0], jnp.where(slot == 1, lengths[0, 1], lengths[0, 2]))
    return slot, (place < length) & ~left


def bring(rows, member):
    source, free, count = move_plan(rows.shape[0])
    moved = lax.ppermute(rows[source:], "mp", [(1, 3)])
    placed = lax.dynamic_update_slice(rows, moved, (free, 0))
    return jnp.where(member == 3, placed, rows)


def put_back(rows, moved, member):
    source, free, count = move_plan(rows.shape[0])
    placed = lax.dynamic_update_slice(rows, moved, (source, 0))
    cleared = lax.dynamic_update_slice(rows, jnp.zeros_like(moved), (free, 0))
    return jnp.where(member == 1, placed, jnp.where(member == 3, cleared, rows))


def send_back(rows, member):
    source, free, count = move_plan(rows.shape[0])
    return put_back(rows, lax.ppermute(rows[free : free + count], "mp", [(3, 1)]), member)


CHAIN = 4
X_FIRST = (False, True, True, False)
WHERE = [(0, 0)] + [(step, sign) for step in range(1, CHAIN) for sign in (1, -1)]


class Place:
    def __init__(self):
        self.dp = lax.axis_index("dp")
        self.mp = lax.axis_index("mp")
        self.z = self.dp // 2
        self.x = lax.rem(self.dp, 2)
        self.up = (self.dp + 2, self.mp)
        self.down = (self.dp - 2, self.mp)
        self.across = (self.dp + 1 - 2 * self.x, self.mp)
        self.other = (self.dp, lax.rem(self.mp + 2, 4))
        self.mate = (self.dp, self.mp + 1 - 2 * lax.rem(self.mp, 2))
        self.has_up = self.z < CHAIN - 1
        self.has_down = self.z > 0

    def ring(self, ahead):
        return (lax.rem(self.dp + 2 * ahead, 2 * CHAIN), self.mp)

    def greet(self, peers):
        barrier = pltpu.get_barrier_semaphore()
        for peer in peers:
            pl.semaphore_signal(
                barrier, inc=1, device_id=peer, device_id_type=pl.DeviceIdType.MESH
            )
        pl.semaphore_wait(barrier, len(peers))


def remote(source, target, sends, arrivals, index, device):
    return pltpu.make_async_remote_copy(
        source,
        target,
        sends.at[index],
        arrivals.at[index],
        device_id=device,
        device_id_type=pl.DeviceIdType.MESH,
    )


def gather_kernel(row_plan, *refs):
    shards, (rows_ref, cot_ref, vec_ref, slot_ref, mask_ref) = refs[0:4], refs[4:9]
    fulls, (rows_out, cot_out, vec_out) = refs[9:13], refs[13:16]
    attn_ref, q_ref, k_ref, v_ref = refs[16:20]
    acts, out_ref, sends, arrivals, side_send, side_arrive, local = refs[20:27]
    here = Place()
    source, free, count = row_plan
    n_rows = rows_ref.shape[0]
    here.greet([here.ring(1), here.ring(2), here.ring(3), here.across, here.other, here.mate,
                (here.dp, 3 - here.mp)])

    def z_of(where):
        step, sign = where
        return here.z - step * sign

    def held(where):
        step, sign = where
        if step == 0:
            return None
        return here.z >= step if sign > 0 else here.z + step < CHAIN

    def maybe(condition, action):
        if condition is None:
            action()
        else:
            pl.when(condition)(action)

    def block(w, where, far, half):
        x = 1 - here.x if far else here.x
        return fulls[w].at[half, z_of(where) * 2 + x]

    def chain(w, where):
        step, sign = where
        origin = shards[w] if step == 0 else block(w, where, False, 0)
        jobs = []
        for way in (1, -1) if step == 0 else (sign,):
            index = step + (0 if way > 0 else 3)
            device = here.up if way > 0 else here.down
            go = here.has_up if way > 0 else here.has_down
            if step < CHAIN - 1:
                jobs.append((go, remote(origin, block_to(w, where), sends.at[w], arrivals.at[w], index, device)))
        return jobs

    def block_to(w, where):
        return fulls[w].at[0, z_of(where) * 2 + here.x]

    def second(w, where):
        origin = shards[w] if where[0] == 0 else block(w, where, False, 0)
        index = 6 + WHERE.index(where)
        if X_FIRST[w]:
            return remote(origin, block(w, where, False, 0), sends.at[w], arrivals.at[w], index, here.across)
        return remote(origin, block(w, where, False, 1), sends.at[w], arrivals.at[w], index, here.other)

    def third(w, where, arrived):
        index = 13 + WHERE.index(where) + (len(WHERE) if arrived else 0)
        if X_FIRST[w]:
            origin = shards[w] if where[0] == 0 and not arrived else block(w, where, arrived, 0)
            return remote(origin, block(w, where, arrived, 1), sends.at[w], arrivals.at[w], index, here.other)
        origin = shards[w] if where[0] == 0 and not arrived else block(w, where, False, int(arrived))
        return remote(origin, block(w, where, False, int(arrived)), sends.at[w], arrivals.at[w], index, here.across)

    def landing(w, where, stage, arrived=False):
        if stage == 2:
            index = 6 + WHERE.index(where)
            target = block(w, where, True, 0) if X_FIRST[w] else block(w, where, False, 1)
            device = here.across if X_FIRST[w] else here.other
        else:
            index = 13 + WHERE.index(where) + (len(WHERE) if arrived else 0)
            if X_FIRST[w]:
                target, device = block(w, where, arrived, 1), here.other
            else:
                target, device = block(w, where, True, int(arrived)), here.across
        return remote(target, target, sends.at[w], arrivals.at[w], index, device)

    def chain_landing(w, where):
        step, sign = where
        index = step - 1 + (0 if sign > 0 else 3)
        target = block(w, where, False, 0)
        return remote(target, target, sends.at[w], arrivals.at[w], index, here.down if sign > 0 else here.up)

    order = (0, 1, 3, 2)
    by_step = [[p for p in WHERE if p[0] == step] for step in range(CHAIN)]

    low, high = pl.ds(0, free), pl.ds(free + count, n_rows - free - count)
    middle, tail = pl.ds(free, count), pl.ds(source, count)
    locals_ = [(None, pltpu.make_async_copy(shards[w], fulls[w].at[0, here.dp], local.at[w])) for w in order]
    not_last, second_core = here.mp != 3, here.mp == 1
    for n, (given, taken) in enumerate(((rows_ref, rows_out.at[0]), (cot_ref, cot_out))):
        for m, part in enumerate((low, high, middle)):
            copy = pltpu.make_async_copy(given.at[part], taken.at[part], local.at[4 + 3 * n + m])
            locals_.append((not_last if m == 2 else None, copy))
    for condition, copy in locals_:
        maybe(condition, copy.start)

    def to_mate(m, part):
        return remote(rows_ref.at[part], rows_out.at[1, part], side_send, side_arrive, m, here.mate)

    side = [(None, to_mate(0, low)), (None, to_mate(1, high)), (not_last, to_mate(2, middle))]
    side.append((None, remote(vec_ref, vec_out, side_send, side_arrive, 3, here.other)))
    moved = [
        remote(rows_ref.at[tail], rows_out.at[0, middle], side_send, side_arrive, 4, here.other),
        remote(cot_ref.at[tail], cot_out.at[middle], side_send, side_arrive, 5, here.other),
        remote(rows_ref.at[tail], rows_out.at[1, middle], side_send, side_arrive, 6, (here.dp, 3 - here.mp)),
    ]
    side += [(second_core, copy) for copy in moved]

    started = []

    def start(condition, copy):
        maybe(condition, copy.start)
        started.append((condition, copy))

    for condition, copy in side:
        start(condition, copy)

    def send_step(step, weights):
        for where in by_step[step]:
            for w in weights:
                if step > 0:
                    maybe(held(where), chain_landing(w, where).wait_recv)
                for go, copy in chain(w, where):
                    both = go if held(where) is None else jnp.logical_and(go, held(where))
                    start(both, copy)
                start(held(where), second(w, where))
                start(held(where), third(w, where, False))

    def relay_step(step, weights):
        for where in by_step[step]:
            for w in weights:
                maybe(held(where), landing(w, where, 2).wait_recv)
                start(held(where), third(w, where, True))

    def land(weights):
        for where in WHERE:
            for w in weights:
                for arrived in (False, True):
                    maybe(held(where), landing(w, where, 3, arrived).wait_recv)

    first, later = (0, 1), (3, 2)
    for step in range(CHAIN):
        send_step(step, first)
        if step > 0:
            relay_step(step - 1, first)
    relay_step(CHAIN - 1, first)
    send_step(0, later)
    land(first)
    to_mate(0, low).wait_recv()
    to_mate(1, high).wait_recv()
    pl.when(here.mp != 2)(to_mate(2, middle).wait_recv)
    side[3][1].wait_recv()
    pl.when(here.mp == 3)(moved[0].wait_recv)
    pl.when(here.mp == 3)(moved[1].wait_recv)
    pl.when(here.mp == 2)(moved[2].wait_recv)
    for condition, copy in locals_:
        maybe(condition, copy.wait)
    width, columns = rows_ref.shape[1], shards[0].shape[1]
    for half, bias_ref in ((0, vec_ref), (1, vec_out)):
        weight = fulls[0][half].reshape(width, columns)
        bias = bias_ref[1:2, 0:columns]
        for at in (0, 1):
            act = dot(rows_out[at], weight, ((1,), (0,))) + bias
            acts[half, at * n_rows : (at + 1) * n_rows, :] = act.astype(BF16)
    attend_prepare((acts.at[0], acts.at[1]), slot_ref, mask_ref, q_ref, k_ref, v_ref)
    heads = q_ref.shape[0]
    due = [step * heads // (CHAIN - 1) for step in range(CHAIN - 1)]
    for head in range(heads):
        for step in range(1, CHAIN):
            if due[step - 1] == head:
                send_step(step, later)
                relay_step(step - 1, later)
        attend_rows(head, slice(None), q_ref, k_ref, v_ref, out_ref)
    relay_step(CHAIN - 1, later)
    for head in range(heads):
        attn_ref[:, head * HEAD_DIM : (head + 1) * HEAD_DIM] = out_ref[head, :, 0:HEAD_DIM]
    land(later)
    for condition, copy in started:
        maybe(condition, copy.wait_send)


def gather_all(shards, rows, cotangent, vectors, slots, masks):
    rows_local, width = rows.shape
    vmem, anywhere = pl.BlockSpec(memory_space=pltpu.VMEM), pl.BlockSpec(memory_space=pl.ANY)
    shapes = [jax.ShapeDtypeStruct((2, 2 * CHAIN) + s.shape, s.dtype) for s in shards]
    shapes += [
        jax.ShapeDtypeStruct((2, rows_local, width), rows.dtype),
        jax.ShapeDtypeStruct((rows_local, width), rows.dtype),
        jax.ShapeDtypeStruct(vectors.shape, vectors.dtype),
    ]
    heads = 2 * shards[1].shape[1] // HEAD_DIM
    wide = jax.ShapeDtypeStruct((heads, 2 * rows_local, 2 * HEAD_DIM), BF16)
    shapes += [jax.ShapeDtypeStruct((2 * rows_local, heads * HEAD_DIM), BF16), wide, wide, wide]
    plan = move_plan(rows_local)
    return pl.pallas_call(
        lambda *refs: gather_kernel(plan, *refs),
        out_shape=shapes,
        in_specs=[vmem] * 9,
        out_specs=[vmem] + [anywhere] * 3 + [vmem, anywhere] + [vmem] * 5,
        scratch_shapes=[
            pltpu.VMEM((2, 2 * rows_local, shards[0].shape[1]), BF16),
            pltpu.VMEM(wide.shape, BF16),
            pltpu.SemaphoreType.DMA((4, 27)),
            pltpu.SemaphoreType.DMA((4, 27)),
            pltpu.SemaphoreType.DMA((7,)),
            pltpu.SemaphoreType.DMA((7,)),
            pltpu.SemaphoreType.DMA((10,)),
        ],
        compiler_params=pltpu.CompilerParams(
            collective_id=0, has_side_effects=True, vmem_limit_bytes=56 * 2**20
        ),
        name="gather_all",
    )(*shards, rows, cotangent, vectors, slots, masks)


def finish_kernel(block, *refs):
    attn_ref, grad_ref, q_ref, k_ref, v_ref, rows_ref, weight_ref = refs[0:7]
    out_near, out_far, up_ref, down_ref, vec_ref, out_edge, branch_ref = refs[7:14]
    sums, (vec_out, out_back, grad_back, grad_out) = refs[14:18], refs[18:22]
    firsts, seconds, thirds, finals = [refs[22 + 4 * i : 26 + 4 * i] for i in range(4)]
    (g_ref, dq_ref, dk_ref, dv_ref, parts_ref, g_qkv, rows_t, to_mate, from_mate, grad_edge) = refs[38:48]
    vec_in, sends, arrivals, side_send, side_arrive = refs[48:53]
    mine = (g_qkv.at[0], out_near, up_ref.at[0], down_ref.at[0])
    theirs = (g_qkv.at[1], out_far, up_ref.at[1], down_ref.at[1])
    n_rows = branch_ref.shape[0]
    _, free, count = move_plan(n_rows)
    here = Place()
    here.greet([here.ring(1), here.ring(2), here.ring(3), here.across, here.other, here.mate])
    early, late = (2, 3, 1), (0,)
    order = (2, 1, 3, 0)

    def owner(ahead):
        return lax.rem(here.z + ahead, CHAIN)

    far = 1 - here.x
    started = []

    def start(copy, condition=None):
        if condition is None:
            copy.start()
        else:
            pl.when(condition)(copy.start)
        started.append((condition, copy))
        return copy

    def add(target, more):
        target[...] = (target[...].astype(F32) + more[...].astype(F32)).astype(BF16)

    first_jobs, second_jobs = {}, {}

    def first_stage(weights):
        for ahead in order:
            target = owner(ahead)
            for w in weights:
                for part in (0, 1):
                    if X_FIRST[w]:
                        origin, device = theirs[w].at[target, part], here.other
                    else:
                        origin, device = (mine, theirs)[part][w].at[target, far], here.across
                    landed = firsts[w].at[target, part]
                    first_jobs[w, ahead, part] = start(
                        remote(origin, landed, sends.at[w], arrivals.at[w], 2 * ahead + part, device)
                    )

    def second_stage(weights):
        for ahead in order:
            target = owner(ahead)
            for w in weights:
                for part in (0, 1):
                    first_jobs[w, ahead, part].wait_recv()
                    if X_FIRST[w]:
                        add(firsts[w].at[target, part], mine[w].at[target, part])
                    else:
                        add(firsts[w].at[target, part], (mine, theirs)[part][w].at[target, here.x])
                if X_FIRST[w]:
                    origin, device = firsts[w].at[target, far], here.across
                else:
                    origin, device = firsts[w].at[target, 1], here.other
                landed = seconds[w].at[target]
                second_jobs[w, ahead] = start(
                    remote(origin, landed, sends.at[w], arrivals.at[w], 8 + ahead, device)
                )

    third_jobs = {}

    def third_stage(weights):
        for ahead in order:
            target = owner(ahead)
            for w in weights:
                second_jobs[w, ahead].wait_recv()
                kept = firsts[w].at[target, here.x] if X_FIRST[w] else firsts[w].at[target, 0]
                add(seconds[w].at[target], kept)
                if ahead > 0:
                    third_jobs[w, ahead] = start(
                        remote(
                            seconds[w].at[target],
                            thirds[w].at[ahead - 1],
                            sends.at[w],
                            arrivals.at[w],
                            11 + ahead,
                            here.ring(ahead),
                        )
                    )

    def settle_sums(weights):
        for w in weights:
            total = seconds[w][here.z].astype(F32)
            for ahead in range(1, CHAIN):
                third_jobs[w, ahead].wait_recv()
                total = total + thirds[w][ahead - 1].astype(F32)
            finals[w][...] = total

    first_stage(early)
    edges = [start(remote(out_edge, out_back, side_send, side_arrive, 6, here.other), here.mp == 3)]

    attend_back_body(
        block, 3, attn_ref, grad_ref, q_ref, k_ref, v_ref, (parts_ref.at[0], parts_ref.at[1]),
        g_ref, dq_ref, dk_ref, dv_ref,
    )
    rows_t[...] = rows_ref[...].T
    d_rows = jnp.zeros(rows_ref.shape, F32)
    vec_out[...] = vec_ref[...]
    depth, columns = g_qkv.shape[3], g_qkv.shape[4]
    for half in (0, 1):
        part = parts_ref[half]
        d_rows = d_rows + dot(part, weight_ref[half], ((1,), (1,)))
        grads = dot(rows_t[...], part, ((1,), (0,))).astype(BF16)
        for at in range(2 * CHAIN):
            g_qkv[half, at // 2, at % 2] = grads[at * depth : (at + 1) * depth, :]
        row = 7 + 2 * half
        vec_out[row : row + 1, 0:columns] = jnp.sum(part.astype(F32), axis=0, keepdims=True)
    to_mate[...] = d_rows[n_rows:, :].astype(BF16)
    grad_out[...] = d_rows[0:n_rows, :] + branch_ref[...]
    mate_job = start(remote(to_mate, from_mate, side_send, side_arrive, 8, here.mate))

    def vec_send(index, device):
        copy = remote(vec_out, vec_in.at[index], side_send, side_arrive, index, device)
        copy.start()
        return copy

    sent = vec_send(0, here.other)
    second_stage(early)
    first_stage(late)
    mate_job.wait_recv()
    grad_out[...] = grad_out[...] + from_mate[...].astype(F32)
    grad_edge[...] = grad_out[free : free + count, :]
    edges.append(start(remote(grad_edge, grad_back, side_send, side_arrive, 7, here.other), here.mp == 3))
    sent.wait()
    vec_out[0:6] = vec_out[0:6] + vec_in[0, 0:6]
    vec_out[6:8] = vec_out[6:8] + vec_in[0, 8:10]
    sent = vec_send(1, here.across)
    third_stage(early)
    second_stage(late)
    sent.wait()
    vec_out[...] = vec_out[...] + vec_in[1]
    ring = [vec_send(1 + ahead, here.ring(ahead)) for ahead in (1, 2, 3)]
    third_stage(late)
    settle_sums(early)
    for copy in ring:
        copy.wait()
    slots = [vec_out[...], vec_in[2], vec_in[3], vec_in[4]]
    total = jnp.zeros_like(slots[0])
    for at in range(CHAIN):
        for behind in range(CHAIN):
            same = lax.rem(here.z + CHAIN - behind, CHAIN) == at
            total = total + jnp.where(same, slots[behind], 0.0)
    vec_out[...] = total
    sent = vec_send(5, here.mate)
    for w in (2, 3):
        sums[w][...] = finals[w][...]
    value = finals[1][...]
    pad = jnp.zeros((LANES - value.shape[0], value.shape[1]), F32)
    sums[1][...] = jnp.concatenate([value, pad], 0).T[:, : value.shape[0]]
    settle_sums(late)
    for c in range(sums[0].shape[0]):
        sums[0][c] = finals[0][:, c * sums[0].shape[2] : (c + 1) * sums[0].shape[2]]

    sent.wait()
    vec_out[0:6] = vec_out[0:6] + vec_in[5, 0:6]
    for copy in edges:
        pl.when(here.mp == 1)(copy.wait_recv)
    for condition, copy in started:
        if condition is None:
            copy.wait_send()
        else:
            pl.when(condition)(copy.wait_send)


def finish_all(attn, grad, query, keys, values, rows, weight, out, up, down, vectors, out_edge, branch, block):
    heads, n_all = query.shape[:2]
    width = rows.shape[1]
    depth = width // (2 * CHAIN)
    out = [g.reshape(CHAIN, 2, depth, -1) for g in out]
    up, down = [g.reshape(2, CHAIN, 2, depth, -1) for g in (up, down)]
    columns = weight.shape[2]
    widths = [columns, out[0].shape[-1], up.shape[-1], down.shape[-1]]
    vmem = pl.BlockSpec(memory_space=pltpu.VMEM)
    shapes = [(3, depth, columns // 3), (widths[1], depth), (depth, widths[2]), (depth, widths[3])]
    shapes = [jax.ShapeDtypeStruct(shape, F32) for shape in shapes]
    shapes += [
        jax.ShapeDtypeStruct(vectors.shape, F32),
        jax.ShapeDtypeStruct(out_edge.shape, BF16),
        jax.ShapeDtypeStruct(out_edge.shape, F32),
        jax.ShapeDtypeStruct(branch.shape, F32),
    ]
    scratch = [pltpu.VMEM((CHAIN, 2, depth, n), BF16) for n in widths]
    scratch += [pltpu.VMEM((CHAIN, depth, n), BF16) for n in widths]
    scratch += [pltpu.VMEM((CHAIN - 1, depth, n), BF16) for n in widths]
    scratch += [pltpu.VMEM((depth, n), F32) for n in widths]
    scratch += [pltpu.VMEM(query.shape, BF16)] * 2 + [pltpu.VMEM(query.shape, F32)] * 2
    scratch += [
        pltpu.VMEM((2, n_all, columns), BF16),
        pltpu.VMEM((2, CHAIN, 2, depth, columns), BF16),
        pltpu.VMEM((width, n_all), BF16),
        pltpu.VMEM(branch.shape, BF16),
        pltpu.VMEM(branch.shape, BF16),
        pltpu.VMEM(out_edge.shape, F32),
        pltpu.VMEM((6,) + vectors.shape, F32),
        pltpu.SemaphoreType.DMA((4, 15)),
        pltpu.SemaphoreType.DMA((4, 15)),
        pltpu.SemaphoreType.DMA((9,)),
        pltpu.SemaphoreType.DMA((9,)),
    ]
    return pl.pallas_call(
        lambda *refs: finish_kernel(block, *refs),
        out_shape=shapes,
        in_specs=[vmem] * 14,
        out_specs=[vmem] * 8,
        scratch_shapes=scratch,
        compiler_params=pltpu.CompilerParams(
            collective_id=1, has_side_effects=True, vmem_limit_bytes=62 * 2**20
        ),
        name="finish_all",
    )(attn, grad, query, keys, values, rows, weight, *out, up, down, vectors, out_edge, branch)


def split_parts(value, count):
    parts = []
    for _ in range(count):
        part = value.astype(BF16).astype(F32)
        parts.append(part)
        value = value - part
    return parts


def lane_fill(base, parts, first):
    lane = lax.broadcasted_iota(jnp.int32, base.shape, 1)
    for index, part in enumerate(parts):
        base = jnp.where(lane == first + index, part, base)
    return base


def head_columns(head, part, per_half):
    half, index = divmod(head, per_half)
    at = (part * per_half + index) * HEAD_DIM
    return half, slice(at, at + HEAD_DIM)


def attend_prepare(acts, slot_ref, mask_ref, q_ref, k_ref, v_ref):
    heads, rows = q_ref.shape[:2]
    ones = lane_fill(jnp.zeros((rows, HEAD_DIM), F32), (1.0, 1.0), 0).astype(BF16)
    for head in range(heads):
        for part, (ref, more) in enumerate(((q_ref, slot_ref), (k_ref, mask_ref), (v_ref, None))):
            half, columns = head_columns(head, part, heads // 2)
            piece = acts[half][:, columns]
            if part == 0:
                piece = (piece.astype(F32) * HEAD_DIM ** (-0.5)).astype(BF16)
            ref[head, :, 0:HEAD_DIM] = piece
            ref[head, :, HEAD_DIM : 2 * HEAD_DIM] = ones if more is None else more[...]


def attend_rows(head, span, q_ref, k_ref, v_ref, out_ref):
    query = q_ref[head, span, :]
    scores = dot(query, k_ref[head], ((1,), (1,)))
    peak = jnp.max(scores, axis=-1, keepdims=True)
    weights = jnp.exp(scores - peak)
    both = dot(weights.astype(BF16), v_ref[head], ((1,), (0,)))
    total = both[:, HEAD_DIM : HEAD_DIM + 1]
    out_ref[head, span, :] = (both * (1.0 / total)).astype(BF16)
    log_sum = peak + jnp.log(total)
    parts = [-p for p in split_parts(log_sum, 3)]
    q_ref[head, span, :] = lane_fill(query.astype(F32), parts, HEAD_DIM + 3).astype(BF16)


def attend_kernel(block, near_ref, far_ref, slot_ref, mask_ref, attn_ref, q_ref, k_ref, v_ref, out_ref):
    heads, rows = q_ref.shape[:2]
    attend_prepare((near_ref, far_ref), slot_ref, mask_ref, q_ref, k_ref, v_ref)

    def step(index, carry):
        head, at = index // (rows // block), lax.rem(index, rows // block)
        span = pl.ds(pl.multiple_of(at * block, 16), block)
        attend_rows(head, span, q_ref, k_ref, v_ref, out_ref)
        return carry

    lax.fori_loop(0, heads * (rows // block), step, 0, unroll=6)
    for head in range(heads):
        attn_ref[:, head * HEAD_DIM : (head + 1) * HEAD_DIM] = out_ref[head, :, 0:HEAD_DIM]


def attend_back_body(block, unroll, attn_ref, grad_ref, q_ref, k_ref, v_ref, outs, g_ref, dq_ref, dk_ref, dv_ref):
    heads, rows = q_ref.shape[:2]
    for head in range(heads):
        columns = slice(head * HEAD_DIM, (head + 1) * HEAD_DIM)
        grad = grad_ref[:, columns]
        mean = jnp.sum(grad.astype(F32) * attn_ref[:, columns].astype(F32), axis=-1, keepdims=True)
        parts = [-p for p in split_parts(mean, 2)]
        g_ref[head, :, 0:HEAD_DIM] = grad
        g_ref[head, :, HEAD_DIM : 2 * HEAD_DIM] = lane_fill(
            jnp.zeros((rows, HEAD_DIM), F32), parts, 0
        ).astype(BF16)
    dk_ref[...] = jnp.zeros_like(dk_ref)
    dv_ref[...] = jnp.zeros_like(dv_ref)

    def step(index, carry):
        head, at = index // (rows // block), lax.rem(index, rows // block)
        span = pl.ds(pl.multiple_of(at * block, 16), block)
        query, grad = q_ref[head, span, :], g_ref[head, span, :]
        keys = k_ref[head]
        probs = jnp.exp(dot(keys, query, ((1,), (1,))))
        change = (probs * dot(v_ref[head], grad, ((1,), (1,)))).astype(BF16)
        dv_ref[head] += dot(probs.astype(BF16), grad, ((1,), (0,)))
        dk_ref[head] += dot(change, query, ((1,), (0,)))
        dq_ref[head, span, :] = (dot(change, keys, ((0,), (0,))) * HEAD_DIM ** (-0.5)).astype(BF16)
        return carry

    lax.fori_loop(0, heads * (rows // block), step, 0, unroll=unroll)
    for head in range(heads):
        for part, ref in enumerate((dq_ref, dk_ref, dv_ref)):
            half, columns = head_columns(head, part, heads // 2)
            outs[half][:, columns] = ref[head, :, 0:HEAD_DIM].astype(BF16)


def attend_back_kernel(block, attn_ref, grad_ref, q_ref, k_ref, v_ref, near_ref, far_ref, *scratch):
    attend_back_body(
        block, 1, attn_ref, grad_ref, q_ref, k_ref, v_ref, (near_ref, far_ref), *scratch
    )


def attend_cost(heads, rows, products):
    return pl.CostEstimate(
        flops=2 * products * heads * rows * rows * 128,
        bytes_accessed=8 * heads * rows * 128,
        transcendentals=heads * rows * rows,
    )


def attend(near, far, slots, masks, block):
    rows = near.shape[0]
    heads = 2 * near.shape[1] // (3 * HEAD_DIM)
    vmem = pl.BlockSpec(memory_space=pltpu.VMEM)
    wide = jax.ShapeDtypeStruct((heads, rows, 2 * HEAD_DIM), BF16)
    return pl.pallas_call(
        lambda *refs: attend_kernel(block, *refs),
        out_shape=[jax.ShapeDtypeStruct((rows, heads * HEAD_DIM), BF16), wide, wide, wide],
        in_specs=[vmem] * 4,
        out_specs=[vmem] * 4,
        scratch_shapes=[pltpu.VMEM(wide.shape, BF16)],
        compiler_params=pltpu.CompilerParams(vmem_limit_bytes=40 * 2**20),
        cost_estimate=attend_cost(heads, rows, 2),
        name="attend",
    )(near, far, slots, masks)


def attend_back(attn, grad, query, keys, values, block):
    heads, rows = query.shape[:2]
    vmem = pl.BlockSpec(memory_space=pltpu.VMEM)
    out = jax.ShapeDtypeStruct((rows, 3 * heads // 2 * HEAD_DIM), BF16)
    return pl.pallas_call(
        lambda *refs: attend_back_kernel(block, *refs),
        out_shape=[out, out],
        in_specs=[vmem] * 5,
        out_specs=[vmem] * 2,
        scratch_shapes=[pltpu.VMEM(query.shape, BF16)] * 2 + [pltpu.VMEM(query.shape, F32)] * 2,
        compiler_params=pltpu.CompilerParams(vmem_limit_bytes=40 * 2**20),
        cost_estimate=attend_cost(heads, rows, 5),
        name="attend_back",
    )(attn, grad, query, keys, values)


def norm_stats(values):
    mean = jnp.mean(values, axis=-1, keepdims=True)
    center = values - mean
    spread = jnp.mean(center * center, axis=-1, keepdims=True)
    inverse = lax.rsqrt(spread + EPS)
    return center * inverse, inverse


def norm_back(grad, unit, inverse, gain):
    scaled = grad * gain
    return inverse * (
        scaled
        - jnp.mean(scaled, axis=-1, keepdims=True)
        - unit * jnp.mean(scaled * unit, axis=-1, keepdims=True)
    )


def feed_back_kernel(n_rows, first_ref, grad_ref, up_ref, down_ref, near_hidden, far_hidden,
                     near_slope, far_slope, g_up_ref, g_down_ref, g_bias_ref, own_ref, mate_ref, total_ref, first_t, grad_t):
    step = pl.program_id(0)

    @pl.when(step == 0)
    def _():
        first_t[...] = first_ref[...].T
        grad_t[...] = grad_ref[...].T
        total_ref[...] = jnp.zeros_like(total_ref)

    near = step < pl.num_programs(0) // 2
    hidden = jnp.where(near, near_hidden[...], far_hidden[...])
    slope = jnp.where(near, near_slope[...], far_slope[...])
    d_hidden = dot(grad_ref[...], down_ref[0], ((1,), (0,)))
    d_pre = (d_hidden * slope.astype(F32)).astype(BF16)
    total_ref[...] += dot(d_pre, up_ref[0], ((1,), (1,)))
    g_bias_ref[0] = jnp.sum(d_pre.astype(F32), axis=0, keepdims=True)
    g_up_ref[0] = dot(first_t[...], d_pre, ((1,), (0,))).astype(BF16)
    g_down_ref[0] = dot(grad_t[...], hidden, ((1,), (0,))).astype(BF16)

    @pl.when(step == pl.num_programs(0) - 1)
    def _():
        own_ref[...] = total_ref[0:n_rows, :]
        mate_ref[...] = total_ref[n_rows:, :].astype(BF16)


def feed_specs(rows, width, units, tile):
    blocks = units // tile
    whole = pl.BlockSpec((rows, width), lambda i: (0, 0))
    half = pl.BlockSpec((rows // 2, width), lambda i: (0, 0))

    def split(count):
        return pl.BlockSpec((1, count, tile), lambda i: (i // blocks, 0, lax.rem(i, blocks)))

    halves = [jax.ShapeDtypeStruct((rows // 2, width), kind) for kind in (F32, BF16)]
    return (2 * blocks,), whole, half, split, halves


def feed_back(first, grad, up, down, hiddens, slopes, tile):
    (rows, width), units = first.shape, up.shape[2]
    grid, whole, half, split, halves = feed_specs(rows, width, units, tile)
    last = units // tile - 1
    near = pl.BlockSpec((rows, tile), lambda i: (0, jnp.minimum(i, last)))
    far = pl.BlockSpec((rows, tile), lambda i: (0, jnp.maximum(i - last - 1, 0)))
    wide = jax.ShapeDtypeStruct((2, width, units), BF16)
    return pl.pallas_call(
        lambda *refs: feed_back_kernel(rows // 2, *refs),
        grid=grid,
        out_shape=[wide, wide, jax.ShapeDtypeStruct((2, 1, units), F32)] + halves,
        in_specs=[whole, whole, split(width), split(width), near, far, near, far],
        out_specs=[split(width), split(width), split(1), half, half],
        scratch_shapes=[
            pltpu.VMEM((rows, width), F32),
            pltpu.VMEM((width, rows), BF16),
            pltpu.VMEM((width, rows), BF16),
        ],
        compiler_params=pltpu.CompilerParams(vmem_limit_bytes=48 * 2**20),
        cost_estimate=pl.CostEstimate(
            flops=16 * rows * width * units,
            bytes_accessed=16 * width * units + 8 * rows * units,
            transcendentals=0,
        ),
        name="feed_back",
    )(first, grad, up, down, *hiddens, *slopes)


def update_one(rate, weight, grad, moment, average):
    moment_next = MOMENTUM * moment + grad
    weight_next = weight - rate * (grad + MOMENTUM * moment_next)
    return (weight_next, moment_next, DECAY * average + (1.0 - DECAY) * weight_next)


def on_device(
    tokens,
    lengths,
    cotangent,
    qkv_weight,
    out_weight,
    up_weight,
    down_weight,
    head_bias,
    up_bias,
    norm_vectors,
    qkv_moment,
    out_moment,
    up_moment,
    down_moment,
    head_bias_moment,
    up_bias_moment,
    norm_moment,
    qkv_average,
    out_average,
    up_average,
    down_average,
    head_bias_average,
    up_bias_average,
    norm_average,
):
    grid = Grid(lax.axis_size("dp"))
    member = lax.axis_index("mp")
    mate = member + 1 - 2 * lax.rem(member, 2)
    rows_local, width = tokens.shape
    head_width = qkv_weight.shape[2]
    stages = len(grid.dims)
    units = up_weight.shape[1]

    slot_own, valid_own = row_table(rows_local, member, lengths)
    slot_mate, valid_mate = row_table(rows_local, mate, lengths)
    slot = jnp.concatenate([slot_own, slot_mate])
    frame = jnp.concatenate([valid_own, valid_mate])
    column = jnp.arange(HEAD_DIM)[None, :]
    here_slot = slot[:, None] == column
    slot_lanes = here_slot.astype(BF16)
    mask_lanes = jnp.where(
        column < len(LENS),
        jnp.where(here_slot & frame[:, None], 0.0, NEG_FILL),
        jnp.where(column < len(LENS) + 3, 1.0, 0.0),
    ).astype(BF16)
    live = valid_own[:, None]

    qkv_shard = jnp.transpose(qkv_weight, (1, 0, 2)).reshape(-1, 3 * head_width).astype(BF16)
    shards = (
        qkv_shard,
        out_weight.astype(BF16).T,
        up_weight.astype(BF16),
        down_weight.astype(BF16).T,
    )
    kernels = grid.size == 2 * CHAIN and units == width
    if kernels:
        flat = jnp.concatenate(
            [
                head_bias[0],
                jnp.zeros((head_width,), F32),
                head_bias[1],
                jnp.zeros((width - 3 * head_width,), F32),
            ]
        )
        vectors = jnp.concatenate([up_bias[None], flat[None], jnp.zeros((6, width), F32)])
        *fulls, rows_both, own_cotangent, far_vectors, attn, query, keys, values = gather_all(
            shards, tokens, cotangent, vectors, slot_lanes, mask_lanes
        )
        qkv_pair, out_pair, up_pair, down_pair = [full.reshape(2, width, -1) for full in fulls]
        up_bias_pair = (up_bias, far_vectors[0])
        tokens_all = rows_both.reshape(2 * rows_local, width)
        own_tokens = rows_both[0]
    else:
        qkv_pair = gather_half(grid, shards[0], stages)
        out_pair = gather_half(grid, shards[1], stages - 1)
        up_pair = jnp.stack(gather_half(grid, shards[2], stages))
        down_pair = jnp.stack(gather_half(grid, shards[3], stages - 1))
        bias_pair = (head_bias, half_swap(head_bias))
        up_bias_pair = (up_bias, half_swap(up_bias))
        own_tokens = bring(tokens, member)
        own_cotangent = bring(cotangent, member)
        tokens_all = jnp.concatenate([own_tokens, core_swap(own_tokens)], 0)

    def share(rows):
        return jnp.concatenate([rows, core_swap(rows)], 0)

    def settle(partial):
        return partial[:rows_local] + core_swap(partial[rows_local:].astype(BF16)).astype(F32)

    block = 2 * rows_local
    if not kernels:
        parts = []
        for weight, bias in zip(qkv_pair, bias_pair):
            rows_bias = jnp.concatenate([bias[0], jnp.zeros_like(bias[0]), bias[1]])
            parts.append((dot(tokens_all, weight, ((1,), (0,))) + rows_bias).astype(BF16))
        attn, query, keys, values = attend(*parts, slot_lanes, mask_lanes, block)
    out_both = jnp.concatenate([out_pair[0], out_pair[1]], 1)
    branch = settle(dot(attn, out_both, ((1,), (1,))))
    unit_one, inverse_one = norm_stats(branch + norm_vectors[0] + own_tokens.astype(F32))
    first = unit_one * norm_vectors[2] + norm_vectors[3]
    first_all = share(first.astype(BF16))

    hiddens, slopes = [], []
    for at in (0, 1):
        pre = dot(first_all, up_pair[at], ((1,), (0,))) + up_bias_pair[at]
        phi = 0.5 * (1.0 + lax.erf(pre * (0.5**0.5)))
        density = jnp.exp(-0.5 * pre * pre) * (1.0 / math.sqrt(2.0 * math.pi))
        hiddens.append((pre * phi).astype(BF16))
        slopes.append((phi + pre * density).astype(BF16))
    ffn = settle(
        dot(hiddens[0], down_pair[0], ((1,), (1,))) + dot(hiddens[1], down_pair[1], ((1,), (1,)))
    )
    unit_two, inverse_two = norm_stats(ffn + norm_vectors[1] + first)
    second = unit_two * norm_vectors[4] + norm_vectors[5]
    layer_out = jnp.where(live, second, 0.0).astype(BF16)

    grad_two = jnp.where(live, own_cotangent.astype(F32), 0.0)
    d_second = norm_back(grad_two, unit_two, inverse_two, norm_vectors[4])
    d_ffn_all = share(d_second.astype(BF16))
    tile = 2 * LANES if units % (2 * LANES) == 0 else units
    grad_up, grad_down, grad_up_bias, d_first_own, d_first_mate = feed_back(
        first_all, d_ffn_all, up_pair, down_pair, hiddens, slopes, tile
    )
    grad_up_bias = grad_up_bias[:, 0, :]
    d_first = d_second + (d_first_own + core_swap(d_first_mate).astype(F32))

    d_branch = norm_back(d_first, unit_one, inverse_one, norm_vectors[2])
    d_branch_all = share(d_branch.astype(BF16))
    d_attn = dot(d_branch_all, out_both, ((1,), (0,))).astype(BF16)
    grad_out = [
        dot(d_branch_all, attn[:, at : at + head_width], ((0,), (0,))).astype(BF16)
        for at in (0, head_width)
    ]
    norm_part = jnp.stack(
        [
            jnp.sum(d_branch, axis=0),
            jnp.sum(d_second, axis=0),
            jnp.sum(d_first * unit_one, axis=0),
            jnp.sum(d_first, axis=0),
            jnp.sum(grad_two * unit_two, axis=0),
            jnp.sum(grad_two, axis=0),
        ]
    )
    if kernels:
        blank = jnp.zeros((1, width), F32)
        vectors = jnp.concatenate(
            [norm_part, grad_up_bias[:1], blank, grad_up_bias[1:], jnp.zeros((7, width), F32)]
        )
        source, free, count = move_plan(rows_local)
        *sums, vectors, out_back, grad_back, tokens_grad = finish_all(
            attn,
            d_attn,
            query,
            keys,
            values,
            tokens_all,
            qkv_pair,
            grad_out,
            grad_up,
            grad_down,
            vectors,
            layer_out[free : free + count],
            d_branch,
            block,
        )
        sum_qkv, sum_out, sum_up, sum_down = sums
        sum_down = sum_down.T
        layer_out = put_back(layer_out, out_back, member)
        tokens_grad = put_back(tokens_grad, grad_back, member)
        sum_norm, sum_up_bias, sum_bias = vectors[:6], vectors[6], vectors[7]
        sum_bias = sum_bias[: 3 * head_width]
    else:
        d_parts = attend_back(attn, d_attn, query, keys, values, block)
        grad_qkv = [dot(tokens_all, part, ((0,), (0,))).astype(BF16) for part in d_parts]
        grad_bias = [jnp.sum(part, axis=0, dtype=F32) for part in d_parts]
        d_tokens = settle(
            dot(d_parts[0], qkv_pair[0], ((1,), (1,))) + dot(d_parts[1], qkv_pair[1], ((1,), (1,)))
        )
        tokens_grad = d_tokens + d_branch
        sum_qkv = scatter_sum(grid, *grad_qkv, True)
        sum_out = scatter_sum(grid, *grad_out, True)
        sum_up = scatter_sum(grid, *grad_up, False)
        sum_down = scatter_sum(grid, *grad_down, True)
        layer_out = send_back(layer_out, member)
        tokens_grad = send_back(tokens_grad, member)
        sum_norm = sum_all(grid, norm_part, True)
        sum_up_bias = sum_half(grid, grad_up_bias)
        sum_bias = sum_half(grid, grad_bias)
        sum_qkv = jnp.transpose(sum_qkv.reshape(-1, 3, head_width), (1, 0, 2))
        sum_out, sum_down = sum_out.T, sum_down.T
    sum_head_bias = jnp.stack([sum_bias[:head_width], sum_bias[2 * head_width :]])

    divisor = math.sqrt(1000.0 * grid.size * UTT)
    params = (qkv_weight, out_weight, up_weight, down_weight, head_bias, up_bias, norm_vectors)
    grads = (sum_qkv, sum_out, sum_up, sum_down, sum_head_bias, sum_up_bias, sum_norm)
    moments = (
        qkv_moment,
        out_moment,
        up_moment,
        down_moment,
        head_bias_moment,
        up_bias_moment,
        norm_moment,
    )
    averages = (
        qkv_average,
        out_average,
        up_average,
        down_average,
        head_bias_average,
        up_bias_average,
        norm_average,
    )
    nexts, moment_nexts, average_nexts = ([], [], [])
    for weight, grad, moment, average, scale_one in zip(
        params, grads, moments, averages, RATE_SCALES
    ):
        weight_next, moment_next, average_next = update_one(
            scale_one / divisor, weight, grad, moment, average
        )
        nexts.append(weight_next)
        moment_nexts.append(moment_next)
        average_nexts.append(average_next)
    return (layer_out, tokens_grad, *grads, *nexts, *moment_nexts, *average_nexts)


ROWS = P(("dp", "mp"), None)
PARAMS = (
    P(None, "dp", "mp"),
    P("mp", "dp"),
    P("dp", "mp"),
    P("mp", "dp"),
    P(None, "mp"),
    P("mp"),
    P(),
)


def solution(mesh):
    return jax.shard_map(
        on_device,
        mesh=mesh,
        in_specs=(ROWS, P("dp", None), ROWS) + PARAMS * 3,
        out_specs=(ROWS, ROWS) + PARAMS * 4,
        check_vma=False,
    )
```
